32 devices in a mesh: dp: 8 (over z, y), expert: 4 (over x, core).
Axes of the slice: x: 2, y: 2, z: 4, core: 2. Of those that a mesh axis runs over, the one named last changes fastest.
Arguments:
- tokens: bfloat16 [1024, 4096], P('dp'), may hold values from -6 to 6
- upstream: bfloat16 [1024, 4096], P('dp', 'expert'), may hold values from -6 to 6
- gates: bfloat16 [1024, 2], P('dp'), may hold values from 0.049804688 to 1
- expert_ids: int32 [1024, 2], P('dp'), may hold values from 0 to 7, all different within a row; in each aligned block of 128 rows (0 to 127, 128 to 255, ...) at most 64 rows name the same one
- w_gate: bfloat16 [8, 1536, 4096], P('dp', 'expert'), may hold values from -0.09375 to 0.09375
- w_up: bfloat16 [8, 1536, 4096], P('dp', 'expert'), may hold values from -0.09375 to 0.09375
- w_down: bfloat16 [8, 1536, 4096], P('dp', 'expert'), may hold values from -0.15625 to 0.15625
Outputs:
- grad_x: bfloat16 [1024, 4096], P('dp', 'expert')
- grad_gates: float32 [1024, 2], P('dp')
- grad_w_gate: bfloat16 [8, 1536, 4096], P('dp', 'expert')
- grad_w_up: bfloat16 [8, 1536, 4096], P('dp', 'expert')
- grad_w_down: bfloat16 [8, 1536, 4096], P('dp', 'expert')
The draws below stay inside these ranges and needn't reach their ends.
Inputs may be any that keep to these rules, and one draw needn't show every extreme that they name: `expert_ids`: each row names 2 different experts. In each aligned block of 128 rows (the tokens of one index of dp) no expert is named by more than 64 rows, a bound that some block reaches.
All inputs are finite; a program needn't handle non-finite values.
Results may differ from the reference program's by a relative error of at most 0.012.
Values may be sent and summed in bfloat16 or wider, within the bound.
A program may use at most 128 MiB of HBM per device.

```python
import math
import jax
import jax.numpy as jnp
import numpy as np
from jax import lax

D = 4096
HID = 1536
TOK_DEV = 128
TOP = 2
EXPERTS = 8
CAP = 64
TOKENS = 1024
N_DP = 8
N_EXPERT = 4


def shard_levels(stream_key, extent, pieces, low, top_value):
    def one(dim, blocks):
        steps = jax.random.uniform(jax.random.fold_in(jax.random.fold_in(stream_key, 6), dim), (blocks,), jnp.float32, low / len(pieces), top_value / len(pieces))
        return jnp.repeat(jnp.exp(steps), extent[dim] // blocks).reshape((-1,) + (1,) * (len(extent) - dim - 1))

    level = one(*pieces[0])
    for cut in pieces[1:]:
        level = level * one(*cut)
    return level


def shared_out(key, own, number, rows, number_of, top, bound, lean):
    ranking = jax.random.permutation(key, number_of)
    crowded, usual = shares(number_of, rows * top, bound, lean, True), shares(number_of, rows * top, bound, lean, False)
    places = jnp.arange(number_of)

    def named(lengths, turn):
        used = int((lengths > 0).sum())
        fixed = max(1, used // 4)
        moved = fixed + (places - fixed + turn * (used - fixed)) % max(1, number_of - fixed)
        return jnp.zeros((number_of,), jnp.int32).at[ranking[jnp.where(places < fixed, places, moved)]].set(jnp.asarray(lengths, jnp.int32))

    lengths = jnp.where(number % 4 == 0, named(crowded, number // 4), named(usual, number - number // 4 - 1))
    mixed = jax.random.permutation(jax.random.fold_in(own, 3), number_of)
    donor, taker = mixed[0:number_of // 2 * 2:2], mixed[1:number_of // 2 * 2:2]
    margin = jnp.minimum(lengths[donor] - 1, bound - lengths[taker]) // 2
    margin = jnp.where((donor == ranking[0]) | (taker == ranking[0]) | (lengths[taker] == 0), 0, jnp.maximum(margin, 0))
    moved = jax.random.randint(jax.random.fold_in(own, 4), (number_of // 2,), 0, 1 << 20) % (margin + 1)
    lengths = lengths.at[donor].add(-moved).at[taker].add(moved)
    members = jnp.searchsorted(jnp.cumsum(lengths), jnp.arange(rows * top), side="right").astype(jnp.int32)
    table = members.reshape(top, rows).T
    table = table[jax.random.permutation(jax.random.fold_in(own, 1), rows)]
    turn = jax.random.randint(jax.random.fold_in(own, 2), (rows, 1), 0, top)
    return jnp.take_along_axis(table, (jnp.arange(top)[None, :] + turn) % top, axis=1)


def shares(number_of, total, most, skew, full):
    weights = [(1 << 20) // math.isqrt(rank ** skew) + 1 for rank in range(1, number_of + 1)]
    largest = most if full else min(most, max(-(-total // number_of), total * weights[0] // sum(weights)))
    least = 1 if total - largest >= number_of - 1 else 0
    holding, rest = [largest] + [least] * (number_of - 1), total - largest - least * (number_of - 1)
    while rest > 0:
        free = [i for i in range(1, number_of) if holding[i] < largest] or [i for i in range(1, number_of) if holding[i] < most]
        mass, left = sum([weights[i] for i in free]), rest
        for i in free:
            more = min(most - holding[i], max(1, left * weights[i] // mass), rest)
            holding[i] = holding[i] + more
            rest = rest - more
    return np.array(holding)


def noise(stream_key, dims, scale, reach, split=(), kind=jnp.bfloat16):
    values = scale * jax.random.normal(stream_key, dims, jnp.float32)
    if split:
        values = values * shard_levels(stream_key, dims, split, -0.22, 0.18)
    return jnp.clip(values, -reach, reach).astype(kind)


def setup_inputs(seed: int = 0) -> dict:
    splits = jax.random.split(jax.random.key(seed), 8)
    tokens = noise(splits[0], (TOKENS, D), 1.0, 6.0, ((0, 8),))
    upstream = noise(splits[1], (TOKENS, D), 1.0, 6.0, ((0, 8), (1, 4)))
    gates = jnp.clip(jnp.exp(math.log(1.0) - 2.9996462 * jax.random.uniform(splits[2], (TOKENS, TOP), jnp.float32) ** shard_levels(splits[2], (TOKENS, TOP), ((0, 8),), -0.2, 0.2)), 0.049804688, 1.0).astype(jnp.bfloat16)
    expert_ids_keys = jax.random.split(jax.random.fold_in(splits[3], 1), TOKENS // TOK_DEV)
    expert_ids_turns = jax.random.permutation(jax.random.fold_in(splits[3], 3), TOKENS // TOK_DEV)
    expert_ids = jax.vmap(lambda own, number: shared_out(jax.random.fold_in(splits[3], 2), own, number, TOK_DEV, EXPERTS, TOP, CAP, 2))(expert_ids_keys, expert_ids_turns).reshape((TOKENS, TOP))
    w_gate = noise(splits[4], (EXPERTS, HID, D), D ** -0.5, 0.09375, ((0, 8), (1, 4)))
    w_up = noise(splits[5], (EXPERTS, HID, D), D ** -0.5, 0.09375, ((0, 8), (1, 4)))
    w_down = noise(splits[6], (EXPERTS, HID, D), HID ** -0.5, 0.15625, ((0, 8), (1, 4)))
    return dict(tokens=tokens, upstream=upstream, gates=gates, expert_ids=expert_ids, w_gate=w_gate, w_up=w_up, w_down=w_down)


def swish_pair(pre):
    sigma = jax.nn.sigmoid(pre)
    return pre * sigma, sigma * (1.0 + pre * (1.0 - sigma))


def contract_last(left, right):
    return lax.dot_general(left, right, (((1,), (1,)), ((), ())), preferred_element_type=jnp.float32)


def contract_first(left, right):
    return lax.dot_general(left, right, (((0,), (0,)), ((), ())), preferred_element_type=jnp.float32)


def reference(tokens, upstream, gates, expert_ids, w_gate, w_up, w_down):
    experts = w_gate.shape[0]
    hidden = w_gate.shape[1]
    width = tokens.shape[1]
    top = expert_ids.shape[1]
    groups = N_DP
    windows = N_EXPERT
    window = hidden // windows
    tok_rows = tokens.shape[0] // groups
    cap = 2 * tok_rows * top // experts
    rows = groups * cap
    block_ids = expert_ids.reshape(groups, tok_rows * top)
    onehot = (block_ids[:, :, None] == jnp.arange(experts, dtype=jnp.int32)[None, None, :]).astype(jnp.int32)
    position = jnp.sum((jnp.cumsum(onehot, axis=1) - onehot) * onehot, axis=2).astype(jnp.int32)
    blocks = jnp.arange(groups, dtype=jnp.int32)[:, None]
    slot = ((block_ids * groups + blocks) * cap + position).reshape(-1).astype(jnp.int32)
    count = slot.shape[0]
    owner = jnp.zeros((experts * rows,), jnp.int32).at[slot].set(jnp.arange(count, dtype=jnp.int32) + 1)
    owner = owner.reshape(experts, rows)
    flat_gates = gates.reshape(-1)

    def per_expert(packed):
        own, w_g, w_u, w_d = packed
        live = own > 0
        source = jnp.maximum(own - 1, 0)
        token_of = source // top
        inputs = jnp.where(live[:, None], tokens[token_of], jnp.zeros((), tokens.dtype))
        upward = jnp.where(live[:, None], upstream[token_of], jnp.zeros((), upstream.dtype))
        scales = jnp.where(live, flat_gates[source], jnp.zeros((), gates.dtype))
        pre_gate = contract_last(inputs, w_g)
        pre_up = contract_last(inputs, w_u)
        swish, slope = swish_pair(pre_gate)
        act = (swish * pre_up).astype(jnp.bfloat16)
        act_f = act.astype(jnp.float32)
        back = contract_last(upward, w_d)
        gate_term = jnp.sum(act_f * back, axis=1)
        scale_col = scales.astype(jnp.float32)[:, None]
        scaled = (scale_col * act_f).astype(jnp.bfloat16)
        grad_down = contract_first(scaled, upward).astype(jnp.bfloat16)
        weighted = scale_col * back
        d_gate = (weighted * pre_up * slope).astype(jnp.bfloat16)
        d_up = (weighted * swish).astype(jnp.bfloat16)
        grad_gate = contract_first(d_gate, inputs).astype(jnp.bfloat16)
        grad_up = contract_first(d_up, inputs).astype(jnp.bfloat16)
        total = jnp.zeros((rows, width), jnp.float32)
        for index in range(windows):
            low = index * window
            high = low + window
            piece = jnp.dot(d_gate[:, low:high], w_g[low:high], preferred_element_type=jnp.float32)
            piece = piece + jnp.dot(d_up[:, low:high], w_u[low:high], preferred_element_type=jnp.float32)
            piece = lax.optimization_barrier(piece.astype(jnp.bfloat16))
            total = total + piece.astype(jnp.float32)
        return total, gate_term, grad_gate, grad_up, grad_down

    totals, gate_terms, grad_w_gate, grad_w_up, grad_w_down = lax.map(per_expert, (owner, w_gate, w_up, w_down))
    totals = totals.reshape(experts * rows, width)
    gate_terms = gate_terms.reshape(-1)
    grad_x = jnp.sum(totals[slot].reshape(tokens.shape[0], top, width), axis=1).astype(jnp.bfloat16)
    grad_gates = gate_terms[slot].reshape(tokens.shape[0], top)
    return grad_x, grad_gates, grad_w_gate, grad_w_up, grad_w_down
```

```python
import functools

import jax
import jax.numpy as jnp
from jax import lax
from jax.experimental import pallas as pl
from jax.experimental.pallas import tpu as pltpu
from jax.sharding import PartitionSpec as P

MESH = pl.DeviceIdType.MESH
LANES = 128


def contract_last(left, right):
    return lax.dot_general(
        left, right, (((1,), (1,)), ((), ())), preferred_element_type=jnp.float32
    )


def contract_first(left, right):
    return lax.dot_general(
        left, right, (((0,), (0,)), ((), ())), preferred_element_type=jnp.float32
    )


def matmul(left, right):
    return jnp.dot(left, right, preferred_element_type=jnp.float32)


def one_hot(slot_row, low, count):
    index = lax.broadcasted_iota(jnp.int32, (count, slot_row.shape[1]), 0) + low
    return jnp.where(index == slot_row, 1.0, 0.0)


def merged(chunks, cap):
    lane = lax.broadcasted_iota(jnp.int32, chunks[0].shape, 1)
    row = chunks[0]
    for i in range(1, len(chunks)):
        row = jnp.where(lane < i * cap, row, chunks[i])
    return row


def kernel(
    groups, parts, cap,
    tokens_hbm, upstream_hbm, ids, gates, w_g_hbm, w_u_hbm, w_d_hbm,
    out_g, out_u, out_d, home, home_far, home_s, slots,
    tok, up, far_t, far_u, far_slots, sel_t, sel_u, sel_far, recv_t, recv_u, send_s, recv_s,
    weights, pre, flipped, straight, term, term_recv, total_s,
    pair_send, pair_recv, own_sum, side_send, side_recv, ret_send, mid_home, comb,
    w_sem, in_sem, raw_send, raw_recv, slot_send, slot_recv, scale_send, scale_recv,
    near_send, wide_fwd, dp_send, pair_fwd, side_fwd, pass_fwd, recv_sem,
    term_send, term_sem, back_send, back_recv,
    pair_send_sem, pair_recv_sem, side_send_sem, side_recv_sem, ret_sem, home_recv, mid_recv,
    comb_send, comb_recv,
):
    me, own = lax.axis_index("dp"), lax.axis_index("expert")
    core, place = lax.rem(own, 2), lax.div(own, 2)
    places = parts // 2
    partner = place * 2 + (1 - core)
    toks, part = up.shape
    near = groups // 2
    half = near * cap
    rows = groups * cap
    hid = weights.shape[2]
    per = LANES // cap
    recvs = (recv_t, recv_u)
    bf, f32 = jnp.bfloat16, jnp.float32

    def crossed(k):
        spot = me
        for bit in [1 << b for b in range(groups.bit_length()) if k >> b & 1]:
            spot = spot + bit * (1 - 2 * lax.rem(lax.div(me, bit), 2))
        return spot

    there = [crossed(k) for k in range(groups)]
    mirror = there[near]

    def aside(j):
        return lax.rem(place + j, places)

    def remote(src, dst, send_sem, sem, target):
        pltpu.make_async_remote_copy(
            src_ref=src, dst_ref=dst, send_sem=send_sem, recv_sem=sem,
            device_id=target, device_id_type=MESH,
        ).start()

    def arrived(ref, sem):
        pltpu.make_async_copy(ref, ref, sem).wait()

    load_up = pltpu.make_async_copy(upstream_hbm, up, in_sem.at[parts])
    load_up.start()
    load_tok = []
    for j in range(parts):
        load = pltpu.make_async_copy(
            tokens_hbm.at[:, pl.ds(j * part, part)], tok.at[j], in_sem.at[j]
        )
        load.start()
        load_tok.append(load)
    loads = []
    for m, w_hbm in enumerate((w_g_hbm, w_u_hbm, w_d_hbm)):
        for j in range(parts):
            load = pltpu.make_async_copy(
                w_hbm.at[:, pl.ds(j * part, part)], weights.at[m, j], w_sem.at[m, j]
            )
            load.start()
            loads.append(load)

    barrier = pltpu.get_barrier_semaphore()
    for k in range(1, groups):
        pl.semaphore_signal(barrier, inc=1, device_id={"dp": there[k]}, device_id_type=MESH)
    for j in range(1, parts):
        pl.semaphore_signal(
            barrier, inc=1, device_id={"expert": lax.rem(own + j, parts)}, device_id_type=MESH
        )

    rel = [jnp.bitwise_xor(ids[i:i + 1, :], me) for i in range(ids.shape[0])]
    padded = max(groups, 16)
    expert_of = lax.broadcasted_iota(jnp.int32, (padded, toks), 0)
    named = jnp.where(expert_of == rel[0], 1.0, 0.0)
    for other in rel[1:]:
        named = named + jnp.where(expert_of == other, 1.0, 0.0)
    earlier = lax.broadcasted_iota(jnp.int32, (toks, toks), 0)
    earlier = jnp.where(earlier < lax.broadcasted_iota(jnp.int32, (toks, toks), 1), 1.0, 0.0)
    before = matmul(named.astype(bf), earlier.astype(bf))
    picks = []
    slots[...] = jnp.full(slots.shape, -1, jnp.int32)
    for i, r in enumerate(rel):
        position = jnp.sum(jnp.where(expert_of == r, before, 0.0), axis=0, keepdims=True)
        slot = r * cap + position.astype(jnp.int32)
        slots[i:i + 1, :] = slot
        picks.append(one_hot(slot, 0, rows))
    scale_rows = None
    pick = None
    for i, p in enumerate(picks):
        gate = jnp.broadcast_to(gates[i:i + 1, :], (16, toks))
        value = contract_last(gate, p.astype(bf))
        scale_rows = value if i == 0 else scale_rows + value
        pick = p if i == 0 else pick + p
    for q in range(rows // LANES):
        send_s[q] = scale_rows[0:8, q * LANES:(q + 1) * LANES]
    recv_s[0] = send_s[0]
    pick = pick.astype(bf)

    load_up.wait()
    for load in load_tok:
        load.wait()
    pl.semaphore_wait(barrier, groups + parts - 2)

    def relay(t, k):
        spot = recvs[t].at[own, k]
        n = t * 2 + (k // near)
        if k % near:
            arrived(spot, recv_sem.at[t, own, k])
        for j in range(1, places):
            remote(spot, spot, side_fwd.at[n, j], recv_sem.at[t, own, k],
                   {"expert": aside(j) * 2 + core})
        remote(spot, spot, pair_fwd.at[n], recv_sem.at[t, own, k], {"expert": partner})

    def pass_on(t, k):
        n = t * 2 + (k // near)
        for j in range(1, places):
            part_of = aside(j) * 2 + core
            spot = recvs[t].at[part_of, k]
            arrived(spot, recv_sem.at[t, part_of, k])
            remote(spot, spot, pass_fwd.at[n, j], recv_sem.at[t, part_of, k], {"expert": partner})

    def wide(k):
        for j in range(places):
            part_of = j * 2 + core
            spot = recv_t.at[part_of, k]
            arrived(spot, recv_sem.at[0, part_of, k])
            remote(spot, spot, wide_fwd.at[j], recv_sem.at[0, part_of, k], {"expert": partner})

    def finish(h, t):
        for k in range(h * near, (h + 1) * near):
            if (h, t) == (0, 0):
                if k:
                    for j in range(places):
                        part_of = j * 2 + 1 - core
                        arrived(recv_t.at[part_of, k], recv_sem.at[0, part_of, k])
            else:
                for j in range(places):
                    part_of = aside(j) * 2 + 1 - core
                    arrived(recvs[t].at[part_of, k], recv_sem.at[t, part_of, k])

    remote(tok.at[own], far_t, raw_send.at[0], raw_recv.at[0], {"dp": mirror})
    remote(slots, far_slots, slot_send, slot_recv, {"dp": mirror})
    chosen = matmul(pick[0:half], up[...]).astype(bf).reshape(near, cap, part)
    recv_u[own, 0] = chosen[0]
    relay(1, 0)
    for k in range(1, near):
        sel_u[k] = chosen[k]
        remote(sel_u.at[k], recv_u.at[own, k], dp_send.at[0], recv_sem.at[1, own, k],
               {"dp": there[k]})
    remote(up, far_u, raw_send.at[1], raw_recv.at[1], {"dp": mirror})
    for j in range(places):
        chosen = matmul(pick[0:half], tok[j * 2 + core]).astype(bf).reshape(near, cap, part)
        recv_t[j * 2 + core, 0] = chosen[0]
        for k in range(1, near):
            sel_t[j, k] = chosen[k]
            remote(sel_t.at[j, k], recv_t.at[j * 2 + core, k], near_send.at[j],
                   recv_sem.at[0, j * 2 + core, k], {"dp": there[k]})
    for k in range(1, groups):
        remote(send_s.at[k // per], recv_s.at[k], scale_send, scale_recv.at[k], {"dp": there[k]})
    for j in range(places):
        recv_t[j * 2 + 1 - core, 0] = matmul(pick[0:cap], tok[j * 2 + 1 - core]).astype(bf)

    far_pick = [None]

    def expand(t):
        if t == 0:
            arrived(far_slots, slot_recv)
            value = one_hot(far_slots[0:1, :], half, half)
            for i in range(1, ids.shape[0]):
                value = value + one_hot(far_slots[i:i + 1, :], half, half)
            far_pick[0] = value.astype(bf)
        source = (far_t, far_u)[t]
        arrived(source, raw_recv.at[t])
        value = matmul(far_pick[0], source[...]).astype(bf).reshape(near, cap, part)
        recvs[t][own, near] = value[0]
        for k in range(1, near):
            sel_far[t, k] = value[k]
            remote(sel_far.at[t, k], recvs[t].at[own, near + k], dp_send.at[1 + t],
                   recv_sem.at[t, own, near + k], {"dp": there[k]})
        relay(t, near)

    def forward_unit(h, m, j):
        if h == 0:
            loads[m * parts + j].wait()
        block = recvs[m // 2][j, h * near:(h + 1) * near].reshape(half, part)
        value = contract_last(weights[m, j], block)
        if j == 0:
            pre[h, m] = value
        else:
            pre[h, m] = pre[h, m] + value

    tile = 32

    def activate(h):
        for k in range(max(1, h * near), (h + 1) * near):
            arrived(recv_s.at[k], scale_recv.at[k])
        scale = jnp.concatenate(
            [merged([recv_s[q * per + i] for i in range(per)], cap)
             for q in range(h * half // LANES, (h + 1) * half // LANES)], axis=1
        )[0:1, :]
        term[h] = jnp.zeros((8, half), f32)

        @pl.loop(0, hid // tile)
        def _(step):
            at = pl.ds(pl.multiple_of(step * tile, tile), tile)
            columns = pl.ds(h * half, half)
            gate, lift, back = pre[h, 0, at, :], pre[h, 1, at, :], pre[h, 2, at, :]
            sigma = jax.nn.sigmoid(gate)
            swish = gate * sigma
            slope = sigma * (1.0 + gate * (1.0 - sigma))
            act = (swish * lift).astype(bf).astype(f32)
            term[h] += jnp.broadcast_to(jnp.sum(act * back, axis=0, keepdims=True), (8, half))
            weighted = scale * back
            flipped[0, at, columns] = (weighted * lift * slope).astype(bf)
            flipped[1, at, columns] = (weighted * swish).astype(bf)
            flipped[2, at, columns] = (scale * act).astype(bf)

        for j in range(1, parts):
            remote(term.at[h], term_recv.at[h, own], term_send.at[h], term_sem.at[h, own],
                   {"expert": lax.rem(own + j, parts)})
        for m in range(2):
            block = flipped[m, :, h * half:(h + 1) * half].astype(f32)
            straight[h, m] = jnp.transpose(block).astype(bf)

    def piece(h, which):
        value = matmul(straight[h, 0], weights[0, which])
        value = value + matmul(straight[h, 1], weights[1, which])
        return value.reshape(near, cap, part)

    def pair_step(h, j):
        spot = aside(j) * 2
        pair_send[h, j] = piece(h, spot + 1 - core).astype(bf)
        remote(pair_send.at[h, j], pair_recv.at[h, j], pair_send_sem.at[h, j],
               pair_recv_sem.at[h, j], {"expert": partner})
        own_sum[h, j] = piece(h, spot + core)

    def side_step(h, j):
        arrived(pair_recv.at[h, j], pair_recv_sem.at[h, j])
        for k in list(range(1, near)) + [0]:
            both = own_sum[h, j, k] + pair_recv[h, j, k].astype(f32)
            side_send[h, j, k] = both.astype(bf)
            remote(side_send.at[h, j, k], side_recv.at[h, j, k], side_send_sem.at[h, j],
                   side_recv_sem.at[h, j, k], {"expert": aside(j) * 2 + core})

    def return_step(h, k):
        if k == 1 % near:
            arrived(pair_recv.at[h, 0], pair_recv_sem.at[h, 0])
        value = own_sum[h, 0, k] + pair_recv[h, 0, k].astype(f32)
        for j in range(1, places):
            arrived(side_recv.at[h, j, k], side_recv_sem.at[h, j, k])
            value = value + side_recv[h, j, k].astype(f32)
        goal, sem = ((home, home_recv), (mid_home, mid_recv))[h]
        if k == 0:
            goal[0] = value.astype(bf)
        else:
            ret_send[h, k] = value.astype(bf)
            remote(ret_send.at[h, k], goal.at[k], ret_sem.at[h], sem.at[k], {"dp": there[k]})

    def term_step(h):
        for j in range(1, parts):
            other = lax.rem(own + j, parts)
            arrived(term_recv.at[h, other], term_sem.at[h, other])
        term_recv[h, own] = term[h]
        total = term_recv[h, 0]
        for j in range(1, parts):
            total = total + term_recv[h, j]
        for q in range(half // LANES):
            total_s[h * half // LANES + q] = total[:, q * LANES:(q + 1) * LANES]
        for k in range(h * near, (h + 1) * near):
            if k == 0:
                home_s[0] = total_s[0]
            else:
                remote(total_s.at[k // per], home_s.at[k], back_send, back_recv.at[k],
                       {"dp": there[k]})

    def grad_unit(m, j):
        block = recvs[m // 2][j].reshape(rows, part)
        (out_g, out_u, out_d)[m][:, j * part:(j + 1) * part] = matmul(flipped[m], block).astype(bf)

    grads = [(m, j) for m in range(3) for j in range(parts)]

    def some_grads(count):
        for _ in range(count):
            if grads:
                grad_unit(*grads.pop(0))

    relay(1, 1)
    pass_on(1, 0)
    wide(1)
    expand(0)
    for k in range(2, near):
        relay(1, k)
        relay(0, near + k - 1)
        pass_on(1, k - 1)
        pass_on(0, near + k - 2)
        wide(k)
    relay(0, rows // cap - 1)
    pass_on(1, near - 1)
    finish(0, 0)
    expand(1)
    for m in range(2):
        for j in range(parts):
            forward_unit(0, m, j)
        if m == 0:
            pass_on(0, groups - 2)
            relay(1, near + 1)
    finish(0, 1)
    for j in range(parts):
        forward_unit(0, 2, j)
    pass_on(0, groups - 1)
    pass_on(1, near)
    for k in range(near + 2, groups):
        relay(1, k)
        pass_on(1, k - 1)
    activate(0)
    pass_on(1, groups - 1)
    for j in list(range(1, places)) + [0]:
        pair_step(0, j)
    for j in range(1, places):
        side_step(0, j)
    finish(1, 0)
    for m in range(2):
        for j in range(parts):
            forward_unit(1, m, j)
    finish(1, 1)
    for j in range(parts):
        forward_unit(1, 2, j)
    activate(1)
    for j in list(range(1, places)) + [0]:
        pair_step(1, j)
    for j in range(1, places):
        side_step(1, j)
    term_step(0)
    term_step(1)
    share = -(-len(grads) // (2 * near))
    order = list(range(1, near)) + [0]
    for k in order:
        return_step(0, k)
        some_grads(share)
    for k in order:
        return_step(1, k)
        some_grads(share)
    some_grads(len(grads))
    for k in range(1, near):
        arrived(mid_home.at[k], mid_recv.at[k])
    value = far_pick[0]
    comb[...] = contract_first(value, mid_home[...].reshape(half, part)).astype(bf)
    remote(comb, home_far, comb_send, comb_recv, {"dp": mirror})

    for k in range(1, near):
        arrived(home.at[k], home_recv.at[k])
    for k in range(1, groups):
        arrived(home_s.at[k], back_recv.at[k])
    arrived(home_far, comb_recv)

    few, all_near = recv_t.at[0, pl.ds(0, near - 1)], recv_t.at[0, pl.ds(0, near)]
    for t in range(2):
        arrived((far_t, far_u)[t], raw_send.at[t])
    arrived(far_slots, slot_send)
    arrived(recv_s.at[pl.ds(0, groups - 1)], scale_send)
    for j in range(places):
        arrived(few, near_send.at[j])
        arrived(few, wide_fwd.at[j])
    for i in range(3):
        arrived(few, dp_send.at[i])
    for n in range(1, 4):
        arrived(all_near, pair_fwd.at[n])
        for j in range(1, places):
            arrived(all_near, side_fwd.at[n, j])
            arrived(all_near, pass_fwd.at[n, j])
    for h in range(2):
        arrived(term_recv.at[h, pl.ds(0, parts - 1)], term_send.at[h])
        arrived(few, ret_sem.at[h])
        for j in range(places):
            arrived(pair_send.at[h, j], pair_send_sem.at[h, j])
            if j:
                arrived(side_send.at[h, j], side_send_sem.at[h, j])
    arrived(home_s.at[pl.ds(0, groups - 1)], back_send)
    arrived(comb, comb_send)


def exchange(tokens, upstream, ids, gates, w_gate, w_up, w_down, groups, parts, cap):
    toks, part = upstream.shape
    rows = groups * cap
    near = groups // 2
    half = near * cap
    hid, width = w_gate.shape
    places = parts // 2
    bf, f32 = jnp.bfloat16, jnp.float32
    dma = pltpu.SemaphoreType.DMA
    vmem = pl.BlockSpec(memory_space=pltpu.VMEM)
    hbm = pl.BlockSpec(memory_space=pl.ANY)
    return pl.pallas_call(
        functools.partial(kernel, groups, parts, cap),
        out_shape=(
            pltpu.VMEM((hid, width), bf), pltpu.VMEM((hid, width), bf), pltpu.VMEM((hid, width), bf),
            pltpu.VMEM((near, cap, part), bf), pltpu.VMEM((toks, part), bf),
            pltpu.VMEM((groups, 8, LANES), f32), pltpu.VMEM((8, toks), jnp.int32),
        ),
        in_specs=[hbm, hbm, vmem, vmem, hbm, hbm, hbm],
        out_specs=(vmem,) * 7,
        scratch_shapes=[
            pltpu.VMEM((parts, toks, part), bf),
            pltpu.VMEM((toks, part), bf),
            pltpu.VMEM((toks, part), bf),
            pltpu.VMEM((toks, part), bf),
            pltpu.VMEM((8, toks), jnp.int32),
            pltpu.VMEM((places, near, cap, part), bf),
            pltpu.VMEM((near, cap, part), bf),
            pltpu.VMEM((2, near, cap, part), bf),
            pltpu.VMEM((parts, groups, cap, part), bf),
            pltpu.VMEM((parts, groups, cap, part), bf),
            pltpu.VMEM((rows // LANES, 8, LANES), f32),
            pltpu.VMEM((groups, 8, LANES), f32),
            pltpu.VMEM((3, parts, hid, part), bf),
            pltpu.VMEM((2, 3, hid, half), f32),
            pltpu.VMEM((3, hid, rows), bf),
            pltpu.VMEM((2, 2, half, hid), bf),
            pltpu.VMEM((2, 8, half), f32),
            pltpu.VMEM((2, parts, 8, half), f32),
            pltpu.VMEM((rows // LANES, 8, LANES), f32),
            pltpu.VMEM((2, places, near, cap, part), bf),
            pltpu.VMEM((2, places, near, cap, part), bf),
            pltpu.VMEM((2, places, near, cap, part), f32),
            pltpu.VMEM((2, places, near, cap, part), bf),
            pltpu.VMEM((2, places, near, cap, part), bf),
            pltpu.VMEM((2, near, cap, part), bf),
            pltpu.VMEM((near, cap, part), bf),
            pltpu.VMEM((toks, part), bf),
            dma((3, parts)), dma((parts + 1,)), dma((2,)), dma((2,)), dma, dma, dma, dma((groups,)),
            dma((places,)), dma((places,)), dma((3,)), dma((4,)), dma((4, places)),
            dma((4, places)), dma((2, parts, groups)),
            dma((2,)), dma((2, parts)), dma, dma((groups,)),
            dma((2, places)), dma((2, places)), dma((2, places)), dma((2, places, near)),
            dma((2,)), dma((near,)), dma((near,)), dma, dma,
        ],
        compiler_params=pltpu.CompilerParams(
            collective_id=0, has_side_effects=True, vmem_limit_bytes=46 * 1024 * 1024
        ),
    )(tokens, upstream, ids, gates, w_gate, w_up, w_down)


def closing(
    groups, cap, top, grad_g, grad_u, grad_d, home, home_far, home_s, slots,
    out_x, out_gates, out_g, out_u, out_d, sems,
):
    copies = []
    for i, (src, dst) in enumerate(((grad_g, out_g), (grad_u, out_u), (grad_d, out_d))):
        copy = pltpu.make_async_copy(src, dst, sems.at[i])
        copy.start()
        copies.append(copy)
    near, _, part = home.shape
    rows, half = groups * cap, near * cap
    per = LANES // cap
    picks = [one_hot(slots[i:i + 1, :], 0, rows) for i in range(top)]
    pick = picks[0][0:half]
    for p in picks[1:]:
        pick = pick + p[0:half]
    value = contract_first(pick.astype(jnp.bfloat16), home[...].reshape(half, part))
    out_x[...] = (value + home_far[...].astype(jnp.float32)).astype(jnp.bfloat16)
    terms = jnp.concatenate(
        [merged([home_s[q * per + i] for i in range(per)], cap) for q in range(rows // LANES)],
        axis=1,
    )
    for i, p in enumerate(picks):
        value = jnp.dot(terms, p, precision=lax.Precision.HIGHEST,
                        preferred_element_type=jnp.float32)
        out_gates[i:i + 1, :] = value[0:1, :]
    for copy in copies:
        copy.wait()


def close(grads, home, home_far, home_s, slots, groups, cap, top):
    vmem = pl.BlockSpec(memory_space=pltpu.VMEM)
    hbm = pl.BlockSpec(memory_space=pl.ANY)
    toks, part = home_far.shape
    operands = [
        pltpu.with_memory_space_constraint(v, pltpu.VMEM)
        for v in (*grads, home, home_far, home_s, slots)
    ]
    return pl.pallas_call(
        functools.partial(closing, groups, cap, top),
        out_shape=(
            jax.ShapeDtypeStruct((toks, part), jnp.bfloat16),
            jax.ShapeDtypeStruct((top, toks), jnp.float32),
            *[jax.ShapeDtypeStruct(g.shape, g.dtype) for g in grads],
        ),
        in_specs=[vmem] * 7,
        out_specs=(vmem, vmem, hbm, hbm, hbm),
        scratch_shapes=[pltpu.SemaphoreType.DMA((3,))],
        compiler_params=pltpu.CompilerParams(vmem_limit_bytes=8 * 1024 * 1024),
    )(*operands)


def per_device(tokens, upstream, gates, expert_ids, w_gate, w_up, w_down):
    groups = lax.axis_size("dp")
    parts = lax.axis_size("expert")
    experts = groups * w_gate.shape[0]
    toks = tokens.shape[0]
    top = expert_ids.shape[1]
    cap = 2 * toks * top // experts
    *grads, home, home_far, home_s, slots = exchange(
        tokens, upstream, expert_ids.T, gates.T, w_gate[0], w_up[0], w_down[0], groups, parts, cap
    )
    grad_x, grad_gates, *grads = close(grads, home, home_far, home_s, slots, groups, cap, top)
    return (grad_x, grad_gates.T, *[g[None] for g in grads])


def solution(mesh):
    in_specs = (
        P("dp", None),
        P("dp", "expert"),
        P("dp", None),
        P("dp", None),
        P("dp", "expert", None),
        P("dp", "expert", None),
        P("dp", "expert", None),
    )
    out_specs = (
        P("dp", "expert"),
        P("dp", None),
        P("dp", "expert", None),
        P("dp", "expert", None),
        P("dp", "expert", None),
    )
    return jax.shard_map(
        per_device, mesh=mesh, in_specs=in_specs, out_specs=out_specs, check_vma=False
    )
```

```python
import functools

import jax
import jax.numpy as jnp
from jax import lax
from jax.experimental import pallas as pl
from jax.experimental.pallas import tpu as pltpu
from jax.sharding import PartitionSpec as P

MESH = pl.DeviceIdType.MESH
LANES = 128


def contract_last(left, right):
    return lax.dot_general(
        left, right, (((1,), (1,)), ((), ())), preferred_element_type=jnp.float32
    )


def contract_first(left, right):
    return lax.dot_general(
        left, right, (((0,), (0,)), ((), ())), preferred_element_type=jnp.float32
    )


def matmul(left, right):
    return jnp.dot(left, right, preferred_element_type=jnp.float32)


def one_hot(slot_row, low, count):
    index = lax.broadcasted_iota(jnp.int32, (count, slot_row.shape[1]), 0) + low
    return jnp.where(index == slot_row, 1.0, 0.0)


def merged(chunks, cap):
    lane = lax.broadcasted_iota(jnp.int32, chunks[0].shape, 1)
    row = chunks[0]
    for i in range(1, len(chunks)):
        row = jnp.where(lane < i * cap, row, chunks[i])
    return row


def kernel(
    groups, parts, cap,
    tokens_hbm, upstream_hbm, ids, gates, w_g_hbm, w_u_hbm, w_d_hbm,
    out_g, out_u, out_d, home, home_far, home_s, slots,
    tok, up, far_t, far_u, far_slots, far_pick, sel_t, sel_u, sel_far, recv_t, recv_u, send_s, recv_s,
    w_gu, w_down, pre_gu, pre_down, flip_gu, flip_down, straight, term, term_recv, total_s,
    pair_send, pair_recv, own_sum, side_send, side_recv, ret_send, mid_home, comb,
    w_sem, in_sem, raw_send, raw_recv, slot_send, slot_recv, scale_send, scale_recv,
    near_send, wide_fwd, dp_send, pair_fwd, side_fwd, pass_fwd, recv_sem,
    term_send, term_sem, back_send, back_recv,
    pair_send_sem, pair_recv_sem, side_send_sem, side_recv_sem, ret_sem, home_recv, mid_recv,
    comb_send, comb_recv,
):
    me, own = lax.axis_index("dp"), lax.axis_index("expert")
    core, place = lax.rem(own, 2), lax.div(own, 2)
    places = parts // 2
    partner = place * 2 + (1 - core)
    toks, part = up.shape
    near = groups // 2
    half = near * cap
    rows = groups * cap
    hid = w_down.shape[1]
    per = LANES // cap
    chunks, wide_part = comb.shape[0], comb.shape[2]
    order = list(range(1, near)) + [0]
    recvs = (recv_t, recv_u)
    bf, f32 = jnp.bfloat16, jnp.float32

    def crossed(k):
        spot = me
        for bit in [1 << b for b in range(groups.bit_length()) if k >> b & 1]:
            spot = spot + bit * (1 - 2 * lax.rem(lax.div(me, bit), 2))
        return spot

    there = [crossed(k) for k in range(groups)]
    mirror = there[near]

    def aside(j):
        return lax.rem(place + j, places)

    def arrived(ref, sem):
        pltpu.make_async_copy(ref, ref, sem).wait()

    load_up = pltpu.make_async_copy(upstream_hbm, up, in_sem.at[parts])
    load_up.start()
    load_tok = []
    for j in range(parts):
        load = pltpu.make_async_copy(
            tokens_hbm.at[:, pl.ds(j * part, part)], tok.at[j], in_sem.at[j]
        )
        load.start()
        load_tok.append(load)
    barrier = pltpu.get_barrier_semaphore()
    for k in range(1, groups):
        pl.semaphore_signal(barrier, inc=1, device_id={"dp": there[k]}, device_id_type=MESH)
    for j in range(1, parts):
        pl.semaphore_signal(
            barrier, inc=1, device_id={"expert": lax.rem(own + j, parts)}, device_id_type=MESH
        )

    rel = [jnp.bitwise_xor(ids[i:i + 1, :], me) for i in range(ids.shape[0])]
    padded = max(groups, 16)
    expert_of = lax.broadcasted_iota(jnp.int32, (padded, toks), 0)
    named = jnp.where(expert_of == rel[0], 1.0, 0.0)
    for other in rel[1:]:
        named = named + jnp.where(expert_of == other, 1.0, 0.0)
    earlier = lax.broadcasted_iota(jnp.int32, (toks, toks), 0)
    earlier = jnp.where(earlier < lax.broadcasted_iota(jnp.int32, (toks, toks), 1), 1.0, 0.0)
    before = matmul(named.astype(bf), earlier.astype(bf))
    slots[...] = jnp.full(slots.shape, -1, jnp.int32)
    for i, r in enumerate(rel):
        position = jnp.sum(jnp.where(expert_of == r, before, 0.0), axis=0, keepdims=True)
        slots[i:i + 1, :] = r * cap + position.astype(jnp.int32)

    def remote(src, dst, send_sem, sem, target):
        pltpu.make_async_remote_copy(
            src_ref=src, dst_ref=dst, send_sem=send_sem, recv_sem=sem,
            device_id=target, device_id_type=MESH,
        ).start()

    load_up.wait()
    for load in load_tok:
        load.wait()
    pl.semaphore_wait(barrier, groups + parts - 2)
    remote(tok.at[own], far_t, raw_send.at[0], raw_recv.at[0], {"dp": mirror})
    remote(slots, far_slots, slot_send, slot_recv, {"dp": mirror})
    loads = {}
    for t in (1, 0):
        for j in range(parts):
            columns = pl.ds(j * part, part)
            if t:
                pairs = [(w_d_hbm.at[:, columns], w_down.at[j], 2)]
            else:
                pairs = [(w_g_hbm.at[:, columns], w_gu.at[j, pl.ds(0, hid)], 0),
                         (w_u_hbm.at[:, columns], w_gu.at[j, pl.ds(hid, hid)], 1)]
            loads[t, j] = [pltpu.make_async_copy(src, dst, w_sem.at[m, j]) for src, dst, m in pairs]
            for load in loads[t, j]:
                load.start()

    picks = [one_hot(slots[i:i + 1, :], 0, rows) for i in range(len(rel))]
    scale_rows = None
    pick = None
    for i, p in enumerate(picks):
        gate = jnp.broadcast_to(gates[i:i + 1, :], (16, toks))
        value = contract_last(gate, p.astype(bf))
        scale_rows = value if i == 0 else scale_rows + value
        pick = p if i == 0 else pick + p
    for q in range(rows // LANES):
        send_s[q] = scale_rows[0:8, q * LANES:(q + 1) * LANES]
    recv_s[0] = send_s[0]
    pick = pick.astype(bf)

    def relay(t, k):
        spot = recvs[t].at[own, k]
        n = t * 2 + (k // near)
        if k % near:
            arrived(spot, recv_sem.at[t, own, k])
        for j in range(1, places):
            remote(spot, spot, side_fwd.at[n, j], recv_sem.at[t, own, k],
                   {"expert": aside(j) * 2 + core})
        remote(spot, spot, pair_fwd.at[n], recv_sem.at[t, own, k], {"expert": partner})

    def pass_on(t, k):
        n = t * 2 + (k // near)
        for j in range(1, places):
            part_of = aside(j) * 2 + core
            spot = recvs[t].at[part_of, k]
            arrived(spot, recv_sem.at[t, part_of, k])
            remote(spot, spot, pass_fwd.at[n, j], recv_sem.at[t, part_of, k], {"expert": partner})

    def wide(k):
        for j in range(places):
            part_of = j * 2 + core
            spot = recv_t.at[part_of, k]
            arrived(spot, recv_sem.at[0, part_of, k])
            remote(spot, spot, wide_fwd.at[j], recv_sem.at[0, part_of, k], {"expert": partner})

    def finish(h, t):
        for k in range(h * near, (h + 1) * near):
            if (h, t) == (0, 0):
                if k:
                    for j in range(places):
                        part_of = j * 2 + 1 - core
                        arrived(recv_t.at[part_of, k], recv_sem.at[0, part_of, k])
            else:
                for j in range(places):
                    part_of = aside(j) * 2 + 1 - core
                    arrived(recvs[t].at[part_of, k], recv_sem.at[t, part_of, k])

    chosen = matmul(pick[0:half], up[...]).astype(bf).reshape(near, cap, part)
    recv_u[own, 0] = chosen[0]
    relay(1, 0)
    for k in range(1, near):
        sel_u[k] = chosen[k]
        remote(sel_u.at[k], recv_u.at[own, k], dp_send.at[0], recv_sem.at[1, own, k],
               {"dp": there[k]})
    remote(up, far_u, raw_send.at[1], raw_recv.at[1], {"dp": mirror})
    for j in range(places):
        chosen = matmul(pick[0:half], tok[j * 2 + core]).astype(bf).reshape(near, cap, part)
        recv_t[j * 2 + core, 0] = chosen[0]
        for k in range(1, near):
            sel_t[j, k] = chosen[k]

    def send_wide(k):
        for j in range(places):
            spot = j * 2 + core
            remote(sel_t.at[j, k], recv_t.at[spot, k], near_send.at[j], recv_sem.at[0, spot, k],
                   {"dp": there[k]})

    for k in range(1, groups):
        remote(send_s.at[k // per], recv_s.at[k], scale_send, scale_recv.at[k], {"dp": there[k]})
    for j in range(places):
        recv_t[j * 2 + 1 - core, 0] = matmul(pick[0:cap], tok[j * 2 + 1 - core]).astype(bf)

    def expand(t):
        if t == 0:
            arrived(far_slots, slot_recv)
            value = one_hot(far_slots[0:1, :], half, half)
            for i in range(1, ids.shape[0]):
                value = value + one_hot(far_slots[i:i + 1, :], half, half)
            far_pick[...] = value.astype(bf)
        source = (far_t, far_u)[t]
        arrived(source, raw_recv.at[t])
        value = matmul(far_pick[...], source[...]).astype(bf).reshape(near, cap, part)
        recvs[t][own, near] = value[0]
        for k in range(1, near):
            sel_far[t, k] = value[k]
            remote(sel_far.at[t, k], recvs[t].at[own, near + k], dp_send.at[1 + t],
                   recv_sem.at[t, own, near + k], {"dp": there[k]})
        relay(t, near)
        if t == 1:
            for k in range(1, near):
                send_wide(k)

    def forward_unit(h, t, j):
        if h == 1 - t:
            for load in loads[t, j]:
                load.wait()
        block = recvs[t][j, h * near:(h + 1) * near].reshape(half, part)
        pre = (pre_gu, pre_down)[t]
        value = contract_last((w_gu, w_down)[t][j], block)
        if j == 0:
            pre[h] = value
        else:
            pre[h] = pre[h] + value

    tile = 32

    def activate(h):
        for k in range(max(1, h * near), (h + 1) * near):
            arrived(recv_s.at[k], scale_recv.at[k])
        scale = jnp.concatenate(
            [merged([recv_s[q * per + i] for i in range(per)], cap)
             for q in range(h * half // LANES, (h + 1) * half // LANES)], axis=1
        )[0:1, :]
        term[h] = jnp.zeros((8, half), f32)

        @pl.loop(0, hid // tile)
        def _(step):
            low = pl.multiple_of(step * tile, tile)
            at = pl.ds(low, tile)
            above = pl.ds(pl.multiple_of(low + hid, tile), tile)
            columns = pl.ds(h * half, half)
            gate, lift, back = pre_gu[h, at, :], pre_gu[h, above, :], pre_down[h, at, :]
            sigma = jax.nn.sigmoid(gate)
            swish = gate * sigma
            slope = sigma * (1.0 + gate * (1.0 - sigma))
            act = (swish * lift).astype(bf).astype(f32)
            term[h] += jnp.broadcast_to(jnp.sum(act * back, axis=0, keepdims=True), (8, half))
            weighted = scale * back
            flip_gu[at, columns] = (weighted * lift * slope).astype(bf)
            flip_gu[above, columns] = (weighted * swish).astype(bf)
            flip_down[at, columns] = (scale * act).astype(bf)

        for j in range(1, parts):
            remote(term.at[h], term_recv.at[h, own], term_send.at[h], term_sem.at[h, own],
                   {"expert": lax.rem(own + j, parts)})
        block = flip_gu[:, h * half:(h + 1) * half].astype(f32)
        straight[h] = jnp.transpose(block).astype(bf)

    def piece(h, c, which):
        columns = pl.ds(c * wide_part, wide_part)
        value = matmul(straight[h], w_gu[which, :, columns])
        return value.reshape(near, cap, wide_part)

    def pair_step(h, c, j):
        spot = aside(j) * 2
        pair_send[h, c, j] = piece(h, c, spot + 1 - core).astype(bf)
        remote(pair_send.at[h, c, j], pair_recv.at[h, c, j], pair_send_sem.at[h, c, j],
               pair_recv_sem.at[h, c, j], {"expert": partner})
        own_sum[h, c, j] = piece(h, c, spot + core)

    def side_step(h, c, j):
        arrived(pair_recv.at[h, c, j], pair_recv_sem.at[h, c, j])
        for k in order:
            both = own_sum[h, c, j, k] + pair_recv[h, c, j, k].astype(f32)
            side_send[h, c, j, k] = both.astype(bf)
            remote(side_send.at[h, c, j, k], side_recv.at[h, c, j, k], side_send_sem.at[h, c, j],
                   side_recv_sem.at[h, c, j, k], {"expert": aside(j) * 2 + core})

    def return_step(h, c, k):
        if k == order[0]:
            arrived(pair_recv.at[h, c, 0], pair_recv_sem.at[h, c, 0])
        value = own_sum[h, c, 0, k] + pair_recv[h, c, 0, k].astype(f32)
        for j in range(1, places):
            arrived(side_recv.at[h, c, j, k], side_recv_sem.at[h, c, j, k])
            value = value + side_recv[h, c, j, k].astype(f32)
        goal, sem = ((home, home_recv), (mid_home, mid_recv))[h]
        if k == 0:
            goal[c, 0] = value.astype(bf)
        else:
            ret_send[h, c, k] = value.astype(bf)
            remote(ret_send.at[h, c, k], goal.at[c, k], ret_sem.at[h, c], sem.at[c, k],
                   {"dp": there[k]})

    def combine(c):
        for k in range(1, near):
            arrived(mid_home.at[c, k], mid_recv.at[c, k])
        value = contract_first(far_pick[...], mid_home[c].reshape(half, wide_part))
        comb[c] = value.astype(bf)
        remote(comb.at[c], home_far.at[c], comb_send.at[c], comb_recv.at[c], {"dp": mirror})

    def term_step(h):
        for j in range(1, parts):
            other = lax.rem(own + j, parts)
            arrived(term_recv.at[h, other], term_sem.at[h, other])
        term_recv[h, own] = term[h]
        total = term_recv[h, 0]
        for j in range(1, parts):
            total = total + term_recv[h, j]
        for q in range(half // LANES):
            total_s[h * half // LANES + q] = total[:, q * LANES:(q + 1) * LANES]
        for k in range(h * near, (h + 1) * near):
            if k == 0:
                home_s[0] = total_s[0]
            else:
                remote(total_s.at[k // per], home_s.at[k], back_send, back_recv.at[k],
                       {"dp": there[k]})

    def grad_unit(m, j):
        block = recvs[m // 2][j].reshape(rows, part)
        left = flip_down[...] if m == 2 else flip_gu[m * hid:(m + 1) * hid, :]
        (out_g, out_u, out_d)[m][:, j * part:(j + 1) * part] = matmul(left, block).astype(bf)

    grads = [(m, j) for m in range(3) for j in range(parts)]

    def some_grads(count):
        for _ in range(count):
            if grads:
                grad_unit(*grads.pop(0))

    def near_up():
        finish(0, 1)
        for j in range(parts):
            forward_unit(0, 1, j)

    later = range(2, near)
    far_later = [near + k for k in later]
    outer_steps = (
        [(relay, 1, 1), (pass_on, 1, 0)] + [(relay, 1, k) for k in later]
        + [(expand, 0), (pass_on, 1, 1), (relay, 0, near + 1)]
        + [(pass_on, 1, k) for k in later] + [(relay, 0, k) for k in far_later]
        + [(pass_on, 0, near), (expand, 1), (near_up,), (pass_on, 0, near + 1)]
        + [(relay, 1, near + 1)] + [(pass_on, 0, k) for k in far_later[:1]]
        + [(relay, 1, k) for k in far_later] + [(pass_on, 0, k) for k in far_later[1:]]
    )
    inner_steps = (
        [(relay, 1, 1), (pass_on, 1, 0), (expand, 0), (pass_on, 1, 1)]
        + [(relay, 1, k) for k in later] + [(relay, 0, near + 1), (pass_on, 0, near), (expand, 1)]
        + [(pass_on, 1, k) for k in later] + [(near_up,), (relay, 1, near + 1)]
        + [(relay, 0, k) for k in far_later] + [(pass_on, 0, near + 1)]
        + [(relay, 1, k) for k in far_later] + [(pass_on, 0, k) for k in far_later]
    )
    inner = lax.rem(lax.div(me, near) + lax.div(me, max(1, near // 2)), 2) == 1

    def run(steps):
        for step, *at in steps:
            step(*at)

    pl.when(inner)(functools.partial(run, inner_steps))
    pl.when(jnp.logical_not(inner))(functools.partial(run, outer_steps))
    finish(1, 0)
    for j in range(parts):
        if j < near:
            pass_on(1, near + j)
        forward_unit(1, 0, j)
    for k in range(near + parts, groups):
        pass_on(1, k)
    finish(1, 1)
    for j in range(parts):
        forward_unit(1, 1, j)
    activate(1)
    aside_first = list(range(1, places)) + [0]
    for c in range(chunks):
        for j in aside_first[:-1]:
            pair_step(1, c, j)
            side_step(1, c, j)
    for c in range(chunks):
        pair_step(1, c, 0)
    for k in range(1, near):
        wide(k)
    finish(0, 0)
    for j in range(parts):
        if j == parts // 2:
            for k in order:
                return_step(1, 0, k)
        forward_unit(0, 0, j)
    activate(0)
    for c in range(chunks):
        for j in aside_first[:-1]:
            pair_step(0, c, j)
            side_step(0, c, j)
        if c + 1 < chunks:
            for k in order:
                return_step(1, c + 1, k)
    for c in range(chunks):
        pair_step(0, c, 0)
    term_step(1)
    term_step(0)
    combine(0)
    some_grads(parts)
    for c in range(1, chunks):
        combine(c)
    for c in range(chunks):
        for k in order:
            return_step(0, c, k)
            some_grads(1)
    some_grads(len(grads))

    for c in range(chunks):
        for k in range(1, near):
            arrived(home.at[c, k], home_recv.at[c, k])
        arrived(home_far.at[c], comb_recv.at[c])
    for k in range(1, groups):
        arrived(home_s.at[k], back_recv.at[k])

    few, all_near = recv_t.at[0, pl.ds(0, near - 1)], recv_t.at[0, pl.ds(0, near)]
    for t in range(2):
        arrived((far_t, far_u)[t], raw_send.at[t])
    arrived(far_slots, slot_send)
    arrived(recv_s.at[pl.ds(0, groups - 1)], scale_send)
    for j in range(places):
        arrived(few, near_send.at[j])
        arrived(few, wide_fwd.at[j])
    for i in range(3):
        arrived(few, dp_send.at[i])
    for n in range(1, 4):
        arrived(all_near, pair_fwd.at[n])
        for j in range(1, places):
            arrived(all_near, side_fwd.at[n, j])
            arrived(all_near, pass_fwd.at[n, j])
    for h in range(2):
        arrived(term_recv.at[h, pl.ds(0, parts - 1)], term_send.at[h])
        for c in range(chunks):
            arrived(ret_send.at[h, c, pl.ds(0, near - 1)], ret_sem.at[h, c])
            for j in range(places):
                arrived(pair_send.at[h, c, j], pair_send_sem.at[h, c, j])
                if j:
                    arrived(side_send.at[h, c, j], side_send_sem.at[h, c, j])
    arrived(home_s.at[pl.ds(0, groups - 1)], back_send)
    for c in range(chunks):
        arrived(comb.at[c], comb_send.at[c])


def exchange(tokens, upstream, ids, gates, w_gate, w_up, w_down, groups, parts, cap):
    toks, part = upstream.shape
    rows = groups * cap
    near = groups // 2
    half = near * cap
    hid, width = w_gate.shape
    places = parts // 2
    chunks = 2
    wide_part = part // chunks
    bf, f32 = jnp.bfloat16, jnp.float32
    dma = pltpu.SemaphoreType.DMA
    vmem = pl.BlockSpec(memory_space=pltpu.VMEM)
    hbm = pl.BlockSpec(memory_space=pl.ANY)
    return pl.pallas_call(
        functools.partial(kernel, groups, parts, cap),
        out_shape=(
            pltpu.VMEM((hid, width), bf), pltpu.VMEM((hid, width), bf), pltpu.VMEM((hid, width), bf),
            pltpu.VMEM((chunks, near, cap, wide_part), bf), pltpu.VMEM((chunks, toks, wide_part), bf),
            pltpu.VMEM((groups, 8, LANES), f32), pltpu.VMEM((8, toks), jnp.int32),
        ),
        in_specs=[hbm, hbm, vmem, vmem, hbm, hbm, hbm],
        out_specs=(vmem,) * 7,
        scratch_shapes=[
            pltpu.VMEM((parts, toks, part), bf),
            pltpu.VMEM((toks, part), bf),
            pltpu.VMEM((toks, part), bf),
            pltpu.VMEM((toks, part), bf),
            pltpu.VMEM((8, toks), jnp.int32),
            pltpu.VMEM((half, toks), bf),
            pltpu.VMEM((places, near, cap, part), bf),
            pltpu.VMEM((near, cap, part), bf),
            pltpu.VMEM((2, near, cap, part), bf),
            pltpu.VMEM((parts, groups, cap, part), bf),
            pltpu.VMEM((parts, groups, cap, part), bf),
            pltpu.VMEM((rows // LANES, 8, LANES), f32),
            pltpu.VMEM((groups, 8, LANES), f32),
            pltpu.VMEM((parts, 2 * hid, part), bf),
            pltpu.VMEM((parts, hid, part), bf),
            pltpu.VMEM((2, 2 * hid, half), f32),
            pltpu.VMEM((2, hid, half), f32),
            pltpu.VMEM((2 * hid, rows), bf),
            pltpu.VMEM((hid, rows), bf),
            pltpu.VMEM((2, half, 2 * hid), bf),
            pltpu.VMEM((2, 8, half), f32),
            pltpu.VMEM((2, parts, 8, half), f32),
            pltpu.VMEM((rows // LANES, 8, LANES), f32),
            pltpu.VMEM((2, chunks, places, near, cap, wide_part), bf),
            pltpu.VMEM((2, chunks, places, near, cap, wide_part), bf),
            pltpu.VMEM((2, chunks, places, near, cap, wide_part), f32),
            pltpu.VMEM((2, chunks, places, near, cap, wide_part), bf),
            pltpu.VMEM((2, chunks, places, near, cap, wide_part), bf),
            pltpu.VMEM((2, chunks, near, cap, wide_part), bf),
            pltpu.VMEM((chunks, near, cap, wide_part), bf),
            pltpu.VMEM((chunks, toks, wide_part), bf),
            dma((3, parts)), dma((parts + 1,)), dma((2,)), dma((2,)), dma, dma, dma, dma((groups,)),
            dma((places,)), dma((places,)), dma((3,)), dma((4,)), dma((4, places)),
            dma((4, places)), dma((2, parts, groups)),
            dma((2,)), dma((2, parts)), dma, dma((groups,)),
            dma((2, chunks, places)), dma((2, chunks, places)), dma((2, chunks, places)),
            dma((2, chunks, places, near)), dma((2, chunks)), dma((chunks, near)),
            dma((chunks, near)), dma((chunks,)), dma((chunks,)),
        ],
        compiler_params=pltpu.CompilerParams(
            collective_id=0, has_side_effects=True, vmem_limit_bytes=46 * 1024 * 1024
        ),
    )(tokens, upstream, ids, gates, w_gate, w_up, w_down)


def closing(
    groups, cap, top, grad_g, grad_u, grad_d, home, home_far, home_s, slots,
    out_x, out_gates, out_g, out_u, out_d, sems,
):
    copies = []
    for i, (src, dst) in enumerate(((grad_g, out_g), (grad_u, out_u), (grad_d, out_d))):
        copy = pltpu.make_async_copy(src, dst, sems.at[i])
        copy.start()
        copies.append(copy)
    chunks, near, _, wide_part = home.shape
    rows, half = groups * cap, near * cap
    per = LANES // cap
    picks = [one_hot(slots[i:i + 1, :], 0, rows) for i in range(top)]
    pick = picks[0][0:half]
    for p in picks[1:]:
        pick = pick + p[0:half]
    pick = pick.astype(jnp.bfloat16)
    for c in range(chunks):
        value = contract_first(pick, home[c].reshape(half, wide_part))
        value = value + home_far[c].astype(jnp.float32)
        out_x[:, c * wide_part:(c + 1) * wide_part] = value.astype(jnp.bfloat16)
    terms = jnp.concatenate(
        [merged([home_s[q * per + i] for i in range(per)], cap) for q in range(rows // LANES)],
        axis=1,
    )
    for i, p in enumerate(picks):
        value = jnp.dot(terms, p, precision=lax.Precision.HIGHEST,
                        preferred_element_type=jnp.float32)
        out_gates[i:i + 1, :] = value[0:1, :]
    for copy in copies:
        copy.wait()


def close(grads, home, home_far, home_s, slots, groups, cap, top):
    vmem = pl.BlockSpec(memory_space=pltpu.VMEM)
    hbm = pl.BlockSpec(memory_space=pl.ANY)
    chunks, toks, wide_part = home_far.shape
    operands = [
        pltpu.with_memory_space_constraint(v, pltpu.VMEM)
        for v in (*grads, home, home_far, home_s, slots)
    ]
    return pl.pallas_call(
        functools.partial(closing, groups, cap, top),
        out_shape=(
            jax.ShapeDtypeStruct((toks, chunks * wide_part), jnp.bfloat16),
            jax.ShapeDtypeStruct((top, toks), jnp.float32),
            *[jax.ShapeDtypeStruct(g.shape, g.dtype) for g in grads],
        ),
        in_specs=[vmem] * 7,
        out_specs=(vmem, vmem, hbm, hbm, hbm),
        scratch_shapes=[pltpu.SemaphoreType.DMA((3,))],
        compiler_params=pltpu.CompilerParams(vmem_limit_bytes=8 * 1024 * 1024),
    )(*operands)


def per_device(tokens, upstream, gates, expert_ids, w_gate, w_up, w_down):
    groups = lax.axis_size("dp")
    parts = lax.axis_size("expert")
    experts = groups * w_gate.shape[0]
    toks = tokens.shape[0]
    top = expert_ids.shape[1]
    cap = 2 * toks * top // experts
    *grads, home, home_far, home_s, slots = exchange(
        tokens, upstream, expert_ids.T, gates.T, w_gate[0], w_up[0], w_down[0], groups, parts, cap
    )
    grad_x, grad_gates, *grads = close(grads, home, home_far, home_s, slots, groups, cap, top)
    return (grad_x, grad_gates.T, *[g[None] for g in grads])


def solution(mesh):
    in_specs = (
        P("dp", None),
        P("dp", "expert"),
        P("dp", None),
        P("dp", None),
        P("dp", "expert", None),
        P("dp", "expert", None),
        P("dp", "expert", None),
    )
    out_specs = (
        P("dp", "expert"),
        P("dp", None),
        P("dp", "expert", None),
        P("dp", "expert", None),
        P("dp", "expert", None),
    )
    return jax.shard_map(
        per_device, mesh=mesh, in_specs=in_specs, out_specs=out_specs, check_vma=False
    )
```

```python
import functools

import jax
import jax.numpy as jnp
from jax import lax
from jax.experimental import pallas as pl
from jax.experimental.pallas import tpu as pltpu
from jax.sharding import PartitionSpec as P

MESH = pl.DeviceIdType.MESH
LANES = 128


def contract_last(left, right):
    return lax.dot_general(
        left, right, (((1,), (1,)), ((), ())), preferred_element_type=jnp.float32
    )


def contract_first(left, right):
    return lax.dot_general(
        left, right, (((0,), (0,)), ((), ())), preferred_element_type=jnp.float32
    )


def matmul(left, right):
    return jnp.dot(left, right, preferred_element_type=jnp.float32)


def one_hot(slot_row, low, count):
    index = lax.broadcasted_iota(jnp.int32, (count, slot_row.shape[1]), 0) + low
    return jnp.where(index == slot_row, 1.0, 0.0)


def merged(chunks, cap):
    lane = lax.broadcasted_iota(jnp.int32, chunks[0].shape, 1)
    row = chunks[0]
    for i in range(1, len(chunks)):
        row = jnp.where(lane < i * cap, row, chunks[i])
    return row


def kernel(
    groups, parts, cap,
    tokens_hbm, upstream_hbm, ids, gates, w_g_hbm, w_u_hbm, w_d_hbm,
    out_g, out_u, out_d, home, home_far, home_s, slots,
    tok, up, far_t, far_u, far_slots, far_pick, sel_t, sel_u, sel_far, recv_t, recv_u, send_s, recv_s,
    w_gu, w_down, pre_gu, pre_down, flip_gu, flip_down, straight, term, term_recv, total_s,
    pair_send, pair_recv, own_sum, side_send, side_recv, ret_send, mid_home, comb,
    w_sem, in_sem, raw_send, raw_recv, slot_send, slot_recv, scale_send, scale_recv,
    near_send, wide_fwd, dp_send, pair_fwd, side_fwd, pass_fwd, recv_sem,
    term_send, term_sem, back_send, back_recv,
    pair_send_sem, pair_recv_sem, side_send_sem, side_recv_sem, ret_sem, home_recv, mid_recv,
    comb_send, comb_recv,
):
    me, own = lax.axis_index("dp"), lax.axis_index("expert")
    core, place = lax.rem(own, 2), lax.div(own, 2)
    places = parts // 2
    partner = place * 2 + (1 - core)
    toks, part = up.shape
    near = groups // 2
    half = near * cap
    rows = groups * cap
    hid = w_down.shape[1]
    per = LANES // cap
    chunks, wide_part = comb.shape[0], comb.shape[2]
    order = list(range(near - 1, -1, -1))
    recvs = (recv_t, recv_u)
    bf, f32 = jnp.bfloat16, jnp.float32

    def crossed(k):
        spot = me
        for bit in [1 << b for b in range(groups.bit_length()) if k >> b & 1]:
            spot = spot + bit * (1 - 2 * lax.rem(lax.div(me, bit), 2))
        return spot

    there = [crossed(k) for k in range(groups)]
    mirror = there[near]

    def aside(j):
        return lax.rem(place + j, places)

    def arrived(ref, sem):
        pltpu.make_async_copy(ref, ref, sem).wait()

    load_up = pltpu.make_async_copy(upstream_hbm, up, in_sem.at[parts])
    load_up.start()
    load_tok = []
    for j in range(parts):
        load = pltpu.make_async_copy(
            tokens_hbm.at[:, pl.ds(j * part, part)], tok.at[j], in_sem.at[j]
        )
        load.start()
        load_tok.append(load)
    barrier = pltpu.get_barrier_semaphore()
    for k in range(1, groups):
        pl.semaphore_signal(barrier, inc=1, device_id={"dp": there[k]}, device_id_type=MESH)
    for j in range(1, parts):
        pl.semaphore_signal(
            barrier, inc=1, device_id={"expert": lax.rem(own + j, parts)}, device_id_type=MESH
        )

    rel = [jnp.bitwise_xor(ids[i:i + 1, :], me) for i in range(ids.shape[0])]
    padded = max(groups, 16)
    expert_of = lax.broadcasted_iota(jnp.int32, (padded, toks), 0)
    named = jnp.where(expert_of == rel[0], 1.0, 0.0)
    for other in rel[1:]:
        named = named + jnp.where(expert_of == other, 1.0, 0.0)
    earlier = lax.broadcasted_iota(jnp.int32, (toks, toks), 0)
    earlier = jnp.where(earlier < lax.broadcasted_iota(jnp.int32, (toks, toks), 1), 1.0, 0.0)
    before = matmul(named.astype(bf), earlier.astype(bf))
    slots[...] = jnp.full(slots.shape, -1, jnp.int32)
    for i, r in enumerate(rel):
        position = jnp.sum(jnp.where(expert_of == r, before, 0.0), axis=0, keepdims=True)
        slots[i:i + 1, :] = r * cap + position.astype(jnp.int32)

    def remote(src, dst, send_sem, sem, target):
        pltpu.make_async_remote_copy(
            src_ref=src, dst_ref=dst, send_sem=send_sem, recv_sem=sem,
            device_id=target, device_id_type=MESH,
        ).start()

    load_up.wait()
    for load in load_tok:
        load.wait()
    pl.semaphore_wait(barrier, groups + parts - 2)
    remote(tok.at[own], far_t, raw_send.at[0], raw_recv.at[0], {"dp": mirror})
    remote(slots, far_slots, slot_send, slot_recv, {"dp": mirror})
    loads = {}
    for t in (1, 0):
        for j in range(parts):
            columns = pl.ds(j * part, part)
            if t:
                pairs = [(w_d_hbm.at[:, columns], w_down.at[j], 2)]
            else:
                pairs = [(w_g_hbm.at[:, columns], w_gu.at[j, pl.ds(0, hid)], 0),
                         (w_u_hbm.at[:, columns], w_gu.at[j, pl.ds(hid, hid)], 1)]
            loads[t, j] = [pltpu.make_async_copy(src, dst, w_sem.at[m, j]) for src, dst, m in pairs]
            for load in loads[t, j]:
                load.start()

    picks = [one_hot(slots[i:i + 1, :], 0, rows) for i in range(len(rel))]
    pick = sum(picks[1:], picks[0]).astype(bf)

    def relay(t, k):
        spot = recvs[t].at[own, k]
        n = t * 2 + (k // near)
        if k % near:
            arrived(spot, recv_sem.at[t, own, k])
        for j in range(1, places):
            remote(spot, spot, side_fwd.at[n, j], recv_sem.at[t, own, k],
                   {"expert": aside(j) * 2 + core})
        remote(spot, spot, pair_fwd.at[n], recv_sem.at[t, own, k], {"expert": partner})

    def pass_on(t, k):
        n = t * 2 + (k // near)
        for j in range(1, places):
            part_of = aside(j) * 2 + core
            spot = recvs[t].at[part_of, k]
            arrived(spot, recv_sem.at[t, part_of, k])
            remote(spot, spot, pass_fwd.at[n, j], recv_sem.at[t, part_of, k], {"expert": partner})

    def wide(k):
        for j in range(places):
            part_of = j * 2 + core
            spot = recv_t.at[part_of, k]
            arrived(spot, recv_sem.at[0, part_of, k])
            remote(spot, spot, wide_fwd.at[j], recv_sem.at[0, part_of, k], {"expert": partner})

    def finish(h, t):
        for k in range(h * near, (h + 1) * near):
            if (h, t) == (0, 0):
                if k:
                    for j in range(places):
                        part_of = j * 2 + 1 - core
                        arrived(recv_t.at[part_of, k], recv_sem.at[0, part_of, k])
            else:
                for j in range(places):
                    part_of = aside(j) * 2 + 1 - core
                    arrived(recvs[t].at[part_of, k], recv_sem.at[t, part_of, k])

    chosen = matmul(pick[0:half], up[...]).astype(bf).reshape(near, cap, part)
    recv_u[own, 0] = chosen[0]
    relay(1, 0)
    for k in range(1, near):
        sel_u[k] = chosen[k]
        remote(sel_u.at[k], recv_u.at[own, k], dp_send.at[0], recv_sem.at[1, own, k],
               {"dp": there[k]})
    remote(up, far_u, raw_send.at[1], raw_recv.at[1], {"dp": mirror})
    for j in range(places):
        chosen = matmul(pick[0:half], tok[j * 2 + core]).astype(bf).reshape(near, cap, part)
        recv_t[j * 2 + core, 0] = chosen[0]
        for k in range(1, near):
            sel_t[j, k] = chosen[k]

    def send_wide(k):
        for j in range(places):
            spot = j * 2 + core
            remote(sel_t.at[j, k], recv_t.at[spot, k], near_send.at[j], recv_sem.at[0, spot, k],
                   {"dp": there[k]})

    scale_rows = None
    for i, p in enumerate(picks):
        gate = jnp.broadcast_to(gates[i:i + 1, :], (16, toks))
        value = contract_last(gate, p.astype(bf))
        scale_rows = value if i == 0 else scale_rows + value
    for q in range(rows // LANES):
        send_s[q] = scale_rows[0:8, q * LANES:(q + 1) * LANES]
    recv_s[0] = send_s[0]
    for k in range(1, groups):
        remote(send_s.at[k // per], recv_s.at[k], scale_send, scale_recv.at[k], {"dp": there[k]})
    for j in range(places):
        recv_t[j * 2 + 1 - core, 0] = matmul(pick[0:cap], tok[j * 2 + 1 - core]).astype(bf)

    def expand(t):
        if t == 0:
            arrived(far_slots, slot_recv)
            value = one_hot(far_slots[0:1, :], half, half)
            for i in range(1, ids.shape[0]):
                value = value + one_hot(far_slots[i:i + 1, :], half, half)
            far_pick[...] = value.astype(bf)
        source = (far_t, far_u)[t]
        arrived(source, raw_recv.at[t])
        value = matmul(far_pick[...], source[...]).astype(bf).reshape(near, cap, part)
        recvs[t][own, near] = value[0]
        for k in range(1, near):
            sel_far[t, k] = value[k]
            remote(sel_far.at[t, k], recvs[t].at[own, near + k], dp_send.at[1 + t],
                   recv_sem.at[t, own, near + k], {"dp": there[k]})
        relay(t, near)

    def forward_unit(h, t, j):
        if h == 1 - t:
            for load in loads[t, j]:
                load.wait()
        block = recvs[t][j, h * near:(h + 1) * near].reshape(half, part)
        pre = (pre_gu, pre_down)[t]
        value = contract_last((w_gu, w_down)[t][j], block)
        if j == 0:
            pre[h] = value
        else:
            pre[h] = pre[h] + value

    tile = 32

    def activate(h):
        for k in range(max(1, h * near), (h + 1) * near):
            arrived(recv_s.at[k], scale_recv.at[k])
        scale = jnp.concatenate(
            [merged([recv_s[q * per + i] for i in range(per)], cap)
             for q in range(h * half // LANES, (h + 1) * half // LANES)], axis=1
        )[0:1, :]
        term[h] = jnp.zeros((8, half), f32)

        @pl.loop(0, hid // tile)
        def _(step):
            low = pl.multiple_of(step * tile, tile)
            at = pl.ds(low, tile)
            above = pl.ds(pl.multiple_of(low + hid, tile), tile)
            columns = pl.ds(h * half, half)
            gate, lift, back = pre_gu[h, at, :], pre_gu[h, above, :], pre_down[h, at, :]
            sigma = jax.nn.sigmoid(gate)
            swish = gate * sigma
            slope = sigma * (1.0 + gate * (1.0 - sigma))
            act = (swish * lift).astype(bf).astype(f32)
            term[h] += jnp.broadcast_to(jnp.sum(act * back, axis=0, keepdims=True), (8, half))
            weighted = scale * back
            flip_gu[at, columns] = (weighted * lift * slope).astype(bf)
            flip_gu[above, columns] = (weighted * swish).astype(bf)
            flip_down[at, columns] = (scale * act).astype(bf)

        for j in range(1, parts):
            remote(term.at[h], term_recv.at[h, own], term_send.at[h], term_sem.at[h, own],
                   {"expert": lax.rem(own + j, parts)})
        block = flip_gu[:, h * half:(h + 1) * half].astype(f32)
        straight[h] = jnp.transpose(block).astype(bf)

    def piece(h, c, which):
        columns = pl.ds(c * wide_part, wide_part)
        value = matmul(straight[h], w_gu[which, :, columns])
        return value.reshape(near, cap, wide_part)

    def pair_step(h, c, j):
        spot = aside(j) * 2
        pair_send[h, c, j] = piece(h, c, spot + 1 - core).astype(bf)
        remote(pair_send.at[h, c, j], pair_recv.at[h, c, j], pair_send_sem.at[h, c, j],
               pair_recv_sem.at[h, c, j], {"expert": partner})
        own_sum[h, c, j] = piece(h, c, spot + core)

    def side_step(h, c, j):
        arrived(pair_recv.at[h, c, j], pair_recv_sem.at[h, c, j])
        for k in order:
            both = own_sum[h, c, j, k] + pair_recv[h, c, j, k].astype(f32)
            side_send[h, c, j, k] = both.astype(bf)
            remote(side_send.at[h, c, j, k], side_recv.at[h, c, j, k], side_send_sem.at[h, c, j],
                   side_recv_sem.at[h, c, j, k], {"expert": aside(j) * 2 + core})

    def return_step(h, c, k):
        if k == order[0]:
            arrived(pair_recv.at[h, c, 0], pair_recv_sem.at[h, c, 0])
        value = own_sum[h, c, 0, k] + pair_recv[h, c, 0, k].astype(f32)
        for j in range(1, places):
            arrived(side_recv.at[h, c, j, k], side_recv_sem.at[h, c, j, k])
            value = value + side_recv[h, c, j, k].astype(f32)
        goal, sem = ((home, home_recv), (mid_home, mid_recv))[h]
        if k == 0:
            goal[c, 0] = value.astype(bf)
        else:
            ret_send[h, c, k] = value.astype(bf)
            remote(ret_send.at[h, c, k], goal.at[c, k], ret_sem.at[h, c], sem.at[c, k],
                   {"dp": there[k]})

    def combine(c):
        for k in range(1, near):
            arrived(mid_home.at[c, k], mid_recv.at[c, k])
        value = contract_first(far_pick[...], mid_home[c].reshape(half, wide_part))
        comb[c] = value.astype(bf)
        remote(comb.at[c], home_far.at[c], comb_send.at[c], comb_recv.at[c], {"dp": mirror})

    def term_step(h):
        for j in range(1, parts):
            other = lax.rem(own + j, parts)
            arrived(term_recv.at[h, other], term_sem.at[h, other])
        term_recv[h, own] = term[h]
        total = term_recv[h, 0]
        for j in range(1, parts):
            total = total + term_recv[h, j]
        for q in range(half // LANES):
            total_s[h * half // LANES + q] = total[:, q * LANES:(q + 1) * LANES]
        for k in range(h * near, (h + 1) * near):
            if k == 0:
                home_s[0] = total_s[0]
            else:
                remote(total_s.at[k // per], home_s.at[k], back_send, back_recv.at[k],
                       {"dp": there[k]})

    def grad_unit(m, j):
        block = recvs[m // 2][j].reshape(rows, part)
        left = flip_down[...] if m == 2 else flip_gu[m * hid:(m + 1) * hid, :]
        (out_g, out_u, out_d)[m][:, j * part:(j + 1) * part] = matmul(left, block).astype(bf)

    grads = [(m, j) for m in range(3) for j in range(parts)]

    def some_grads(count):
        for _ in range(count):
            if grads:
                grad_unit(*grads.pop(0))

    def near_up():
        finish(0, 1)
        for j in range(parts):
            forward_unit(0, 1, j)

    later = range(2, near)
    far_later = [near + k for k in later]
    outer_steps = (
        [(relay, 1, 1), (pass_on, 1, 0)] + [(relay, 1, k) for k in later]
        + [(expand, 0), (pass_on, 1, 1), (relay, 0, near + 1)]
        + [(pass_on, 1, k) for k in later] + [(relay, 0, k) for k in far_later]
        + [(pass_on, 0, near), (expand, 1), (pass_on, 0, near + 1)]
        + [(send_wide, k) for k in later] + [(relay, 1, k) for k in far_later[:1]]
        + [(relay, 1, near + 1)] + [(relay, 1, k) for k in far_later[1:]]
        + [(send_wide, 1)] + [(pass_on, 0, k) for k in far_later] + [(near_up,)]
    )
    inner_steps = (
        [(relay, 1, 1), (pass_on, 1, 0), (expand, 0), (pass_on, 1, 1)]
        + [(relay, 1, k) for k in later] + [(relay, 0, near + 1), (pass_on, 0, near)]
        + [(pass_on, 1, k) for k in later]
        + [(expand, 1), (pass_on, 0, near + 1)] + [(relay, 0, k) for k in far_later]
        + [(relay, 1, near + 1)] + [(send_wide, k) for k in later]
        + [(relay, 1, k) for k in far_later] + [(send_wide, 1), (near_up,)] + [(pass_on, 0, k) for k in far_later]
    )
    inner = lax.rem(lax.div(me, near) + lax.div(me, max(1, near // 2)), 2) == 1

    def run(steps):
        for step, *at in steps:
            step(*at)

    pl.when(inner)(functools.partial(run, inner_steps))
    pl.when(jnp.logical_not(inner))(functools.partial(run, outer_steps))
    finish(1, 0)
    for j in range(parts):
        if j < near:
            pass_on(1, near + j)
        forward_unit(1, 0, j)
    for k in range(near + parts, groups):
        pass_on(1, k)
    finish(1, 1)
    for j in range(parts):
        forward_unit(1, 1, j)
    activate(1)
    aside_first = list(range(1, places)) + [0]
    for c in range(chunks):
        for j in aside_first[:-1]:
            pair_step(1, c, j)
            side_step(1, c, j)
    for k in range(1, near):
        wide(k)
    for c in range(chunks):
        pair_step(1, c, 0)
    finish(0, 0)
    for j in range(parts):
        if j == parts // 2:
            for k in order:
                return_step(1, 0, k)
        forward_unit(0, 0, j)
    activate(0)
    for c in range(chunks):
        for j in aside_first[:-1]:
            pair_step(0, c, j)
            side_step(0, c, j)
        if c + 1 < chunks:
            combine(c)
            for k in order:
                return_step(1, c + 1, k)
    for c in range(chunks):
        pair_step(0, c, 0)
    term_step(1)
    term_step(0)
    some_grads(1)
    for k in order:
        return_step(0, 0, k)
    combine(chunks - 1)
    some_grads(1)
    for c in range(1, chunks):
        for k in order:
            some_grads(1)
            return_step(0, c, k)
    some_grads(len(grads))

    for c in range(chunks):
        for k in range(1, near):
            arrived(home.at[c, k], home_recv.at[c, k])
        arrived(home_far.at[c], comb_recv.at[c])
    for k in range(1, groups):
        arrived(home_s.at[k], back_recv.at[k])

    few, all_near = recv_t.at[0, pl.ds(0, near - 1)], recv_t.at[0, pl.ds(0, near)]
    for t in range(2):
        arrived((far_t, far_u)[t], raw_send.at[t])
    arrived(far_slots, slot_send)
    arrived(recv_s.at[pl.ds(0, groups - 1)], scale_send)
    for j in range(places):
        arrived(few, near_send.at[j])
        arrived(few, wide_fwd.at[j])
    for i in range(3):
        arrived(few, dp_send.at[i])
    for n in range(1, 4):
        arrived(all_near, pair_fwd.at[n])
        for j in range(1, places):
            arrived(all_near, side_fwd.at[n, j])
            arrived(all_near, pass_fwd.at[n, j])
    for h in range(2):
        arrived(term_recv.at[h, pl.ds(0, parts - 1)], term_send.at[h])
        for c in range(chunks):
            arrived(ret_send.at[h, c, pl.ds(0, near - 1)], ret_sem.at[h, c])
            for j in range(places):
                arrived(pair_send.at[h, c, j], pair_send_sem.at[h, c, j])
                if j:
                    arrived(side_send.at[h, c, j], side_send_sem.at[h, c, j])
    arrived(home_s.at[pl.ds(0, groups - 1)], back_send)
    for c in range(chunks):
        arrived(comb.at[c], comb_send.at[c])


def exchange(tokens, upstream, ids, gates, w_gate, w_up, w_down, groups, parts, cap):
    toks, part = upstream.shape
    rows = groups * cap
    near = groups // 2
    half = near * cap
    hid, width = w_gate.shape
    places = parts // 2
    chunks = 2
    wide_part = part // chunks
    bf, f32 = jnp.bfloat16, jnp.float32
    dma = pltpu.SemaphoreType.DMA
    vmem = pl.BlockSpec(memory_space=pltpu.VMEM)
    hbm = pl.BlockSpec(memory_space=pl.ANY)
    return pl.pallas_call(
        functools.partial(kernel, groups, parts, cap),
        out_shape=(
            pltpu.VMEM((hid, width), bf), pltpu.VMEM((hid, width), bf), pltpu.VMEM((hid, width), bf),
            pltpu.VMEM((chunks, near, cap, wide_part), bf), pltpu.VMEM((chunks, toks, wide_part), bf),
            pltpu.VMEM((groups, 8, LANES), f32), pltpu.VMEM((8, toks), jnp.int32),
        ),
        in_specs=[hbm, hbm, vmem, vmem, hbm, hbm, hbm],
        out_specs=(vmem,) * 7,
        scratch_shapes=[
            pltpu.VMEM((parts, toks, part), bf),
            pltpu.VMEM((toks, part), bf),
            pltpu.VMEM((toks, part), bf),
            pltpu.VMEM((toks, part), bf),
            pltpu.VMEM((8, toks), jnp.int32),
            pltpu.VMEM((half, toks), bf),
            pltpu.VMEM((places, near, cap, part), bf),
            pltpu.VMEM((near, cap, part), bf),
            pltpu.VMEM((2, near, cap, part), bf),
            pltpu.VMEM((parts, groups, cap, part), bf),
            pltpu.VMEM((parts, groups, cap, part), bf),
            pltpu.VMEM((rows // LANES, 8, LANES), f32),
            pltpu.VMEM((groups, 8, LANES), f32),
            pltpu.VMEM((parts, 2 * hid, part), bf),
            pltpu.VMEM((parts, hid, part), bf),
            pltpu.VMEM((2, 2 * hid, half), f32),
            pltpu.VMEM((2, hid, half), f32),
            pltpu.VMEM((2 * hid, rows), bf),
            pltpu.VMEM((hid, rows), bf),
            pltpu.VMEM((2, half, 2 * hid), bf),
            pltpu.VMEM((2, 8, half), f32),
            pltpu.VMEM((2, parts, 8, half), f32),
            pltpu.VMEM((rows // LANES, 8, LANES), f32),
            pltpu.VMEM((2, chunks, places, near, cap, wide_part), bf),
            pltpu.VMEM((2, chunks, places, near, cap, wide_part), bf),
            pltpu.VMEM((2, chunks, places, near, cap, wide_part), f32),
            pltpu.VMEM((2, chunks, places, near, cap, wide_part), bf),
            pltpu.VMEM((2, chunks, places, near, cap, wide_part), bf),
            pltpu.VMEM((2, chunks, near, cap, wide_part), bf),
            pltpu.VMEM((chunks, near, cap, wide_part), bf),
            pltpu.VMEM((chunks, toks, wide_part), bf),
            dma((3, parts)), dma((parts + 1,)), dma((2,)), dma((2,)), dma, dma, dma, dma((groups,)),
            dma((places,)), dma((places,)), dma((3,)), dma((4,)), dma((4, places)),
            dma((4, places)), dma((2, parts, groups)),
            dma((2,)), dma((2, parts)), dma, dma((groups,)),
            dma((2, chunks, places)), dma((2, chunks, places)), dma((2, chunks, places)),
            dma((2, chunks, places, near)), dma((2, chunks)), dma((chunks, near)),
            dma((chunks, near)), dma((chunks,)), dma((chunks,)),
        ],
        compiler_params=pltpu.CompilerParams(
            collective_id=0, has_side_effects=True, vmem_limit_bytes=46 * 1024 * 1024
        ),
    )(tokens, upstream, ids, gates, w_gate, w_up, w_down)


def closing(
    groups, cap, top, grad_g, grad_u, grad_d, home, home_far, home_s, slots,
    out_x, out_gates, out_g, out_u, out_d, sems,
):
    copies = []
    for i, (src, dst) in enumerate(((grad_g, out_g), (grad_u, out_u), (grad_d, out_d))):
        copy = pltpu.make_async_copy(src, dst, sems.at[i])
        copy.start()
        copies.append(copy)
    chunks, near, _, wide_part = home.shape
    rows, half = groups * cap, near * cap
    per = LANES // cap
    picks = [one_hot(slots[i:i + 1, :], 0, rows) for i in range(top)]
    pick = picks[0][0:half]
    for p in picks[1:]:
        pick = pick + p[0:half]
    pick = pick.astype(jnp.bfloat16)
    for c in range(chunks):
        value = contract_first(pick, home[c].reshape(half, wide_part))
        value = value + home_far[c].astype(jnp.float32)
        out_x[:, c * wide_part:(c + 1) * wide_part] = value.astype(jnp.bfloat16)
    terms = jnp.concatenate(
        [merged([home_s[q * per + i] for i in range(per)], cap) for q in range(rows // LANES)],
        axis=1,
    )
    for i, p in enumerate(picks):
        value = jnp.dot(terms, p, precision=lax.Precision.HIGHEST,
                        preferred_element_type=jnp.float32)
        out_gates[i:i + 1, :] = value[0:1, :]
    for copy in copies:
        copy.wait()


def close(grads, home, home_far, home_s, slots, groups, cap, top):
    vmem = pl.BlockSpec(memory_space=pltpu.VMEM)
    hbm = pl.BlockSpec(memory_space=pl.ANY)
    chunks, toks, wide_part = home_far.shape
    operands = [
        pltpu.with_memory_space_constraint(v, pltpu.VMEM)
        for v in (*grads, home, home_far, home_s, slots)
    ]
    return pl.pallas_call(
        functools.partial(closing, groups, cap, top),
        out_shape=(
            jax.ShapeDtypeStruct((toks, chunks * wide_part), jnp.bfloat16),
            jax.ShapeDtypeStruct((top, toks), jnp.float32),
            *[jax.ShapeDtypeStruct(g.shape, g.dtype) for g in grads],
        ),
        in_specs=[vmem] * 7,
        out_specs=(vmem, vmem, hbm, hbm, hbm),
        scratch_shapes=[pltpu.SemaphoreType.DMA((3,))],
        compiler_params=pltpu.CompilerParams(vmem_limit_bytes=8 * 1024 * 1024),
    )(*operands)


def per_device(tokens, upstream, gates, expert_ids, w_gate, w_up, w_down):
    groups = lax.axis_size("dp")
    parts = lax.axis_size("expert")
    experts = groups * w_gate.shape[0]
    toks = tokens.shape[0]
    top = expert_ids.shape[1]
    cap = 2 * toks * top // experts
    *grads, home, home_far, home_s, slots = exchange(
        tokens, upstream, expert_ids.T, gates.T, w_gate[0], w_up[0], w_down[0], groups, parts, cap
    )
    grad_x, grad_gates, *grads = close(grads, home, home_far, home_s, slots, groups, cap, top)
    return (grad_x, grad_gates.T, *[g[None] for g in grads])


def solution(mesh):
    in_specs = (
        P("dp", None),
        P("dp", "expert"),
        P("dp", None),
        P("dp", None),
        P("dp", "expert", None),
        P("dp", "expert", None),
        P("dp", "expert", None),
    )
    out_specs = (
        P("dp", "expert"),
        P("dp", None),
        P("dp", "expert", None),
        P("dp", "expert", None),
        P("dp", "expert", None),
    )
    return jax.shard_map(
        per_device, mesh=mesh, in_specs=in_specs, out_specs=out_specs, check_vma=False
    )
```

```python
import functools

import jax
import jax.numpy as jnp
from jax import lax
from jax.experimental import pallas as pl
from jax.experimental.pallas import tpu as pltpu
from jax.sharding import PartitionSpec as P

MESH = pl.DeviceIdType.MESH
LANES = 128


def contract_last(left, right):
    return lax.dot_general(
        left, right, (((1,), (1,)), ((), ())), preferred_element_type=jnp.float32
    )


def contract_first(left, right):
    return lax.dot_general(
        left, right, (((0,), (0,)), ((), ())), preferred_element_type=jnp.float32
    )


def matmul(left, right):
    return jnp.dot(left, right, preferred_element_type=jnp.float32)


def one_hot(slot_row, low, count):
    index = lax.broadcasted_iota(jnp.int32, (count, slot_row.shape[1]), 0) + low
    return jnp.where(index == slot_row, 1.0, 0.0)


def merged(chunks, cap):
    lane = lax.broadcasted_iota(jnp.int32, chunks[0].shape, 1)
    row = chunks[0]
    for i in range(1, len(chunks)):
        row = jnp.where(lane < i * cap, row, chunks[i])
    return row


def kernel(
    groups, parts, cap,
    tokens_hbm, upstream_hbm, ids, gates, w_g_hbm, w_u_hbm, w_d_hbm,
    out_g, out_u, out_d, home, home_far, home_s, slots,
    tok, up, far_t, far_u, far_slots, far_pick, sel_t, sel_u, sel_far, recv_t, recv_u, send_s, recv_s,
    w_gu, w_down, pre_gu, pre_down, flip_gu, flip_down, straight, term, term_recv, total_s,
    pair_send, pair_recv, own_sum, side_send, side_recv, ret_send, mid_home, comb,
    w_sem, in_sem, raw_send, raw_recv, slot_send, slot_recv, scale_send, scale_recv,
    near_send, wide_fwd, dp_send, pair_fwd, side_fwd, pass_fwd, recv_sem,
    term_send, term_sem, back_send, back_recv,
    pair_send_sem, pair_recv_sem, side_send_sem, side_recv_sem, ret_sem, home_recv, mid_recv,
    comb_send, comb_recv,
):
    me, own = lax.axis_index("dp"), lax.axis_index("expert")
    core, place = lax.rem(own, 2), lax.div(own, 2)
    places = parts // 2
    partner = place * 2 + (1 - core)
    toks, part = up.shape
    near = groups // 2
    half = near * cap
    rows = groups * cap
    hid = w_down.shape[1]
    per = LANES // cap
    chunks, wide_part = comb.shape[0], comb.shape[2]
    order = list(range(near - 1, -1, -1))
    recvs = (recv_t, recv_u)
    bf, f32 = jnp.bfloat16, jnp.float32

    def crossed(k):
        spot = me
        for bit in [1 << b for b in range(groups.bit_length()) if k >> b & 1]:
            spot = spot + bit * (1 - 2 * lax.rem(lax.div(me, bit), 2))
        return spot

    there = [crossed(k) for k in range(groups)]
    mirror = there[near]

    def aside(j):
        return lax.rem(place + j, places)

    def arrived(ref, sem):
        pltpu.make_async_copy(ref, ref, sem).wait()

    load_up = pltpu.make_async_copy(upstream_hbm, up, in_sem.at[parts])
    load_up.start()
    load_tok = []
    for j in range(parts):
        load = pltpu.make_async_copy(
            tokens_hbm.at[:, pl.ds(j * part, part)], tok.at[j], in_sem.at[j]
        )
        load.start()
        load_tok.append(load)
    barrier = pltpu.get_barrier_semaphore()
    for k in range(1, groups):
        pl.semaphore_signal(barrier, inc=1, device_id={"dp": there[k]}, device_id_type=MESH)
    for j in range(1, parts):
        pl.semaphore_signal(
            barrier, inc=1, device_id={"expert": lax.rem(own + j, parts)}, device_id_type=MESH
        )

    rel = [jnp.bitwise_xor(ids[i:i + 1, :], me) for i in range(ids.shape[0])]
    padded = max(groups, 16)
    expert_of = lax.broadcasted_iota(jnp.int32, (padded, toks), 0)
    named = jnp.where(expert_of == rel[0], 1.0, 0.0)
    for other in rel[1:]:
        named = named + jnp.where(expert_of == other, 1.0, 0.0)
    earlier = lax.broadcasted_iota(jnp.int32, (toks, toks), 0)
    earlier = jnp.where(earlier < lax.broadcasted_iota(jnp.int32, (toks, toks), 1), 1.0, 0.0)
    before = matmul(named.astype(bf), earlier.astype(bf))
    slots[...] = jnp.full(slots.shape, -1, jnp.int32)
    for i, r in enumerate(rel):
        position = jnp.sum(jnp.where(expert_of == r, before, 0.0), axis=0, keepdims=True)
        slots[i:i + 1, :] = r * cap + position.astype(jnp.int32)

    def remote(src, dst, send_sem, sem, target):
        pltpu.make_async_remote_copy(
            src_ref=src, dst_ref=dst, send_sem=send_sem, recv_sem=sem,
            device_id=target, device_id_type=MESH,
        ).start()

    load_up.wait()
    for load in load_tok:
        load.wait()
    pl.semaphore_wait(barrier, groups + parts - 2)
    remote(tok.at[own], far_t, raw_send.at[0], raw_recv.at[0], {"dp": mirror})
    remote(slots, far_slots, slot_send, slot_recv, {"dp": mirror})
    loads = {}
    for t in (1, 0):
        for j in range(parts):
            columns = pl.ds(j * part, part)
            if t:
                pairs = [(w_d_hbm.at[:, columns], w_down.at[j], 2)]
            else:
                pairs = [(w_g_hbm.at[:, columns], w_gu.at[j, pl.ds(0, hid)], 0),
                         (w_u_hbm.at[:, columns], w_gu.at[j, pl.ds(hid, hid)], 1)]
            loads[t, j] = [pltpu.make_async_copy(src, dst, w_sem.at[m, j]) for src, dst, m in pairs]
            for load in loads[t, j]:
                load.start()

    picks = [one_hot(slots[i:i + 1, :], 0, rows) for i in range(len(rel))]
    pick = sum(picks[1:], picks[0]).astype(bf)

    def relay(t, k):
        spot = recvs[t].at[own, k]
        n = t * 2 + (k // near)
        if k % near:
            arrived(spot, recv_sem.at[t, own, k])
        for j in range(1, places):
            remote(spot, spot, side_fwd.at[n, j], recv_sem.at[t, own, k],
                   {"expert": aside(j) * 2 + core})
        remote(spot, spot, pair_fwd.at[n], recv_sem.at[t, own, k], {"expert": partner})

    def pass_on(t, k):
        n = t * 2 + (k // near)
        for j in range(1, places):
            part_of = aside(j) * 2 + core
            spot = recvs[t].at[part_of, k]
            arrived(spot, recv_sem.at[t, part_of, k])
            remote(spot, spot, pass_fwd.at[n, j], recv_sem.at[t, part_of, k], {"expert": partner})

    def wide(k):
        for j in range(places):
            part_of = j * 2 + core
            spot = recv_t.at[part_of, k]
            arrived(spot, recv_sem.at[0, part_of, k])
            remote(spot, spot, wide_fwd.at[j], recv_sem.at[0, part_of, k], {"expert": partner})

    def finish(h, t):
        for k in range(h * near, (h + 1) * near):
            if (h, t) == (0, 0):
                if k:
                    for j in range(places):
                        part_of = j * 2 + 1 - core
                        arrived(recv_t.at[part_of, k], recv_sem.at[0, part_of, k])
            else:
                for j in range(places):
                    part_of = aside(j) * 2 + 1 - core
                    arrived(recvs[t].at[part_of, k], recv_sem.at[t, part_of, k])

    chosen = matmul(pick[0:half], up[...]).astype(bf).reshape(near, cap, part)
    recv_u[own, 0] = chosen[0]
    relay(1, 0)
    for k in range(1, near):
        sel_u[k] = chosen[k]
        remote(sel_u.at[k], recv_u.at[own, k], dp_send.at[0], recv_sem.at[1, own, k],
               {"dp": there[k]})
    for j in range(places):
        chosen = matmul(pick[0:half], tok[j * 2 + core]).astype(bf).reshape(near, cap, part)
        recv_t[j * 2 + core, 0] = chosen[0]
        for k in range(1, near):
            sel_t[j, k] = chosen[k]

    def send_wide(k):
        for j in range(places):
            spot = j * 2 + core
            remote(sel_t.at[j, k], recv_t.at[spot, k], near_send.at[j], recv_sem.at[0, spot, k],
                   {"dp": there[k]})

    scale_rows = None
    for i, p in enumerate(picks):
        gate = jnp.broadcast_to(gates[i:i + 1, :], (16, toks))
        value = contract_last(gate, p.astype(bf))
        scale_rows = value if i == 0 else scale_rows + value
    for q in range(rows // LANES):
        send_s[q] = scale_rows[0:8, q * LANES:(q + 1) * LANES]
    recv_s[0] = send_s[0]
    for k in range(1, groups):
        remote(send_s.at[k // per], recv_s.at[k], scale_send, scale_recv.at[k], {"dp": there[k]})
    for j in range(places):
        recv_t[j * 2 + 1 - core, 0] = matmul(pick[0:cap], tok[j * 2 + 1 - core]).astype(bf)

    def expand(t):
        if t == 0:
            arrived(far_slots, slot_recv)
            value = one_hot(far_slots[0:1, :], half, half)
            for i in range(1, ids.shape[0]):
                value = value + one_hot(far_slots[i:i + 1, :], half, half)
            far_pick[...] = value.astype(bf)
        source = (far_t, far_u)[t]
        arrived(source, raw_recv.at[t])
        value = matmul(far_pick[...], source[...]).astype(bf).reshape(near, cap, part)
        recvs[t][own, near] = value[0]
        for k in range(1, near):
            sel_far[t, k] = value[k]
            remote(sel_far.at[t, k], recvs[t].at[own, near + k], dp_send.at[1 + t],
                   recv_sem.at[t, own, near + k], {"dp": there[k]})
        relay(t, near)

    def forward_unit(h, t, j):
        if h == 1 - t:
            for load in loads[t, j]:
                load.wait()
        block = recvs[t][j, h * near:(h + 1) * near].reshape(half, part)
        pre = (pre_gu, pre_down)[t]
        value = contract_last((w_gu, w_down)[t][j], block)
        if j == 0:
            pre[h] = value
        else:
            pre[h] = pre[h] + value

    tile = 32

    def activate(h):
        for k in range(max(1, h * near), (h + 1) * near):
            arrived(recv_s.at[k], scale_recv.at[k])
        scale = jnp.concatenate(
            [merged([recv_s[q * per + i] for i in range(per)], cap)
             for q in range(h * half // LANES, (h + 1) * half // LANES)], axis=1
        )[0:1, :]
        term[h] = jnp.zeros((8, half), f32)

        @pl.loop(0, hid // tile)
        def _(step):
            low = pl.multiple_of(step * tile, tile)
            at = pl.ds(low, tile)
            above = pl.ds(pl.multiple_of(low + hid, tile), tile)
            columns = pl.ds(h * half, half)
            gate, lift, back = pre_gu[h, at, :], pre_gu[h, above, :], pre_down[h, at, :]
            sigma = jax.nn.sigmoid(gate)
            swish = gate * sigma
            slope = sigma * (1.0 + gate * (1.0 - sigma))
            act = (swish * lift).astype(bf).astype(f32)
            term[h] += jnp.broadcast_to(jnp.sum(act * back, axis=0, keepdims=True), (8, half))
            weighted = scale * back
            flip_gu[at, columns] = (weighted * lift * slope).astype(bf)
            flip_gu[above, columns] = (weighted * swish).astype(bf)
            flip_down[at, columns] = (scale * act).astype(bf)

        for j in range(1, parts):
            remote(term.at[h], term_recv.at[h, own], term_send.at[h], term_sem.at[h, own],
                   {"expert": lax.rem(own + j, parts)})
        block = flip_gu[:, h * half:(h + 1) * half].astype(f32)
        straight[h] = jnp.transpose(block).astype(bf)

    def piece(h, c, which):
        columns = pl.ds(c * wide_part, wide_part)
        value = matmul(straight[h], w_gu[which, :, columns])
        return value.reshape(near, cap, wide_part)

    def pair_step(h, c, j):
        spot = aside(j) * 2
        pair_send[h, c, j] = piece(h, c, spot + 1 - core).astype(bf)
        remote(pair_send.at[h, c, j], pair_recv.at[h, c, j], pair_send_sem.at[h, c, j],
               pair_recv_sem.at[h, c, j], {"expert": partner})
        own_sum[h, c, j] = piece(h, c, spot + core)

    def side_step(h, c, j):
        arrived(pair_recv.at[h, c, j], pair_recv_sem.at[h, c, j])
        for k in order:
            both = own_sum[h, c, j, k] + pair_recv[h, c, j, k].astype(f32)
            side_send[h, c, j, k] = both.astype(bf)
            remote(side_send.at[h, c, j, k], side_recv.at[h, c, j, k], side_send_sem.at[h, c, j],
                   side_recv_sem.at[h, c, j, k], {"expert": aside(j) * 2 + core})

    def return_step(h, c, k):
        if k == order[0]:
            arrived(pair_recv.at[h, c, 0], pair_recv_sem.at[h, c, 0])
        value = own_sum[h, c, 0, k] + pair_recv[h, c, 0, k].astype(f32)
        for j in range(1, places):
            arrived(side_recv.at[h, c, j, k], side_recv_sem.at[h, c, j, k])
            value = value + side_recv[h, c, j, k].astype(f32)
        goal, sem = ((home, home_recv), (mid_home, mid_recv))[h]
        if k == 0:
            goal[c, 0] = value.astype(bf)
        else:
            ret_send[h, c, k] = value.astype(bf)
            remote(ret_send.at[h, c, k], goal.at[c, k], ret_sem.at[h, c], sem.at[c, k],
                   {"dp": there[k]})

    def combine(c):
        for k in range(1, near):
            arrived(mid_home.at[c, k], mid_recv.at[c, k])
        value = contract_first(far_pick[...], mid_home[c].reshape(half, wide_part))
        comb[c] = value.astype(bf)
        remote(comb.at[c], home_far.at[c], comb_send.at[c], comb_recv.at[c], {"dp": mirror})

    def term_step(h):
        for j in range(1, parts):
            other = lax.rem(own + j, parts)
            arrived(term_recv.at[h, other], term_sem.at[h, other])
        term_recv[h, own] = term[h]
        total = term_recv[h, 0]
        for j in range(1, parts):
            total = total + term_recv[h, j]
        for q in range(half // LANES):
            total_s[h * half // LANES + q] = total[:, q * LANES:(q + 1) * LANES]
        for k in range(h * near, (h + 1) * near):
            if k == 0:
                home_s[0] = total_s[0]
            else:
                remote(total_s.at[k // per], home_s.at[k], back_send, back_recv.at[k],
                       {"dp": there[k]})

    def grad_unit(m, j):
        block = recvs[m // 2][j].reshape(rows, part)
        left = flip_down[...] if m == 2 else flip_gu[m * hid:(m + 1) * hid, :]
        (out_g, out_u, out_d)[m][:, j * part:(j + 1) * part] = matmul(left, block).astype(bf)

    grads = [(m, j) for m in range(3) for j in range(parts)]

    def some_grads(count):
        for _ in range(count):
            if grads:
                grad_unit(*grads.pop(0))

    def raw_up():
        remote(up, far_u, raw_send.at[1], raw_recv.at[1], {"dp": mirror})

    def near_up():
        finish(0, 1)
        for j in range(parts):
            forward_unit(0, 1, j)

    later = range(2, near)
    far_later = [near + k for k in later]
    outer_steps = (
        [(relay, 1, 1), (pass_on, 1, 0)] + [(relay, 1, k) for k in later]
        + [(pass_on, 1, 1)] + [(pass_on, 1, k) for k in later[:1]] + [(raw_up,), (expand, 0)]
        + [(relay, 0, near + 1)] + [(pass_on, 1, k) for k in later[1:]] + [(relay, 0, k) for k in far_later]
        + [(pass_on, 0, near), (expand, 1), (pass_on, 0, near + 1)]
        + [(send_wide, k) for k in later] + [(relay, 1, k) for k in far_later[:1]]
        + [(relay, 1, near + 1)] + [(relay, 1, k) for k in far_later[1:]]
        + [(send_wide, 1)] + [(pass_on, 0, k) for k in far_later] + [(near_up,)]
    )
    inner_steps = (
        [(raw_up,), (relay, 1, 1), (pass_on, 1, 0), (expand, 0), (pass_on, 1, 1)]
        + [(relay, 1, k) for k in later] + [(relay, 0, near + 1), (pass_on, 0, near)]
        + [(pass_on, 1, k) for k in later]
        + [(expand, 1), (pass_on, 0, near + 1)] + [(relay, 0, k) for k in far_later]
        + [(relay, 1, near + 1)] + [(send_wide, k) for k in later]
        + [(relay, 1, k) for k in far_later] + [(send_wide, 1)]
        + [(pass_on, 0, k) for k in far_later] + [(near_up,)]
    )
    inner = lax.rem(lax.div(me, near) + lax.div(me, max(1, near // 2)), 2) == 1

    def run(steps):
        for step, *at in steps:
            step(*at)

    pl.when(inner)(functools.partial(run, inner_steps))
    pl.when(jnp.logical_not(inner))(functools.partial(run, outer_steps))
    finish(1, 0)
    passes = [near] + far_later[:1] + [near + 1] + far_later[1:]
    for j in range(parts):
        if passes:
            pass_on(1, passes.pop(0))
        forward_unit(1, 0, j)
    for k in passes:
        pass_on(1, k)
    finish(1, 1)
    for j in range(parts):
        forward_unit(1, 1, j)
    activate(1)
    aside_first = list(range(1, places)) + [0]
    for c in range(chunks):
        for j in aside_first[:-1]:
            pair_step(1, c, j)
            side_step(1, c, j)
    for k in range(1, near):
        wide(k)
    for c in range(chunks):
        pair_step(1, c, 0)
    finish(0, 0)
    for j in range(parts):
        if j == parts // 2:
            for k in order:
                return_step(1, 0, k)
        forward_unit(0, 0, j)
    activate(0)
    for c in range(chunks):
        for j in aside_first[:-1]:
            pair_step(0, c, j)
            side_step(0, c, j)
        if c + 1 < chunks:
            combine(c)
            for k in order:
                return_step(1, c + 1, k)
    for c in range(chunks):
        pair_step(0, c, 0)
    term_step(1)
    term_step(0)
    some_grads(1)
    for k in order:
        some_grads(1)
        return_step(0, 0, k)
    combine(chunks - 1)
    for c in range(1, chunks):
        for k in order:
            some_grads(1)
            return_step(0, c, k)
    some_grads(len(grads))

    for c in range(chunks):
        for k in range(1, near):
            arrived(home.at[c, k], home_recv.at[c, k])
        arrived(home_far.at[c], comb_recv.at[c])
    for k in range(1, groups):
        arrived(home_s.at[k], back_recv.at[k])

    few, all_near = recv_t.at[0, pl.ds(0, near - 1)], recv_t.at[0, pl.ds(0, near)]
    for t in range(2):
        arrived((far_t, far_u)[t], raw_send.at[t])
    arrived(far_slots, slot_send)
    arrived(recv_s.at[pl.ds(0, groups - 1)], scale_send)
    for j in range(places):
        arrived(few, near_send.at[j])
        arrived(few, wide_fwd.at[j])
    for i in range(3):
        arrived(few, dp_send.at[i])
    for n in range(1, 4):
        arrived(all_near, pair_fwd.at[n])
        for j in range(1, places):
            arrived(all_near, side_fwd.at[n, j])
            arrived(all_near, pass_fwd.at[n, j])
    for h in range(2):
        arrived(term_recv.at[h, pl.ds(0, parts - 1)], term_send.at[h])
        for c in range(chunks):
            arrived(ret_send.at[h, c, pl.ds(0, near - 1)], ret_sem.at[h, c])
            for j in range(places):
                arrived(pair_send.at[h, c, j], pair_send_sem.at[h, c, j])
                if j:
                    arrived(side_send.at[h, c, j], side_send_sem.at[h, c, j])
    arrived(home_s.at[pl.ds(0, groups - 1)], back_send)
    for c in range(chunks):
        arrived(comb.at[c], comb_send.at[c])


def exchange(tokens, upstream, ids, gates, w_gate, w_up, w_down, groups, parts, cap):
    toks, part = upstream.shape
    rows = groups * cap
    near = groups // 2
    half = near * cap
    hid, width = w_gate.shape
    places = parts // 2
    chunks = 2
    wide_part = part // chunks
    bf, f32 = jnp.bfloat16, jnp.float32
    dma = pltpu.SemaphoreType.DMA
    vmem = pl.BlockSpec(memory_space=pltpu.VMEM)
    hbm = pl.BlockSpec(memory_space=pl.ANY)
    return pl.pallas_call(
        functools.partial(kernel, groups, parts, cap),
        out_shape=(
            pltpu.VMEM((hid, width), bf), pltpu.VMEM((hid, width), bf), pltpu.VMEM((hid, width), bf),
            pltpu.VMEM((chunks, near, cap, wide_part), bf), pltpu.VMEM((chunks, toks, wide_part), bf),
            pltpu.VMEM((groups, 8, LANES), f32), pltpu.VMEM((8, toks), jnp.int32),
        ),
        in_specs=[hbm, hbm, vmem, vmem, hbm, hbm, hbm],
        out_specs=(vmem,) * 7,
        scratch_shapes=[
            pltpu.VMEM((parts, toks, part), bf),
            pltpu.VMEM((toks, part), bf),
            pltpu.VMEM((toks, part), bf),
            pltpu.VMEM((toks, part), bf),
            pltpu.VMEM((8, toks), jnp.int32),
            pltpu.VMEM((half, toks), bf),
            pltpu.VMEM((places, near, cap, part), bf),
            pltpu.VMEM((near, cap, part), bf),
            pltpu.VMEM((2, near, cap, part), bf),
            pltpu.VMEM((parts, groups, cap, part), bf),
            pltpu.VMEM((parts, groups, cap, part), bf),
            pltpu.VMEM((rows // LANES, 8, LANES), f32),
            pltpu.VMEM((groups, 8, LANES), f32),
            pltpu.VMEM((parts, 2 * hid, part), bf),
            pltpu.VMEM((parts, hid, part), bf),
            pltpu.VMEM((2, 2 * hid, half), f32),
            pltpu.VMEM((2, hid, half), f32),
            pltpu.VMEM((2 * hid, rows), bf),
            pltpu.VMEM((hid, rows), bf),
            pltpu.VMEM((2, half, 2 * hid), bf),
            pltpu.VMEM((2, 8, half), f32),
            pltpu.VMEM((2, parts, 8, half), f32),
            pltpu.VMEM((rows // LANES, 8, LANES), f32),
            pltpu.VMEM((2, chunks, places, near, cap, wide_part), bf),
            pltpu.VMEM((2, chunks, places, near, cap, wide_part), bf),
            pltpu.VMEM((2, chunks, places, near, cap, wide_part), f32),
            pltpu.VMEM((2, chunks, places, near, cap, wide_part), bf),
            pltpu.VMEM((2, chunks, places, near, cap, wide_part), bf),
            pltpu.VMEM((2, chunks, near, cap, wide_part), bf),
            pltpu.VMEM((chunks, near, cap, wide_part), bf),
            pltpu.VMEM((chunks, toks, wide_part), bf),
            dma((3, parts)), dma((parts + 1,)), dma((2,)), dma((2,)), dma, dma, dma, dma((groups,)),
            dma((places,)), dma((places,)), dma((3,)), dma((4,)), dma((4, places)),
            dma((4, places)), dma((2, parts, groups)),
            dma((2,)), dma((2, parts)), dma, dma((groups,)),
            dma((2, chunks, places)), dma((2, chunks, places)), dma((2, chunks, places)),
            dma((2, chunks, places, near)), dma((2, chunks)), dma((chunks, near)),
            dma((chunks, near)), dma((chunks,)), dma((chunks,)),
        ],
        compiler_params=pltpu.CompilerParams(
            collective_id=0, has_side_effects=True, vmem_limit_bytes=46 * 1024 * 1024
        ),
    )(tokens, upstream, ids, gates, w_gate, w_up, w_down)


def closing(
    groups, cap, top, grad_g, grad_u, grad_d, home, home_far, home_s, slots,
    out_x, out_gates, out_g, out_u, out_d, sems,
):
    copies = []
    for i, (src, dst) in enumerate(((grad_g, out_g), (grad_u, out_u), (grad_d, out_d))):
        copy = pltpu.make_async_copy(src, dst, sems.at[i])
        copy.start()
        copies.append(copy)
    chunks, near, _, wide_part = home.shape
    rows, half = groups * cap, near * cap
    per = LANES // cap
    picks = [one_hot(slots[i:i + 1, :], 0, rows) for i in range(top)]
    pick = picks[0][0:half]
    for p in picks[1:]:
        pick = pick + p[0:half]
    pick = pick.astype(jnp.bfloat16)
    for c in range(chunks):
        value = contract_first(pick, home[c].reshape(half, wide_part))
        value = value + home_far[c].astype(jnp.float32)
        out_x[:, c * wide_part:(c + 1) * wide_part] = value.astype(jnp.bfloat16)
    terms = jnp.concatenate(
        [merged([home_s[q * per + i] for i in range(per)], cap) for q in range(rows // LANES)],
        axis=1,
    )
    for i, p in enumerate(picks):
        value = jnp.dot(terms, p, precision=lax.Precision.HIGHEST,
                        preferred_element_type=jnp.float32)
        out_gates[i:i + 1, :] = value[0:1, :]
    for copy in copies:
        copy.wait()


def close(grads, home, home_far, home_s, slots, groups, cap, top):
    vmem = pl.BlockSpec(memory_space=pltpu.VMEM)
    hbm = pl.BlockSpec(memory_space=pl.ANY)
    chunks, toks, wide_part = home_far.shape
    operands = [
        pltpu.with_memory_space_constraint(v, pltpu.VMEM)
        for v in (*grads, home, home_far, home_s, slots)
    ]
    return pl.pallas_call(
        functools.partial(closing, groups, cap, top),
        out_shape=(
            jax.ShapeDtypeStruct((toks, chunks * wide_part), jnp.bfloat16),
            jax.ShapeDtypeStruct((top, toks), jnp.float32),
            *[jax.ShapeDtypeStruct(g.shape, g.dtype) for g in grads],
        ),
        in_specs=[vmem] * 7,
        out_specs=(vmem, vmem, hbm, hbm, hbm),
        scratch_shapes=[pltpu.SemaphoreType.DMA((3,))],
        compiler_params=pltpu.CompilerParams(vmem_limit_bytes=8 * 1024 * 1024),
    )(*operands)


def per_device(tokens, upstream, gates, expert_ids, w_gate, w_up, w_down):
    groups = lax.axis_size("dp")
    parts = lax.axis_size("expert")
    experts = groups * w_gate.shape[0]
    toks = tokens.shape[0]
    top = expert_ids.shape[1]
    cap = 2 * toks * top // experts
    *grads, home, home_far, home_s, slots = exchange(
        tokens, upstream, expert_ids.T, gates.T, w_gate[0], w_up[0], w_down[0], groups, parts, cap
    )
    grad_x, grad_gates, *grads = close(grads, home, home_far, home_s, slots, groups, cap, top)
    return (grad_x, grad_gates.T, *[g[None] for g in grads])


def solution(mesh):
    in_specs = (
        P("dp", None),
        P("dp", "expert"),
        P("dp", None),
        P("dp", None),
        P("dp", "expert", None),
        P("dp", "expert", None),
        P("dp", "expert", None),
    )
    out_specs = (
        P("dp", "expert"),
        P("dp", None),
        P("dp", "expert", None),
        P("dp", "expert", None),
        P("dp", "expert", None),
    )
    return jax.shard_map(
        per_device, mesh=mesh, in_specs=in_specs, out_specs=out_specs, check_vma=False
    )
```

```python
import functools

import jax
import jax.numpy as jnp
from jax import lax
from jax.experimental import pallas as pl
from jax.experimental.pallas import tpu as pltpu
from jax.sharding import PartitionSpec as P

MESH = pl.DeviceIdType.MESH
LANES = 128


def contract_last(left, right):
    return lax.dot_general(
        left, right, (((1,), (1,)), ((), ())), preferred_element_type=jnp.float32
    )


def contract_first(left, right):
    return lax.dot_general(
        left, right, (((0,), (0,)), ((), ())), preferred_element_type=jnp.float32
    )


def matmul(left, right):
    return jnp.dot(left, right, preferred_element_type=jnp.float32)


def one_hot(slot_row, low, count):
    index = lax.broadcasted_iota(jnp.int32, (count, slot_row.shape[1]), 0) + low
    return jnp.where(index == slot_row, 1.0, 0.0)


def merged(chunks, cap):
    lane = lax.broadcasted_iota(jnp.int32, chunks[0].shape, 1)
    row = chunks[0]
    for i in range(1, len(chunks)):
        row = jnp.where(lane < i * cap, row, chunks[i])
    return row


def kernel(
    groups, parts, cap,
    tokens_hbm, upstream_hbm, ids, gates, w_g_hbm, w_u_hbm, w_d_hbm,
    out_g, out_u, out_d, home, home_far, home_s, slots,
    tok, up, far_t, far_u, far_slots, far_pick, sel_t, sel_u, sel_far, recv_t, recv_u, send_s, recv_s,
    w_gu, w_down, pre_gu, pre_down, flip_gu, flip_down, straight, term, term_recv, total_s,
    pair_send, pair_recv, own_sum, side_send, side_recv, ret_send, mid_home, comb,
    w_sem, in_sem, raw_send, raw_recv, slot_send, slot_recv, scale_send, scale_recv,
    near_send, wide_fwd, dp_send, pair_fwd, side_fwd, pass_fwd, recv_sem,
    term_send, term_sem, back_send, back_recv,
    pair_send_sem, pair_recv_sem, side_send_sem, side_recv_sem, ret_sem, home_recv, mid_recv,
    comb_send, comb_recv,
):
    me, own = lax.axis_index("dp"), lax.axis_index("expert")
    core, place = lax.rem(own, 2), lax.div(own, 2)
    places = parts // 2
    partner = place * 2 + (1 - core)
    toks, part = up.shape
    near = groups // 2
    half = near * cap
    rows = groups * cap
    hid = w_down.shape[1]
    per = LANES // cap
    chunks, wide_part = comb.shape[0], comb.shape[2]
    order = list(range(near - 1, -1, -1))
    recvs = (recv_t, recv_u)
    bf, f32 = jnp.bfloat16, jnp.float32

    def crossed(k):
        spot = me
        for bit in [1 << b for b in range(groups.bit_length()) if k >> b & 1]:
            spot = spot + bit * (1 - 2 * lax.rem(lax.div(me, bit), 2))
        return spot

    there = [crossed(k) for k in range(groups)]
    mirror = there[near]

    def aside(j):
        return lax.rem(place + j, places)

    def arrived(ref, sem):
        pltpu.make_async_copy(ref, ref, sem).wait()

    load_up = pltpu.make_async_copy(upstream_hbm, up, in_sem.at[parts])
    load_up.start()
    load_tok = []
    for j in range(parts):
        load = pltpu.make_async_copy(
            tokens_hbm.at[:, pl.ds(j * part, part)], tok.at[j], in_sem.at[j]
        )
        load.start()
        load_tok.append(load)
    barrier = pltpu.get_barrier_semaphore()
    for k in range(1, groups):
        pl.semaphore_signal(barrier, inc=1, device_id={"dp": there[k]}, device_id_type=MESH)
    for j in range(1, parts):
        pl.semaphore_signal(
            barrier, inc=1, device_id={"expert": lax.rem(own + j, parts)}, device_id_type=MESH
        )

    rel = [jnp.bitwise_xor(ids[i:i + 1, :], me) for i in range(ids.shape[0])]
    padded = max(groups, 16)
    expert_of = lax.broadcasted_iota(jnp.int32, (padded, toks), 0)
    named = jnp.where(expert_of == rel[0], 1.0, 0.0)
    for other in rel[1:]:
        named = named + jnp.where(expert_of == other, 1.0, 0.0)
    earlier = lax.broadcasted_iota(jnp.int32, (toks, toks), 0)
    earlier = jnp.where(earlier < lax.broadcasted_iota(jnp.int32, (toks, toks), 1), 1.0, 0.0)
    before = matmul(named.astype(bf), earlier.astype(bf))
    slots[...] = jnp.full(slots.shape, -1, jnp.int32)
    for i, r in enumerate(rel):
        position = jnp.sum(jnp.where(expert_of == r, before, 0.0), axis=0, keepdims=True)
        slots[i:i + 1, :] = r * cap + position.astype(jnp.int32)

    def remote(src, dst, send_sem, sem, target):
        pltpu.make_async_remote_copy(
            src_ref=src, dst_ref=dst, send_sem=send_sem, recv_sem=sem,
            device_id=target, device_id_type=MESH,
        ).start()

    load_up.wait()
    for load in load_tok:
        load.wait()
    pl.semaphore_wait(barrier, groups + parts - 2)
    remote(tok.at[own], far_t, raw_send.at[0], raw_recv.at[0], {"dp": mirror})
    remote(slots, far_slots, slot_send, slot_recv, {"dp": mirror})
    loads = {}
    for t in (1, 0):
        for j in range(parts):
            columns = pl.ds(j * part, part)
            if t:
                pairs = [(w_d_hbm.at[:, columns], w_down.at[j], 2)]
            else:
                pairs = [(w_g_hbm.at[:, columns], w_gu.at[j, pl.ds(0, hid)], 0),
                         (w_u_hbm.at[:, columns], w_gu.at[j, pl.ds(hid, hid)], 1)]
            loads[t, j] = [pltpu.make_async_copy(src, dst, w_sem.at[m, j]) for src, dst, m in pairs]
            for load in loads[t, j]:
                load.start()

    picks = [one_hot(slots[i:i + 1, :], 0, rows) for i in range(len(rel))]
    pick = sum(picks[1:], picks[0]).astype(bf)

    def relay(t, k):
        spot = recvs[t].at[own, k]
        n = t * 2 + (k // near)
        if k % near:
            arrived(spot, recv_sem.at[t, own, k])
        for j in range(1, places):
            remote(spot, spot, side_fwd.at[n, j], recv_sem.at[t, own, k],
                   {"expert": aside(j) * 2 + core})
        remote(spot, spot, pair_fwd.at[n], recv_sem.at[t, own, k], {"expert": partner})

    def pass_on(t, k):
        n = t * 2 + (k // near)
        for j in range(1, places):
            part_of = aside(j) * 2 + core
            spot = recvs[t].at[part_of, k]
            arrived(spot, recv_sem.at[t, part_of, k])
            remote(spot, spot, pass_fwd.at[n, j], recv_sem.at[t, part_of, k], {"expert": partner})

    def wide(k):
        for j in range(places):
            part_of = j * 2 + core
            spot = recv_t.at[part_of, k]
            arrived(spot, recv_sem.at[0, part_of, k])
            remote(spot, spot, wide_fwd.at[j], recv_sem.at[0, part_of, k], {"expert": partner})

    def finish(h, t):
        for k in range(h * near, (h + 1) * near):
            if (h, t) == (0, 0):
                if k:
                    for j in range(places):
                        part_of = j * 2 + 1 - core
                        arrived(recv_t.at[part_of, k], recv_sem.at[0, part_of, k])
            else:
                for j in range(places):
                    part_of = aside(j) * 2 + 1 - core
                    arrived(recvs[t].at[part_of, k], recv_sem.at[t, part_of, k])

    chosen = matmul(pick[0:half], up[...]).astype(bf).reshape(near, cap, part)
    recv_u[own, 0] = chosen[0]
    relay(1, 0)
    for k in range(1, near):
        sel_u[k] = chosen[k]
        remote(sel_u.at[k], recv_u.at[own, k], dp_send.at[0], recv_sem.at[1, own, k],
               {"dp": there[k]})
    for j in range(places):
        chosen = matmul(pick[0:half], tok[j * 2 + core]).astype(bf).reshape(near, cap, part)
        recv_t[j * 2 + core, 0] = chosen[0]
        for k in range(1, near):
            sel_t[j, k] = chosen[k]

    def send_wide(k):
        for j in range(places):
            spot = j * 2 + core
            remote(sel_t.at[j, k], recv_t.at[spot, k], near_send.at[j], recv_sem.at[0, spot, k],
                   {"dp": there[k]})

    scale_rows = None
    for i, p in enumerate(picks):
        gate = jnp.broadcast_to(gates[i:i + 1, :], (16, toks))
        value = contract_last(gate, p.astype(bf))
        scale_rows = value if i == 0 else scale_rows + value
    for q in range(rows // LANES):
        send_s[q] = scale_rows[0:8, q * LANES:(q + 1) * LANES]
    recv_s[0] = send_s[0]
    for k in range(1, groups):
        remote(send_s.at[k // per], recv_s.at[k], scale_send, scale_recv.at[k], {"dp": there[k]})
    for j in range(places):
        recv_t[j * 2 + 1 - core, 0] = matmul(pick[0:cap], tok[j * 2 + 1 - core]).astype(bf)

    def expand(t):
        if t == 0:
            arrived(far_slots, slot_recv)
            value = one_hot(far_slots[0:1, :], half, half)
            for i in range(1, ids.shape[0]):
                value = value + one_hot(far_slots[i:i + 1, :], half, half)
            far_pick[...] = value.astype(bf)
        source = (far_t, far_u)[t]
        arrived(source, raw_recv.at[t])
        value = matmul(far_pick[...], source[...]).astype(bf).reshape(near, cap, part)
        recvs[t][own, near] = value[0]
        for k in range(1, near):
            sel_far[t, k] = value[k]
            remote(sel_far.at[t, k], recvs[t].at[own, near + k], dp_send.at[1 + t],
                   recv_sem.at[t, own, near + k], {"dp": there[k]})
        relay(t, near)

    def forward_unit(h, t, j):
        if h == 1 - t:
            for load in loads[t, j]:
                load.wait()
        block = recvs[t][j, h * near:(h + 1) * near].reshape(half, part)
        pre = (pre_gu, pre_down)[t]
        value = contract_last((w_gu, w_down)[t][j], block)
        if j == 0:
            pre[h] = value
        else:
            pre[h] = pre[h] + value

    tile = 32

    def activate(h):
        for k in range(max(1, h * near), (h + 1) * near):
            arrived(recv_s.at[k], scale_recv.at[k])
        scale = jnp.concatenate(
            [merged([recv_s[q * per + i] for i in range(per)], cap)
             for q in range(h * half // LANES, (h + 1) * half // LANES)], axis=1
        )[0:1, :]
        term[h] = jnp.zeros((8, half), f32)

        @pl.loop(0, hid // tile)
        def _(step):
            low = pl.multiple_of(step * tile, tile)
            at = pl.ds(low, tile)
            above = pl.ds(pl.multiple_of(low + hid, tile), tile)
            columns = pl.ds(h * half, half)
            gate, lift, back = pre_gu[h, at, :], pre_gu[h, above, :], pre_down[h, at, :]
            sigma = jax.nn.sigmoid(gate)
            swish = gate * sigma
            slope = sigma * (1.0 + gate * (1.0 - sigma))
            act = (swish * lift).astype(bf).astype(f32)
            term[h] += jnp.broadcast_to(jnp.sum(act * back, axis=0, keepdims=True), (8, half))
            weighted = scale * back
            flip_gu[at, columns] = (weighted * lift * slope).astype(bf)
            flip_gu[above, columns] = (weighted * swish).astype(bf)
            flip_down[at, columns] = (scale * act).astype(bf)

        for j in range(1, parts):
            remote(term.at[h], term_recv.at[h, own], term_send.at[h], term_sem.at[h, own],
                   {"expert": lax.rem(own + j, parts)})
        block = flip_gu[:, h * half:(h + 1) * half].astype(f32)
        straight[h] = jnp.transpose(block).astype(bf)

    def piece(h, c, which):
        columns = pl.ds(c * wide_part, wide_part)
        value = matmul(straight[h], w_gu[which, :, columns])
        return value.reshape(near, cap, wide_part)

    def pair_step(h, c, j):
        spot = aside(j) * 2
        pair_send[h, c, j] = piece(h, c, spot + 1 - core).astype(bf)
        remote(pair_send.at[h, c, j], pair_recv.at[h, c, j], pair_send_sem.at[h, c, j],
               pair_recv_sem.at[h, c, j], {"expert": partner})
        own_sum[h, c, j] = piece(h, c, spot + core)

    def side_step(h, c, j):
        arrived(pair_recv.at[h, c, j], pair_recv_sem.at[h, c, j])
        for k in order:
            both = own_sum[h, c, j, k] + pair_recv[h, c, j, k].astype(f32)
            side_send[h, c, j, k] = both.astype(bf)
            remote(side_send.at[h, c, j, k], side_recv.at[h, c, j, k], side_send_sem.at[h, c, j],
                   side_recv_sem.at[h, c, j, k], {"expert": aside(j) * 2 + core})

    def return_step(h, c, k):
        if k == order[0]:
            arrived(pair_recv.at[h, c, 0], pair_recv_sem.at[h, c, 0])
        value = own_sum[h, c, 0, k] + pair_recv[h, c, 0, k].astype(f32)
        for j in range(1, places):
            arrived(side_recv.at[h, c, j, k], side_recv_sem.at[h, c, j, k])
            value = value + side_recv[h, c, j, k].astype(f32)
        goal, sem = ((home, home_recv), (mid_home, mid_recv))[h]
        if k == 0:
            goal[c, 0] = value.astype(bf)
        else:
            ret_send[h, c, k] = value.astype(bf)
            remote(ret_send.at[h, c, k], goal.at[c, k], ret_sem.at[h, c], sem.at[c, k],
                   {"dp": there[k]})

    def combine(c):
        for k in range(1, near):
            arrived(mid_home.at[c, k], mid_recv.at[c, k])
        value = contract_first(far_pick[...], mid_home[c].reshape(half, wide_part))
        comb[c] = value.astype(bf)
        remote(comb.at[c], home_far.at[c], comb_send.at[c], comb_recv.at[c], {"dp": mirror})

    def term_step(h):
        for j in range(1, parts):
            other = lax.rem(own + j, parts)
            arrived(term_recv.at[h, other], term_sem.at[h, other])
        term_recv[h, own] = term[h]
        total = term_recv[h, 0]
        for j in range(1, parts):
            total = total + term_recv[h, j]
        for q in range(half // LANES):
            total_s[h * half // LANES + q] = total[:, q * LANES:(q + 1) * LANES]
        for k in range(h * near, (h + 1) * near):
            if k == 0:
                home_s[0] = total_s[0]
            else:
                remote(total_s.at[k // per], home_s.at[k], back_send, back_recv.at[k],
                       {"dp": there[k]})

    def grad_unit(m, j):
        block = recvs[m // 2][j].reshape(rows, part)
        left = flip_down[...] if m == 2 else flip_gu[m * hid:(m + 1) * hid, :]
        (out_g, out_u, out_d)[m][:, j * part:(j + 1) * part] = matmul(left, block).astype(bf)

    grads = [(m, j) for m in range(3) for j in range(parts)]

    def some_grads(count):
        for _ in range(count):
            if grads:
                grad_unit(*grads.pop(0))

    def raw_up():
        remote(up, far_u, raw_send.at[1], raw_recv.at[1], {"dp": mirror})

    def near_up():
        finish(0, 1)
        for j in range(parts):
            forward_unit(0, 1, j)

    later = range(2, near)
    far_later = [near + k for k in later]
    outer_steps = (
        [(relay, 1, 1), (pass_on, 1, 0)] + [(relay, 1, k) for k in later]
        + [(pass_on, 1, 1)] + [(pass_on, 1, k) for k in later[:1]] + [(raw_up,), (expand, 0)]
        + [(relay, 0, near + 1)] + [(pass_on, 1, k) for k in later[1:]] + [(relay, 0, k) for k in far_later]
        + [(pass_on, 0, near), (expand, 1), (pass_on, 0, near + 1)]
        + [(send_wide, k) for k in later] + [(relay, 1, k) for k in far_later[:1]]
        + [(relay, 1, near + 1)] + [(relay, 1, k) for k in far_later[1:]]
        + [(send_wide, 1)] + [(pass_on, 0, k) for k in far_later] + [(near_up,)]
    )
    inner_steps = (
        [(raw_up,), (relay, 1, 1), (pass_on, 1, 0), (expand, 0), (pass_on, 1, 1)]
        + [(relay, 1, k) for k in later] + [(relay, 0, near + 1), (pass_on, 0, near)]
        + [(pass_on, 1, k) for k in later]
        + [(expand, 1), (pass_on, 0, near + 1)] + [(relay, 0, k) for k in far_later]
        + [(relay, 1, near + 1)] + [(send_wide, k) for k in later]
        + [(relay, 1, k) for k in far_later] + [(send_wide, 1)]
        + [(pass_on, 0, k) for k in far_later] + [(near_up,)]
    )
    inner = lax.rem(lax.div(me, near) + lax.div(me, max(1, near // 2)), 2) == 1

    def run(steps):
        for step, *at in steps:
            step(*at)

    pl.when(inner)(functools.partial(run, inner_steps))
    pl.when(jnp.logical_not(inner))(functools.partial(run, outer_steps))
    finish(1, 0)
    passes = [near] + far_later[:1] + [near + 1] + far_later[1:]
    for j in range(parts):
        if passes:
            pass_on(1, passes.pop(0))
        forward_unit(1, 0, j)
    for k in passes:
        pass_on(1, k)
    finish(1, 1)
    for j in range(parts):
        forward_unit(1, 1, j)
    activate(1)
    aside_first = list(range(1, places)) + [0]
    for c in range(chunks):
        for j in aside_first[:-1]:
            pair_step(1, c, j)
            side_step(1, c, j)
    for k in range(1, near):
        wide(k)
    for c in range(chunks):
        pair_step(1, c, 0)
    finish(0, 0)
    rest = list(order)
    for j in range(parts):
        forward_unit(0, 0, j)
        if j and rest:
            return_step(1, 0, rest.pop(0))
    activate(0)
    for k in rest:
        return_step(1, 0, k)
    rest = [(c, k) for c in range(1, chunks) for k in order]
    for c in range(chunks):
        for j in aside_first[:-1]:
            pair_step(0, c, j)
            side_step(0, c, j)
        for _ in range(near // 2):
            if rest:
                return_step(1, *rest.pop(0))
    for at in rest:
        return_step(1, *at)
    combine(0)
    for c in range(chunks):
        pair_step(0, c, 0)
    term_step(1)
    term_step(0)
    some_grads(1)
    for k in order:
        some_grads(1)
        return_step(0, 0, k)
    combine(chunks - 1)
    for c in range(1, chunks):
        for k in order:
            some_grads(1)
            return_step(0, c, k)
    some_grads(len(grads))

    for c in range(chunks):
        for k in range(1, near):
            arrived(home.at[c, k], home_recv.at[c, k])
        arrived(home_far.at[c], comb_recv.at[c])
    for k in range(1, groups):
        arrived(home_s.at[k], back_recv.at[k])

    few, all_near = recv_t.at[0, pl.ds(0, near - 1)], recv_t.at[0, pl.ds(0, near)]
    for t in range(2):
        arrived((far_t, far_u)[t], raw_send.at[t])
    arrived(far_slots, slot_send)
    arrived(recv_s.at[pl.ds(0, groups - 1)], scale_send)
    for j in range(places):
        arrived(few, near_send.at[j])
        arrived(few, wide_fwd.at[j])
    for i in range(3):
        arrived(few, dp_send.at[i])
    for n in range(1, 4):
        arrived(all_near, pair_fwd.at[n])
        for j in range(1, places):
            arrived(all_near, side_fwd.at[n, j])
            arrived(all_near, pass_fwd.at[n, j])
    for h in range(2):
        arrived(term_recv.at[h, pl.ds(0, parts - 1)], term_send.at[h])
        for c in range(chunks):
            arrived(ret_send.at[h, c, pl.ds(0, near - 1)], ret_sem.at[h, c])
            for j in range(places):
                arrived(pair_send.at[h, c, j], pair_send_sem.at[h, c, j])
                if j:
                    arrived(side_send.at[h, c, j], side_send_sem.at[h, c, j])
    arrived(home_s.at[pl.ds(0, groups - 1)], back_send)
    for c in range(chunks):
        arrived(comb.at[c], comb_send.at[c])


def exchange(tokens, upstream, ids, gates, w_gate, w_up, w_down, groups, parts, cap):
    toks, part = upstream.shape
    rows = groups * cap
    near = groups // 2
    half = near * cap
    hid, width = w_gate.shape
    places = parts // 2
    chunks = 2
    wide_part = part // chunks
    bf, f32 = jnp.bfloat16, jnp.float32
    dma = pltpu.SemaphoreType.DMA
    vmem = pl.BlockSpec(memory_space=pltpu.VMEM)
    hbm = pl.BlockSpec(memory_space=pl.ANY)
    return pl.pallas_call(
        functools.partial(kernel, groups, parts, cap),
        out_shape=(
            pltpu.VMEM((hid, width), bf), pltpu.VMEM((hid, width), bf), pltpu.VMEM((hid, width), bf),
            pltpu.VMEM((chunks, near, cap, wide_part), bf), pltpu.VMEM((chunks, toks, wide_part), bf),
            pltpu.VMEM((groups, 8, LANES), f32), pltpu.VMEM((8, toks), jnp.int32),
        ),
        in_specs=[hbm, hbm, vmem, vmem, hbm, hbm, hbm],
        out_specs=(vmem,) * 7,
        scratch_shapes=[
            pltpu.VMEM((parts, toks, part), bf),
            pltpu.VMEM((toks, part), bf),
            pltpu.VMEM((toks, part), bf),
            pltpu.VMEM((toks, part), bf),
            pltpu.VMEM((8, toks), jnp.int32),
            pltpu.VMEM((half, toks), bf),
            pltpu.VMEM((places, near, cap, part), bf),
            pltpu.VMEM((near, cap, part), bf),
            pltpu.VMEM((2, near, cap, part), bf),
            pltpu.VMEM((parts, groups, cap, part), bf),
            pltpu.VMEM((parts, groups, cap, part), bf),
            pltpu.VMEM((rows // LANES, 8, LANES), f32),
            pltpu.VMEM((groups, 8, LANES), f32),
            pltpu.VMEM((parts, 2 * hid, part), bf),
            pltpu.VMEM((parts, hid, part), bf),
            pltpu.VMEM((2, 2 * hid, half), f32),
            pltpu.VMEM((2, hid, half), f32),
            pltpu.VMEM((2 * hid, rows), bf),
            pltpu.VMEM((hid, rows), bf),
            pltpu.VMEM((2, half, 2 * hid), bf),
            pltpu.VMEM((2, 8, half), f32),
            pltpu.VMEM((2, parts, 8, half), f32),
            pltpu.VMEM((rows // LANES, 8, LANES), f32),
            pltpu.VMEM((2, chunks, places, near, cap, wide_part), bf),
            pltpu.VMEM((2, chunks, places, near, cap, wide_part), bf),
            pltpu.VMEM((2, chunks, places, near, cap, wide_part), f32),
            pltpu.VMEM((2, chunks, places, near, cap, wide_part), bf),
            pltpu.VMEM((2, chunks, places, near, cap, wide_part), bf),
            pltpu.VMEM((2, chunks, near, cap, wide_part), bf),
            pltpu.VMEM((chunks, near, cap, wide_part), bf),
            pltpu.VMEM((chunks, toks, wide_part), bf),
            dma((3, parts)), dma((parts + 1,)), dma((2,)), dma((2,)), dma, dma, dma, dma((groups,)),
            dma((places,)), dma((places,)), dma((3,)), dma((4,)), dma((4, places)),
            dma((4, places)), dma((2, parts, groups)),
            dma((2,)), dma((2, parts)), dma, dma((groups,)),
            dma((2, chunks, places)), dma((2, chunks, places)), dma((2, chunks, places)),
            dma((2, chunks, places, near)), dma((2, chunks)), dma((chunks, near)),
            dma((chunks, near)), dma((chunks,)), dma((chunks,)),
        ],
        compiler_params=pltpu.CompilerParams(
            collective_id=0, has_side_effects=True, vmem_limit_bytes=46 * 1024 * 1024
        ),
    )(tokens, upstream, ids, gates, w_gate, w_up, w_down)


def closing(
    groups, cap, top, grad_g, grad_u, grad_d, home, home_far, home_s, slots,
    out_x, out_gates, out_g, out_u, out_d, sems,
):
    copies = []
    for i, (src, dst) in enumerate(((grad_g, out_g), (grad_u, out_u), (grad_d, out_d))):
        copy = pltpu.make_async_copy(src, dst, sems.at[i])
        copy.start()
        copies.append(copy)
    chunks, near, _, wide_part = home.shape
    rows, half = groups * cap, near * cap
    per = LANES // cap
    picks = [one_hot(slots[i:i + 1, :], 0, rows) for i in range(top)]
    pick = picks[0][0:half]
    for p in picks[1:]:
        pick = pick + p[0:half]
    pick = pick.astype(jnp.bfloat16)
    for c in range(chunks):
        value = contract_first(pick, home[c].reshape(half, wide_part))
        value = value + home_far[c].astype(jnp.float32)
        out_x[:, c * wide_part:(c + 1) * wide_part] = value.astype(jnp.bfloat16)
    terms = jnp.concatenate(
        [merged([home_s[q * per + i] for i in range(per)], cap) for q in range(rows // LANES)],
        axis=1,
    )
    for i, p in enumerate(picks):
        value = jnp.dot(terms, p, precision=lax.Precision.HIGHEST,
                        preferred_element_type=jnp.float32)
        out_gates[i:i + 1, :] = value[0:1, :]
    for copy in copies:
        copy.wait()


def close(grads, home, home_far, home_s, slots, groups, cap, top):
    vmem = pl.BlockSpec(memory_space=pltpu.VMEM)
    hbm = pl.BlockSpec(memory_space=pl.ANY)
    chunks, toks, wide_part = home_far.shape
    operands = [
        pltpu.with_memory_space_constraint(v, pltpu.VMEM)
        for v in (*grads, home, home_far, home_s, slots)
    ]
    return pl.pallas_call(
        functools.partial(closing, groups, cap, top),
        out_shape=(
            jax.ShapeDtypeStruct((toks, chunks * wide_part), jnp.bfloat16),
            jax.ShapeDtypeStruct((top, toks), jnp.float32),
            *[jax.ShapeDtypeStruct(g.shape, g.dtype) for g in grads],
        ),
        in_specs=[vmem] * 7,
        out_specs=(vmem, vmem, hbm, hbm, hbm),
        scratch_shapes=[pltpu.SemaphoreType.DMA((3,))],
        compiler_params=pltpu.CompilerParams(vmem_limit_bytes=8 * 1024 * 1024),
    )(*operands)


def per_device(tokens, upstream, gates, expert_ids, w_gate, w_up, w_down):
    groups = lax.axis_size("dp")
    parts = lax.axis_size("expert")
    experts = groups * w_gate.shape[0]
    toks = tokens.shape[0]
    top = expert_ids.shape[1]
    cap = 2 * toks * top // experts
    *grads, home, home_far, home_s, slots = exchange(
        tokens, upstream, expert_ids.T, gates.T, w_gate[0], w_up[0], w_down[0], groups, parts, cap
    )
    grad_x, grad_gates, *grads = close(grads, home, home_far, home_s, slots, groups, cap, top)
    return (grad_x, grad_gates.T, *[g[None] for g in grads])


def solution(mesh):
    in_specs = (
        P("dp", None),
        P("dp", "expert"),
        P("dp", None),
        P("dp", None),
        P("dp", "expert", None),
        P("dp", "expert", None),
        P("dp", "expert", None),
    )
    out_specs = (
        P("dp", "expert"),
        P("dp", None),
        P("dp", "expert", None),
        P("dp", "expert", None),
        P("dp", "expert", None),
    )
    return jax.shard_map(
        per_device, mesh=mesh, in_specs=in_specs, out_specs=out_specs, check_vma=False
    )
```

```python
import functools

import jax
import jax.numpy as jnp
from jax import lax
from jax.experimental import pallas as pl
from jax.experimental.pallas import tpu as pltpu
from jax.sharding import PartitionSpec as P

MESH = pl.DeviceIdType.MESH
LANES = 128


def contract_last(left, right):
    return lax.dot_general(
        left, right, (((1,), (1,)), ((), ())), preferred_element_type=jnp.float32
    )


def contract_first(left, right):
    return lax.dot_general(
        left, right, (((0,), (0,)), ((), ())), preferred_element_type=jnp.float32
    )


def matmul(left, right):
    return jnp.dot(left, right, preferred_element_type=jnp.float32)


def one_hot(slot_row, low, count):
    index = lax.broadcasted_iota(jnp.int32, (count, slot_row.shape[1]), 0) + low
    return jnp.where(index == slot_row, 1.0, 0.0)


def merged(chunks, cap):
    lane = lax.broadcasted_iota(jnp.int32, chunks[0].shape, 1)
    row = chunks[0]
    for i in range(1, len(chunks)):
        row = jnp.where(lane < i * cap, row, chunks[i])
    return row


def kernel(
    groups, parts, cap,
    tokens_hbm, upstream_hbm, ids, gates, w_g_hbm, w_u_hbm, w_d_hbm,
    out_g, out_u, out_d, home, home_far, home_s, slots,
    tok, up, far_t, far_u, far_slots, far_pick, sel_t, sel_u, sel_far, recv_t, recv_u, send_s, recv_s,
    w_gu, w_down, pre_gu, pre_down, flip_gu, flip_down, straight, term, term_recv, total_s,
    pair_send, pair_recv, own_sum, side_send, side_recv, ret_send, mid_home, comb,
    w_sem, in_sem, raw_send, raw_recv, slot_send, slot_recv, scale_send, scale_recv,
    near_send, wide_fwd, dp_send, pair_fwd, side_fwd, pass_fwd, recv_sem,
    term_send, term_sem, back_send, back_recv,
    pair_send_sem, pair_recv_sem, side_send_sem, side_recv_sem, ret_sem, home_recv, mid_recv,
    comb_send, comb_recv,
):
    me, own = lax.axis_index("dp"), lax.axis_index("expert")
    core, place = lax.rem(own, 2), lax.div(own, 2)
    places = parts // 2
    partner = place * 2 + (1 - core)
    toks, part = up.shape
    near = groups // 2
    half = near * cap
    rows = groups * cap
    hid = w_down.shape[1]
    per = LANES // cap
    chunks, wide_part = comb.shape[0], comb.shape[2]
    order = list(range(near - 1, -1, -1))
    recvs = (recv_t, recv_u)
    bf, f32 = jnp.bfloat16, jnp.float32

    def crossed(k):
        spot = me
        for bit in [1 << b for b in range(groups.bit_length()) if k >> b & 1]:
            spot = spot + bit * (1 - 2 * lax.rem(lax.div(me, bit), 2))
        return spot

    there = [crossed(k) for k in range(groups)]
    mirror = there[near]

    def aside(j):
        return lax.rem(place + j, places)

    def arrived(ref, sem):
        pltpu.make_async_copy(ref, ref, sem).wait()

    load_up = pltpu.make_async_copy(upstream_hbm, up, in_sem.at[parts])
    load_up.start()
    load_tok = []
    for j in range(parts):
        load = pltpu.make_async_copy(
            tokens_hbm.at[:, pl.ds(j * part, part)], tok.at[j], in_sem.at[j]
        )
        load.start()
        load_tok.append(load)
    barrier = pltpu.get_barrier_semaphore()
    for k in range(1, groups):
        pl.semaphore_signal(barrier, inc=1, device_id={"dp": there[k]}, device_id_type=MESH)
    for j in range(1, parts):
        pl.semaphore_signal(
            barrier, inc=1, device_id={"expert": lax.rem(own + j, parts)}, device_id_type=MESH
        )

    rel = [jnp.bitwise_xor(ids[i:i + 1, :], me) for i in range(ids.shape[0])]
    padded = max(groups, 16)
    expert_of = lax.broadcasted_iota(jnp.int32, (padded, toks), 0)
    named = jnp.where(expert_of == rel[0], 1.0, 0.0)
    for other in rel[1:]:
        named = named + jnp.where(expert_of == other, 1.0, 0.0)
    earlier = lax.broadcasted_iota(jnp.int32, (toks, toks), 0)
    earlier = jnp.where(earlier < lax.broadcasted_iota(jnp.int32, (toks, toks), 1), 1.0, 0.0)
    before = matmul(named.astype(bf), earlier.astype(bf))
    slots[...] = jnp.full(slots.shape, -1, jnp.int32)
    for i, r in enumerate(rel):
        position = jnp.sum(jnp.where(expert_of == r, before, 0.0), axis=0, keepdims=True)
        slots[i:i + 1, :] = r * cap + position.astype(jnp.int32)

    def remote(src, dst, send_sem, sem, target):
        pltpu.make_async_remote_copy(
            src_ref=src, dst_ref=dst, send_sem=send_sem, recv_sem=sem,
            device_id=target, device_id_type=MESH,
        ).start()

    load_up.wait()
    for load in load_tok:
        load.wait()
    pl.semaphore_wait(barrier, groups + parts - 2)
    remote(tok.at[own], far_t, raw_send.at[0], raw_recv.at[0], {"dp": mirror})
    remote(slots, far_slots, slot_send, slot_recv, {"dp": mirror})
    loads = {}
    for t in (1, 0):
        for j in range(parts):
            columns = pl.ds(j * part, part)
            if t:
                pairs = [(w_d_hbm.at[:, columns], w_down.at[j], 2)]
            else:
                pairs = [(w_g_hbm.at[:, columns], w_gu.at[j, pl.ds(0, hid)], 0),
                         (w_u_hbm.at[:, columns], w_gu.at[j, pl.ds(hid, hid)], 1)]
            loads[t, j] = [pltpu.make_async_copy(src, dst, w_sem.at[m, j]) for src, dst, m in pairs]
            for load in loads[t, j]:
                load.start()

    picks = [one_hot(slots[i:i + 1, :], 0, rows) for i in range(len(rel))]
    pick = sum(picks[1:], picks[0]).astype(bf)

    def relay(t, k):
        spot = recvs[t].at[own, k]
        n = t * 2 + (k // near)
        if k % near:
            arrived(spot, recv_sem.at[t, own, k])
        for j in range(1, places):
            remote(spot, spot, side_fwd.at[n, j], recv_sem.at[t, own, k],
                   {"expert": aside(j) * 2 + core})
        remote(spot, spot, pair_fwd.at[n], recv_sem.at[t, own, k], {"expert": partner})

    def pass_on(t, k):
        n = t * 2 + (k // near)
        for j in range(1, places):
            part_of = aside(j) * 2 + core
            spot = recvs[t].at[part_of, k]
            arrived(spot, recv_sem.at[t, part_of, k])
            remote(spot, spot, pass_fwd.at[n, j], recv_sem.at[t, part_of, k], {"expert": partner})

    def wide(k):
        for j in range(places):
            part_of = j * 2 + core
            spot = recv_t.at[part_of, k]
            arrived(spot, recv_sem.at[0, part_of, k])
            remote(spot, spot, wide_fwd.at[j], recv_sem.at[0, part_of, k], {"expert": partner})

    def finish(h, t):
        for k in range(h * near, (h + 1) * near):
            if (h, t) == (0, 0):
                if k:
                    for j in range(places):
                        part_of = j * 2 + 1 - core
                        arrived(recv_t.at[part_of, k], recv_sem.at[0, part_of, k])
            else:
                for j in range(places):
                    part_of = aside(j) * 2 + 1 - core
                    arrived(recvs[t].at[part_of, k], recv_sem.at[t, part_of, k])

    chosen = matmul(pick[0:half], up[...]).astype(bf).reshape(near, cap, part)
    recv_u[own, 0] = chosen[0]
    relay(1, 0)
    for k in range(1, near):
        sel_u[k] = chosen[k]
        remote(sel_u.at[k], recv_u.at[own, k], dp_send.at[0], recv_sem.at[1, own, k],
               {"dp": there[k]})
    for j in range(places):
        chosen = matmul(pick[0:half], tok[j * 2 + core]).astype(bf).reshape(near, cap, part)
        recv_t[j * 2 + core, 0] = chosen[0]
        for k in range(1, near):
            sel_t[j, k] = chosen[k]

    def send_wide(k):
        for j in range(places):
            spot = j * 2 + core
            remote(sel_t.at[j, k], recv_t.at[spot, k], near_send.at[j], recv_sem.at[0, spot, k],
                   {"dp": there[k]})

    scale_rows = None
    for i, p in enumerate(picks):
        gate = jnp.broadcast_to(gates[i:i + 1, :], (16, toks))
        value = contract_last(gate, p.astype(bf))
        scale_rows = value if i == 0 else scale_rows + value
    for q in range(rows // LANES):
        send_s[q] = scale_rows[0:8, q * LANES:(q + 1) * LANES]
    recv_s[0] = send_s[0]
    for k in range(1, groups):
        remote(send_s.at[k // per], recv_s.at[k], scale_send, scale_recv.at[k], {"dp": there[k]})
    for j in range(places):
        recv_t[j * 2 + 1 - core, 0] = matmul(pick[0:cap], tok[j * 2 + 1 - core]).astype(bf)

    def expand(t):
        if t == 0:
            arrived(far_slots, slot_recv)
            value = one_hot(far_slots[0:1, :], half, half)
            for i in range(1, ids.shape[0]):
                value = value + one_hot(far_slots[i:i + 1, :], half, half)
            far_pick[...] = value.astype(bf)
        source = (far_t, far_u)[t]
        arrived(source, raw_recv.at[t])
        value = matmul(far_pick[...], source[...]).astype(bf).reshape(near, cap, part)
        recvs[t][own, near] = value[0]
        for k in range(1, near):
            sel_far[t, k] = value[k]
            remote(sel_far.at[t, k], recvs[t].at[own, near + k], dp_send.at[1 + t],
                   recv_sem.at[t, own, near + k], {"dp": there[k]})
        relay(t, near)

    def forward_unit(h, t, j, first):
        block = recvs[t][j, h * near:(h + 1) * near].reshape(half, part)
        pre = (pre_gu, pre_down)[t]
        value = contract_last((w_gu, w_down)[t][j], block)
        if first:
            pre[h] = value
        else:
            pre[h] = pre[h] + value

    tile = 32

    def activate(h):
        for k in range(max(1, h * near), (h + 1) * near):
            arrived(recv_s.at[k], scale_recv.at[k])
        scale = jnp.concatenate(
            [merged([recv_s[q * per + i] for i in range(per)], cap)
             for q in range(h * half // LANES, (h + 1) * half // LANES)], axis=1
        )[0:1, :]
        term[h] = jnp.zeros((8, half), f32)

        @pl.loop(0, hid // tile)
        def _(step):
            low = pl.multiple_of(step * tile, tile)
            at = pl.ds(low, tile)
            above = pl.ds(pl.multiple_of(low + hid, tile), tile)
            columns = pl.ds(h * half, half)
            gate, lift, back = pre_gu[h, at, :], pre_gu[h, above, :], pre_down[h, at, :]
            sigma = jax.nn.sigmoid(gate)
            swish = gate * sigma
            slope = sigma * (1.0 + gate * (1.0 - sigma))
            act = (swish * lift).astype(bf).astype(f32)
            term[h] += jnp.broadcast_to(jnp.sum(act * back, axis=0, keepdims=True), (8, half))
            weighted = scale * back
            flip_gu[at, columns] = (weighted * lift * slope).astype(bf)
            flip_gu[above, columns] = (weighted * swish).astype(bf)
            flip_down[at, columns] = (scale * act).astype(bf)

        for j in range(1, parts):
            remote(term.at[h], term_recv.at[h, own], term_send.at[h], term_sem.at[h, own],
                   {"expert": lax.rem(own + j, parts)})
        block = flip_gu[:, h * half:(h + 1) * half].astype(f32)
        straight[h] = jnp.transpose(block).astype(bf)

    def piece(h, c, which):
        columns = pl.ds(c * wide_part, wide_part)
        value = matmul(straight[h], w_gu[which, :, columns])
        return value.reshape(near, cap, wide_part)

    def pair_step(h, c, j):
        spot = aside(j) * 2
        pair_send[h, c, j] = piece(h, c, spot + 1 - core).astype(bf)
        remote(pair_send.at[h, c, j], pair_recv.at[h, c, j], pair_send_sem.at[h, c, j],
               pair_recv_sem.at[h, c, j], {"expert": partner})
        own_sum[h, c, j] = piece(h, c, spot + core)

    def side_step(h, c, j):
        arrived(pair_recv.at[h, c, j], pair_recv_sem.at[h, c, j])
        for k in order:
            both = own_sum[h, c, j, k] + pair_recv[h, c, j, k].astype(f32)
            side_send[h, c, j, k] = both.astype(bf)
            remote(side_send.at[h, c, j, k], side_recv.at[h, c, j, k], side_send_sem.at[h, c, j],
                   side_recv_sem.at[h, c, j, k], {"expert": aside(j) * 2 + core})

    def return_step(h, c, k):
        if k == order[0]:
            arrived(pair_recv.at[h, c, 0], pair_recv_sem.at[h, c, 0])
        value = own_sum[h, c, 0, k] + pair_recv[h, c, 0, k].astype(f32)
        for j in range(1, places):
            arrived(side_recv.at[h, c, j, k], side_recv_sem.at[h, c, j, k])
            value = value + side_recv[h, c, j, k].astype(f32)
        goal, sem = ((home, home_recv), (mid_home, mid_recv))[h]
        if k == 0:
            goal[c, 0] = value.astype(bf)
        else:
            ret_send[h, c, k] = value.astype(bf)
            remote(ret_send.at[h, c, k], goal.at[c, k], ret_sem.at[h, c], sem.at[c, k],
                   {"dp": there[k]})

    def combine(c):
        for k in range(1, near):
            arrived(mid_home.at[c, k], mid_recv.at[c, k])
        value = contract_first(far_pick[...], mid_home[c].reshape(half, wide_part))
        comb[c] = value.astype(bf)
        remote(comb.at[c], home_far.at[c], comb_send.at[c], comb_recv.at[c], {"dp": mirror})

    def term_step(h):
        for j in range(1, parts):
            other = lax.rem(own + j, parts)
            arrived(term_recv.at[h, other], term_sem.at[h, other])
        term_recv[h, own] = term[h]
        total = term_recv[h, 0]
        for j in range(1, parts):
            total = total + term_recv[h, j]
        for q in range(half // LANES):
            total_s[h * half // LANES + q] = total[:, q * LANES:(q + 1) * LANES]
        for k in range(h * near, (h + 1) * near):
            if k == 0:
                home_s[0] = total_s[0]
            else:
                remote(total_s.at[k // per], home_s.at[k], back_send, back_recv.at[k],
                       {"dp": there[k]})

    def grad_unit(m, j):
        block = recvs[m // 2][j].reshape(rows, part)
        left = flip_down[...] if m == 2 else flip_gu[m * hid:(m + 1) * hid, :]
        (out_g, out_u, out_d)[m][:, j * part:(j + 1) * part] = matmul(left, block).astype(bf)

    grads = [(m, j) for m in range(3) for j in range(parts)]

    def some_grads(count):
        for _ in range(count):
            if grads:
                grad_unit(*grads.pop(0))

    def raw_up():
        remote(up, far_u, raw_send.at[1], raw_recv.at[1], {"dp": mirror})

    def near_up():
        finish(0, 1)
        for j in range(parts):
            loads[1, j][0].wait()
            forward_unit(0, 1, j, j == 0)

    later = range(2, near)
    far_later = [near + k for k in later]
    outer_steps = (
        [(relay, 1, 1), (pass_on, 1, 0)] + [(relay, 1, k) for k in later]
        + [(pass_on, 1, 1)] + [(pass_on, 1, k) for k in later[:1]] + [(raw_up,), (expand, 0)]
        + [(relay, 0, near + 1)] + [(pass_on, 1, k) for k in later[1:]] + [(relay, 0, k) for k in far_later]
        + [(pass_on, 0, near), (expand, 1), (pass_on, 0, near + 1)]
        + [(send_wide, k) for k in later] + [(relay, 1, k) for k in far_later[:1]]
        + [(relay, 1, near + 1)] + [(relay, 1, k) for k in far_later[1:]]
        + [(send_wide, 1)] + [(pass_on, 0, k) for k in far_later] + [(near_up,)]
    )
    inner_steps = (
        [(raw_up,), (relay, 1, 1), (pass_on, 1, 0), (expand, 0), (pass_on, 1, 1)]
        + [(relay, 1, k) for k in later] + [(relay, 0, near + 1), (pass_on, 0, near)]
        + [(pass_on, 1, k) for k in later]
        + [(expand, 1), (pass_on, 0, near + 1)] + [(relay, 0, k) for k in far_later]
        + [(relay, 1, near + 1)] + [(send_wide, k) for k in later]
        + [(relay, 1, k) for k in far_later] + [(send_wide, 1)]
        + [(pass_on, 0, k) for k in far_later] + [(near_up,)]
    )
    inner = lax.rem(lax.div(me, near) + lax.div(me, max(1, near // 2)), 2) == 1

    def run(steps):
        for step, *at in steps:
            step(*at)

    pl.when(inner)(functools.partial(run, inner_steps))
    pl.when(jnp.logical_not(inner))(functools.partial(run, outer_steps))
    for j in range(parts):
        for load in loads[0, j]:
            load.wait()
    mine = [aside(j) * 2 + core for j in range(places)]
    passed = [aside(j) * 2 + 1 - core for j in range(places)]
    passes = [near] + far_later[:1] + [near + 1] + far_later[1:]
    for i, j in enumerate(mine + passed):
        if passes:
            pass_on(1, passes.pop(0))
        if i == places:
            finish(1, 0)
        forward_unit(1, 0, j, i == 0)
    for k in passes:
        pass_on(1, k)
    for i, j in enumerate(mine + passed):
        if i == places:
            finish(1, 1)
        forward_unit(1, 1, j, i == 0)
    activate(1)
    aside_first = list(range(1, places)) + [0]
    for c in range(chunks):
        for j in aside_first[:-1]:
            pair_step(1, c, j)
            side_step(1, c, j)
    for k in range(1, near):
        wide(k)
    for c in range(chunks):
        pair_step(1, c, 0)
    finish(0, 0)
    rest = list(order)
    for j in range(parts):
        forward_unit(0, 0, j, j == 0)
        if j and rest:
            return_step(1, 0, rest.pop(0))
    activate(0)
    for k in rest:
        return_step(1, 0, k)
    rest = [(c, k) for c in range(1, chunks) for k in order]
    for c in range(chunks):
        for j in aside_first[:-1]:
            pair_step(0, c, j)
            side_step(0, c, j)
        for _ in range(near // 2):
            if rest:
                return_step(1, *rest.pop(0))
    for at in rest:
        return_step(1, *at)
    combine(0)
    for c in range(chunks):
        pair_step(0, c, 0)
    term_step(1)
    term_step(0)
    some_grads(1)
    for k in order:
        some_grads(1)
        return_step(0, 0, k)
    combine(chunks - 1)
    for c in range(1, chunks):
        for k in order:
            some_grads(1)
            return_step(0, c, k)
    some_grads(len(grads))

    for c in range(chunks):
        for k in range(1, near):
            arrived(home.at[c, k], home_recv.at[c, k])
        arrived(home_far.at[c], comb_recv.at[c])
    for k in range(1, groups):
        arrived(home_s.at[k], back_recv.at[k])

    few, all_near = recv_t.at[0, pl.ds(0, near - 1)], recv_t.at[0, pl.ds(0, near)]
    for t in range(2):
        arrived((far_t, far_u)[t], raw_send.at[t])
    arrived(far_slots, slot_send)
    arrived(recv_s.at[pl.ds(0, groups - 1)], scale_send)
    for j in range(places):
        arrived(few, near_send.at[j])
        arrived(few, wide_fwd.at[j])
    for i in range(3):
        arrived(few, dp_send.at[i])
    for n in range(1, 4):
        arrived(all_near, pair_fwd.at[n])
        for j in range(1, places):
            arrived(all_near, side_fwd.at[n, j])
            arrived(all_near, pass_fwd.at[n, j])
    for h in range(2):
        arrived(term_recv.at[h, pl.ds(0, parts - 1)], term_send.at[h])
        for c in range(chunks):
            arrived(ret_send.at[h, c, pl.ds(0, near - 1)], ret_sem.at[h, c])
            for j in range(places):
                arrived(pair_send.at[h, c, j], pair_send_sem.at[h, c, j])
                if j:
                    arrived(side_send.at[h, c, j], side_send_sem.at[h, c, j])
    arrived(home_s.at[pl.ds(0, groups - 1)], back_send)
    for c in range(chunks):
        arrived(comb.at[c], comb_send.at[c])


def exchange(tokens, upstream, ids, gates, w_gate, w_up, w_down, groups, parts, cap):
    toks, part = upstream.shape
    rows = groups * cap
    near = groups // 2
    half = near * cap
    hid, width = w_gate.shape
    places = parts // 2
    chunks = 2
    wide_part = part // chunks
    bf, f32 = jnp.bfloat16, jnp.float32
    dma = pltpu.SemaphoreType.DMA
    vmem = pl.BlockSpec(memory_space=pltpu.VMEM)
    hbm = pl.BlockSpec(memory_space=pl.ANY)
    return pl.pallas_call(
        functools.partial(kernel, groups, parts, cap),
        out_shape=(
            pltpu.VMEM((hid, width), bf), pltpu.VMEM((hid, width), bf), pltpu.VMEM((hid, width), bf),
            pltpu.VMEM((chunks, near, cap, wide_part), bf), pltpu.VMEM((chunks, toks, wide_part), bf),
            pltpu.VMEM((groups, 8, LANES), f32), pltpu.VMEM((8, toks), jnp.int32),
        ),
        in_specs=[hbm, hbm, vmem, vmem, hbm, hbm, hbm],
        out_specs=(vmem,) * 7,
        scratch_shapes=[
            pltpu.VMEM((parts, toks, part), bf),
            pltpu.VMEM((toks, part), bf),
            pltpu.VMEM((toks, part), bf),
            pltpu.VMEM((toks, part), bf),
            pltpu.VMEM((8, toks), jnp.int32),
            pltpu.VMEM((half, toks), bf),
            pltpu.VMEM((places, near, cap, part), bf),
            pltpu.VMEM((near, cap, part), bf),
            pltpu.VMEM((2, near, cap, part), bf),
            pltpu.VMEM((parts, groups, cap, part), bf),
            pltpu.VMEM((parts, groups, cap, part), bf),
            pltpu.VMEM((rows // LANES, 8, LANES), f32),
            pltpu.VMEM((groups, 8, LANES), f32),
            pltpu.VMEM((parts, 2 * hid, part), bf),
            pltpu.VMEM((parts, hid, part), bf),
            pltpu.VMEM((2, 2 * hid, half), f32),
            pltpu.VMEM((2, hid, half), f32),
            pltpu.VMEM((2 * hid, rows), bf),
            pltpu.VMEM((hid, rows), bf),
            pltpu.VMEM((2, half, 2 * hid), bf),
            pltpu.VMEM((2, 8, half), f32),
            pltpu.VMEM((2, parts, 8, half), f32),
            pltpu.VMEM((rows // LANES, 8, LANES), f32),
            pltpu.VMEM((2, chunks, places, near, cap, wide_part), bf),
            pltpu.VMEM((2, chunks, places, near, cap, wide_part), bf),
            pltpu.VMEM((2, chunks, places, near, cap, wide_part), f32),
            pltpu.VMEM((2, chunks, places, near, cap, wide_part), bf),
            pltpu.VMEM((2, chunks, places, near, cap, wide_part), bf),
            pltpu.VMEM((2, chunks, near, cap, wide_part), bf),
            pltpu.VMEM((chunks, near, cap, wide_part), bf),
            pltpu.VMEM((chunks, toks, wide_part), bf),
            dma((3, parts)), dma((parts + 1,)), dma((2,)), dma((2,)), dma, dma, dma, dma((groups,)),
            dma((places,)), dma((places,)), dma((3,)), dma((4,)), dma((4, places)),
            dma((4, places)), dma((2, parts, groups)),
            dma((2,)), dma((2, parts)), dma, dma((groups,)),
            dma((2, chunks, places)), dma((2, chunks, places)), dma((2, chunks, places)),
            dma((2, chunks, places, near)), dma((2, chunks)), dma((chunks, near)),
            dma((chunks, near)), dma((chunks,)), dma((chunks,)),
        ],
        compiler_params=pltpu.CompilerParams(
            collective_id=0, has_side_effects=True, vmem_limit_bytes=46 * 1024 * 1024
        ),
    )(tokens, upstream, ids, gates, w_gate, w_up, w_down)


def closing(
    groups, cap, top, grad_g, grad_u, grad_d, home, home_far, home_s, slots,
    out_x, out_gates, out_g, out_u, out_d, sems,
):
    copies = []
    for i, (src, dst) in enumerate(((grad_g, out_g), (grad_u, out_u), (grad_d, out_d))):
        copy = pltpu.make_async_copy(src, dst, sems.at[i])
        copy.start()
        copies.append(copy)
    chunks, near, _, wide_part = home.shape
    rows, half = groups * cap, near * cap
    per = LANES // cap
    picks = [one_hot(slots[i:i + 1, :], 0, rows) for i in range(top)]
    pick = picks[0][0:half]
    for p in picks[1:]:
        pick = pick + p[0:half]
    pick = pick.astype(jnp.bfloat16)
    for c in range(chunks):
        value = contract_first(pick, home[c].reshape(half, wide_part))
        value = value + home_far[c].astype(jnp.float32)
        out_x[:, c * wide_part:(c + 1) * wide_part] = value.astype(jnp.bfloat16)
    terms = jnp.concatenate(
        [merged([home_s[q * per + i] for i in range(per)], cap) for q in range(rows // LANES)],
        axis=1,
    )
    for i, p in enumerate(picks):
        value = jnp.dot(terms, p, precision=lax.Precision.HIGHEST,
                        preferred_element_type=jnp.float32)
        out_gates[i:i + 1, :] = value[0:1, :]
    for copy in copies:
        copy.wait()


def close(grads, home, home_far, home_s, slots, groups, cap, top):
    vmem = pl.BlockSpec(memory_space=pltpu.VMEM)
    hbm = pl.BlockSpec(memory_space=pl.ANY)
    chunks, toks, wide_part = home_far.shape
    operands = [
        pltpu.with_memory_space_constraint(v, pltpu.VMEM)
        for v in (*grads, home, home_far, home_s, slots)
    ]
    return pl.pallas_call(
        functools.partial(closing, groups, cap, top),
        out_shape=(
            jax.ShapeDtypeStruct((toks, chunks * wide_part), jnp.bfloat16),
            jax.ShapeDtypeStruct((top, toks), jnp.float32),
            *[jax.ShapeDtypeStruct(g.shape, g.dtype) for g in grads],
        ),
        in_specs=[vmem] * 7,
        out_specs=(vmem, vmem, hbm, hbm, hbm),
        scratch_shapes=[pltpu.SemaphoreType.DMA((3,))],
        compiler_params=pltpu.CompilerParams(vmem_limit_bytes=8 * 1024 * 1024),
    )(*operands)


def per_device(tokens, upstream, gates, expert_ids, w_gate, w_up, w_down):
    groups = lax.axis_size("dp")
    parts = lax.axis_size("expert")
    experts = groups * w_gate.shape[0]
    toks = tokens.shape[0]
    top = expert_ids.shape[1]
    cap = 2 * toks * top // experts
    *grads, home, home_far, home_s, slots = exchange(
        tokens, upstream, expert_ids.T, gates.T, w_gate[0], w_up[0], w_down[0], groups, parts, cap
    )
    grad_x, grad_gates, *grads = close(grads, home, home_far, home_s, slots, groups, cap, top)
    return (grad_x, grad_gates.T, *[g[None] for g in grads])


def solution(mesh):
    in_specs = (
        P("dp", None),
        P("dp", "expert"),
        P("dp", None),
        P("dp", None),
        P("dp", "expert", None),
        P("dp", "expert", None),
        P("dp", "expert", None),
    )
    out_specs = (
        P("dp", "expert"),
        P("dp", None),
        P("dp", "expert", None),
        P("dp", "expert", None),
        P("dp", "expert", None),
    )
    return jax.shard_map(
        per_device, mesh=mesh, in_specs=in_specs, out_specs=out_specs, check_vma=False
    )
```

```python
import functools

import jax
import jax.numpy as jnp
from jax import lax
from jax.experimental import pallas as pl
from jax.experimental.pallas import tpu as pltpu
from jax.sharding import PartitionSpec as P

MESH = pl.DeviceIdType.MESH
LANES = 128


def contract_last(left, right):
    return lax.dot_general(
        left, right, (((1,), (1,)), ((), ())), preferred_element_type=jnp.float32
    )


def contract_first(left, right):
    return lax.dot_general(
        left, right, (((0,), (0,)), ((), ())), preferred_element_type=jnp.float32
    )


def matmul(left, right):
    return jnp.dot(left, right, preferred_element_type=jnp.float32)


def one_hot(slot_row, low, count):
    index = lax.broadcasted_iota(jnp.int32, (count, slot_row.shape[1]), 0) + low
    return jnp.where(index == slot_row, 1.0, 0.0)


def merged(chunks, cap):
    lane = lax.broadcasted_iota(jnp.int32, chunks[0].shape, 1)
    row = chunks[0]
    for i in range(1, len(chunks)):
        row = jnp.where(lane < i * cap, row, chunks[i])
    return row


def kernel(
    groups, parts, cap,
    tokens_hbm, upstream_hbm, ids, gates, w_g_hbm, w_u_hbm, w_d_hbm,
    out_g, out_u, out_d, home, home_far, home_s, slots,
    tok, up, far_t, far_u, far_slots, far_pick, sel_t, sel_u, sel_far, recv_t, recv_u, send_s, recv_s,
    w_gu, w_down, pre_gu, pre_down, flip_gu, flip_down, straight, term, term_recv, total_s,
    pair_send, pair_recv, own_sum, side_send, side_recv, ret_send, mid_home, comb,
    w_sem, in_sem, raw_send, raw_recv, slot_send, slot_recv, scale_send, scale_recv,
    near_send, wide_fwd, dp_send, pair_fwd, side_fwd, pass_fwd, recv_sem,
    term_send, term_sem, back_send, back_recv,
    pair_send_sem, pair_recv_sem, side_send_sem, side_recv_sem, ret_sem, home_recv, mid_recv,
    comb_send, comb_recv,
):
    me, own = lax.axis_index("dp"), lax.axis_index("expert")
    core, place = lax.rem(own, 2), lax.div(own, 2)
    places = parts // 2
    partner = place * 2 + (1 - core)
    toks, part = up.shape
    near = groups // 2
    half = near * cap
    rows = groups * cap
    hid = w_down.shape[1]
    per = LANES // cap
    chunks, wide_part = comb.shape[0], comb.shape[2]
    order = list(range(near - 1, -1, -1))
    recvs = (recv_t, recv_u)
    bf, f32 = jnp.bfloat16, jnp.float32

    def crossed(k):
        spot = me
        for bit in [1 << b for b in range(groups.bit_length()) if k >> b & 1]:
            spot = spot + bit * (1 - 2 * lax.rem(lax.div(me, bit), 2))
        return spot

    there = [crossed(k) for k in range(groups)]
    mirror = there[near]

    def aside(j):
        return lax.rem(place + j, places)

    def arrived(ref, sem):
        pltpu.make_async_copy(ref, ref, sem).wait()

    load_tok = []
    for j in range(parts):
        quarter = lax.rem(own + j, parts)
        columns = pl.ds(pl.multiple_of(quarter * part, LANES), part)
        load = pltpu.make_async_copy(tokens_hbm.at[:, columns], tok.at[quarter], in_sem.at[j])
        load.start()
        load_tok.append(load)
        if j == 0:
            load_up = pltpu.make_async_copy(upstream_hbm, up, in_sem.at[parts])
            load_up.start()
    barrier = pltpu.get_barrier_semaphore()
    for k in range(1, groups):
        pl.semaphore_signal(barrier, inc=1, device_id={"dp": there[k]}, device_id_type=MESH)
    for j in range(1, parts):
        pl.semaphore_signal(
            barrier, inc=1, device_id={"expert": lax.rem(own + j, parts)}, device_id_type=MESH
        )

    rel = [jnp.bitwise_xor(ids[i:i + 1, :], me) for i in range(ids.shape[0])]
    padded = max(groups, 16)
    expert_of = lax.broadcasted_iota(jnp.int32, (padded, toks), 0)
    named = jnp.where(expert_of == rel[0], 1.0, 0.0)
    for other in rel[1:]:
        named = named + jnp.where(expert_of == other, 1.0, 0.0)
    earlier = lax.broadcasted_iota(jnp.int32, (toks, toks), 0)
    earlier = jnp.where(earlier < lax.broadcasted_iota(jnp.int32, (toks, toks), 1), 1.0, 0.0)
    before = matmul(named.astype(bf), earlier.astype(bf))
    slots[...] = jnp.full(slots.shape, -1, jnp.int32)
    for i, r in enumerate(rel):
        position = jnp.sum(jnp.where(expert_of == r, before, 0.0), axis=0, keepdims=True)
        slots[i:i + 1, :] = r * cap + position.astype(jnp.int32)

    def remote(src, dst, send_sem, sem, target):
        pltpu.make_async_remote_copy(
            src_ref=src, dst_ref=dst, send_sem=send_sem, recv_sem=sem,
            device_id=target, device_id_type=MESH,
        ).start()

    load_tok[0].wait()
    pl.semaphore_wait(barrier, groups + parts - 2)
    remote(tok.at[own], far_t, raw_send.at[0], raw_recv.at[0], {"dp": mirror})
    remote(slots, far_slots, slot_send, slot_recv, {"dp": mirror})
    load_up.wait()
    for load in load_tok[1:]:
        load.wait()
    loads = {}
    for t in (1, 0):
        for j in range(parts):
            columns = pl.ds(j * part, part)
            if t:
                pairs = [(w_d_hbm.at[:, columns], w_down.at[j], 2)]
            else:
                pairs = [(w_g_hbm.at[:, columns], w_gu.at[j, pl.ds(0, hid)], 0),
                         (w_u_hbm.at[:, columns], w_gu.at[j, pl.ds(hid, hid)], 1)]
            loads[t, j] = [pltpu.make_async_copy(src, dst, w_sem.at[m, j]) for src, dst, m in pairs]
            for load in loads[t, j]:
                load.start()

    picks = [one_hot(slots[i:i + 1, :], 0, rows) for i in range(len(rel))]
    pick = sum(picks[1:], picks[0]).astype(bf)

    def relay(t, k):
        spot = recvs[t].at[own, k]
        n = t * 2 + (k // near)
        if k % near:
            arrived(spot, recv_sem.at[t, own, k])
        for j in range(1, places):
            remote(spot, spot, side_fwd.at[n, j], recv_sem.at[t, own, k],
                   {"expert": aside(j) * 2 + core})
        remote(spot, spot, pair_fwd.at[n], recv_sem.at[t, own, k], {"expert": partner})

    def pass_on(t, k):
        n = t * 2 + (k // near)
        for j in range(1, places):
            part_of = aside(j) * 2 + core
            spot = recvs[t].at[part_of, k]
            arrived(spot, recv_sem.at[t, part_of, k])
            remote(spot, spot, pass_fwd.at[n, j], recv_sem.at[t, part_of, k], {"expert": partner})

    def wide(k):
        for j in range(places):
            part_of = j * 2 + core
            spot = recv_t.at[part_of, k]
            arrived(spot, recv_sem.at[0, part_of, k])
            remote(spot, spot, wide_fwd.at[j], recv_sem.at[0, part_of, k], {"expert": partner})

    def finish(h, t):
        for k in range(h * near, (h + 1) * near):
            if (h, t) == (0, 0):
                if k:
                    for j in range(places):
                        part_of = j * 2 + 1 - core
                        arrived(recv_t.at[part_of, k], recv_sem.at[0, part_of, k])
            else:
                for j in range(places):
                    part_of = aside(j) * 2 + 1 - core
                    arrived(recvs[t].at[part_of, k], recv_sem.at[t, part_of, k])

    chosen = matmul(pick[0:half], up[...]).astype(bf).reshape(near, cap, part)
    recv_u[own, 0] = chosen[0]
    relay(1, 0)
    for k in range(1, near):
        sel_u[k] = chosen[k]
        remote(sel_u.at[k], recv_u.at[own, k], dp_send.at[0], recv_sem.at[1, own, k],
               {"dp": there[k]})
    for j in range(places):
        chosen = matmul(pick[0:half], tok[j * 2 + core]).astype(bf).reshape(near, cap, part)
        recv_t[j * 2 + core, 0] = chosen[0]
        for k in range(1, near):
            sel_t[j, k] = chosen[k]

    def send_wide(k):
        for j in range(places):
            spot = j * 2 + core
            remote(sel_t.at[j, k], recv_t.at[spot, k], near_send.at[j], recv_sem.at[0, spot, k],
                   {"dp": there[k]})

    scale_rows = None
    for i, p in enumerate(picks):
        gate = jnp.broadcast_to(gates[i:i + 1, :], (16, toks))
        value = contract_last(gate, p.astype(bf))
        scale_rows = value if i == 0 else scale_rows + value
    for q in range(rows // LANES):
        send_s[q] = scale_rows[0:8, q * LANES:(q + 1) * LANES]
    recv_s[0] = send_s[0]
    for k in range(1, groups):
        remote(send_s.at[k // per], recv_s.at[k], scale_send, scale_recv.at[k], {"dp": there[k]})
    for j in range(places):
        recv_t[j * 2 + 1 - core, 0] = matmul(pick[0:cap], tok[j * 2 + 1 - core]).astype(bf)

    def expand(t):
        if t == 0:
            arrived(far_slots, slot_recv)
            value = one_hot(far_slots[0:1, :], half, half)
            for i in range(1, ids.shape[0]):
                value = value + one_hot(far_slots[i:i + 1, :], half, half)
            far_pick[...] = value.astype(bf)
        source = (far_t, far_u)[t]
        arrived(source, raw_recv.at[t])
        value = matmul(far_pick[...], source[...]).astype(bf).reshape(near, cap, part)
        recvs[t][own, near] = value[0]
        for k in range(1, near):
            sel_far[t, k] = value[k]
            remote(sel_far.at[t, k], recvs[t].at[own, near + k], dp_send.at[1 + t],
                   recv_sem.at[t, own, near + k], {"dp": there[k]})
        relay(t, near)

    def forward_unit(h, t, j, first):
        block = recvs[t][j, h * near:(h + 1) * near].reshape(half, part)
        pre = (pre_gu, pre_down)[t]
        value = contract_last((w_gu, w_down)[t][j], block)
        if first:
            pre[h] = value
        else:
            pre[h] = pre[h] + value

    tile = 32

    def activate(h):
        for k in range(max(1, h * near), (h + 1) * near):
            arrived(recv_s.at[k], scale_recv.at[k])
        scale = jnp.concatenate(
            [merged([recv_s[q * per + i] for i in range(per)], cap)
             for q in range(h * half // LANES, (h + 1) * half // LANES)], axis=1
        )[0:1, :]
        term[h] = jnp.zeros((8, half), f32)

        @pl.loop(0, hid // tile)
        def _(step):
            low = pl.multiple_of(step * tile, tile)
            at = pl.ds(low, tile)
            above = pl.ds(pl.multiple_of(low + hid, tile), tile)
            columns = pl.ds(h * half, half)
            gate, lift, back = pre_gu[h, at, :], pre_gu[h, above, :], pre_down[h, at, :]
            sigma = jax.nn.sigmoid(gate)
            swish = gate * sigma
            slope = sigma * (1.0 + gate * (1.0 - sigma))
            act = (swish * lift).astype(bf).astype(f32)
            term[h] += jnp.broadcast_to(jnp.sum(act * back, axis=0, keepdims=True), (8, half))
            weighted = scale * back
            flip_gu[at, columns] = (weighted * lift * slope).astype(bf)
            flip_gu[above, columns] = (weighted * swish).astype(bf)
            flip_down[at, columns] = (scale * act).astype(bf)

        for j in range(1, parts):
            remote(term.at[h], term_recv.at[h, own], term_send.at[h], term_sem.at[h, own],
                   {"expert": lax.rem(own + j, parts)})
        block = flip_gu[:, h * half:(h + 1) * half].astype(f32)
        straight[h] = jnp.transpose(block).astype(bf)

    def piece(h, c, which):
        columns = pl.ds(c * wide_part, wide_part)
        value = matmul(straight[h], w_gu[which, :, columns])
        return value.reshape(near, cap, wide_part)

    def pair_step(h, c, j):
        spot = aside(j) * 2
        pair_send[h, c, j] = piece(h, c, spot + 1 - core).astype(bf)
        remote(pair_send.at[h, c, j], pair_recv.at[h, c, j], pair_send_sem.at[h, c, j],
               pair_recv_sem.at[h, c, j], {"expert": partner})
        own_sum[h, c, j] = piece(h, c, spot + core)

    def side_step(h, c, j):
        arrived(pair_recv.at[h, c, j], pair_recv_sem.at[h, c, j])
        for k in order:
            both = own_sum[h, c, j, k] + pair_recv[h, c, j, k].astype(f32)
            side_send[h, c, j, k] = both.astype(bf)
            remote(side_send.at[h, c, j, k], side_recv.at[h, c, j, k], side_send_sem.at[h, c, j],
                   side_recv_sem.at[h, c, j, k], {"expert": aside(j) * 2 + core})

    def return_step(h, c, k):
        if k == order[0]:
            arrived(pair_recv.at[h, c, 0], pair_recv_sem.at[h, c, 0])
        value = own_sum[h, c, 0, k] + pair_recv[h, c, 0, k].astype(f32)
        for j in range(1, places):
            arrived(side_recv.at[h, c, j, k], side_recv_sem.at[h, c, j, k])
            value = value + side_recv[h, c, j, k].astype(f32)
        goal, sem = ((home, home_recv), (mid_home, mid_recv))[h]
        if k == 0:
            goal[c, 0] = value.astype(bf)
        else:
            ret_send[h, c, k] = value.astype(bf)
            remote(ret_send.at[h, c, k], goal.at[c, k], ret_sem.at[h, c], sem.at[c, k],
                   {"dp": there[k]})

    def combine(c):
        for k in range(1, near):
            arrived(mid_home.at[c, k], mid_recv.at[c, k])
        value = contract_first(far_pick[...], mid_home[c].reshape(half, wide_part))
        comb[c] = value.astype(bf)
        remote(comb.at[c], home_far.at[c], comb_send.at[c], comb_recv.at[c], {"dp": mirror})

    def term_step(h):
        for j in range(1, parts):
            other = lax.rem(own + j, parts)
            arrived(term_recv.at[h, other], term_sem.at[h, other])
        term_recv[h, own] = term[h]
        total = term_recv[h, 0]
        for j in range(1, parts):
            total = total + term_recv[h, j]
        for q in range(half // LANES):
            total_s[h * half // LANES + q] = total[:, q * LANES:(q + 1) * LANES]
        for k in range(h * near, (h + 1) * near):
            if k == 0:
                home_s[0] = total_s[0]
            else:
                remote(total_s.at[k // per], home_s.at[k], back_send, back_recv.at[k],
                       {"dp": there[k]})

    def grad_unit(m, j):
        block = recvs[m // 2][j].reshape(rows, part)
        left = flip_down[...] if m == 2 else flip_gu[m * hid:(m + 1) * hid, :]
        (out_g, out_u, out_d)[m][:, j * part:(j + 1) * part] = matmul(left, block).astype(bf)

    grads = [(m, j) for m in range(3) for j in range(parts)]

    def some_grads(count):
        for _ in range(count):
            if grads:
                grad_unit(*grads.pop(0))

    def raw_up():
        remote(up, far_u, raw_send.at[1], raw_recv.at[1], {"dp": mirror})

    def near_up():
        finish(0, 1)
        for j in range(parts):
            loads[1, j][0].wait()
            forward_unit(0, 1, j, j == 0)

    later = range(2, near)
    far_later = [near + k for k in later]
    outer_steps = (
        [(relay, 1, 1), (pass_on, 1, 0)] + [(relay, 1, k) for k in later]
        + [(pass_on, 1, 1)] + [(pass_on, 1, k) for k in later[:1]] + [(raw_up,), (expand, 0)]
        + [(relay, 0, near + 1)] + [(pass_on, 1, k) for k in later[1:]] + [(relay, 0, k) for k in far_later]
        + [(pass_on, 0, near), (expand, 1), (pass_on, 0, near + 1)]
        + [(send_wide, k) for k in later] + [(relay, 1, k) for k in far_later[:1]]
        + [(relay, 1, near + 1)] + [(relay, 1, k) for k in far_later[1:]]
        + [(send_wide, 1)] + [(pass_on, 0, k) for k in far_later] + [(near_up,)]
    )
    inner_steps = (
        [(raw_up,), (relay, 1, 1), (pass_on, 1, 0), (expand, 0), (pass_on, 1, 1)]
        + [(relay, 1, k) for k in later] + [(relay, 0, near + 1), (pass_on, 0, near)]
        + [(pass_on, 1, k) for k in later]
        + [(expand, 1), (pass_on, 0, near + 1)] + [(relay, 0, k) for k in far_later]
        + [(relay, 1, near + 1)] + [(send_wide, k) for k in later]
        + [(relay, 1, k) for k in far_later] + [(send_wide, 1)]
        + [(pass_on, 0, k) for k in far_later] + [(near_up,)]
    )
    inner = lax.rem(lax.div(me, near) + lax.div(me, max(1, near // 2)), 2) == 1

    def run(steps):
        for step, *at in steps:
            step(*at)

    pl.when(inner)(functools.partial(run, inner_steps))
    pl.when(jnp.logical_not(inner))(functools.partial(run, outer_steps))
    for j in range(parts):
        for load in loads[0, j]:
            load.wait()
    mine = [aside(j) * 2 + core for j in range(places)]
    passed = [aside(j) * 2 + 1 - core for j in range(places)]
    passes = [near] + far_later[:1] + [near + 1] + far_later[1:]
    for i, j in enumerate(mine + passed):
        if passes:
            pass_on(1, passes.pop(0))
        if i == places:
            finish(1, 0)
        forward_unit(1, 0, j, i == 0)
    for k in passes:
        pass_on(1, k)
    for i, j in enumerate(mine + passed):
        if i == places:
            finish(1, 1)
        forward_unit(1, 1, j, i == 0)
    activate(1)
    aside_first = list(range(1, places)) + [0]
    for c in range(chunks):
        for j in aside_first[:-1]:
            pair_step(1, c, j)
            side_step(1, c, j)
    for k in range(1, near):
        wide(k)
    for c in range(chunks):
        pair_step(1, c, 0)
    finish(0, 0)
    rest = list(order)
    for j in range(parts):
        forward_unit(0, 0, j, j == 0)
        if j and rest:
            return_step(1, 0, rest.pop(0))
    activate(0)
    for k in rest:
        return_step(1, 0, k)
    rest = [(c, k) for c in range(1, chunks) for k in order]
    for c in range(chunks):
        for j in aside_first[:-1]:
            pair_step(0, c, j)
            side_step(0, c, j)
        for _ in range(near // 2):
            if rest:
                return_step(1, *rest.pop(0))
    for at in rest:
        return_step(1, *at)
    combine(0)
    for c in range(chunks):
        pair_step(0, c, 0)
    term_step(1)
    term_step(0)
    some_grads(1)
    for k in order:
        some_grads(1)
        return_step(0, 0, k)
    combine(chunks - 1)
    for c in range(1, chunks):
        for k in order:
            some_grads(1)
            return_step(0, c, k)
    some_grads(len(grads))

    for c in range(chunks):
        for k in range(1, near):
            arrived(home.at[c, k], home_recv.at[c, k])
        arrived(home_far.at[c], comb_recv.at[c])
    for k in range(1, groups):
        arrived(home_s.at[k], back_recv.at[k])

    few, all_near = recv_t.at[0, pl.ds(0, near - 1)], recv_t.at[0, pl.ds(0, near)]
    for t in range(2):
        arrived((far_t, far_u)[t], raw_send.at[t])
    arrived(far_slots, slot_send)
    arrived(recv_s.at[pl.ds(0, groups - 1)], scale_send)
    for j in range(places):
        arrived(few, near_send.at[j])
        arrived(few, wide_fwd.at[j])
    for i in range(3):
        arrived(few, dp_send.at[i])
    for n in range(1, 4):
        arrived(all_near, pair_fwd.at[n])
        for j in range(1, places):
            arrived(all_near, side_fwd.at[n, j])
            arrived(all_near, pass_fwd.at[n, j])
    for h in range(2):
        arrived(term_recv.at[h, pl.ds(0, parts - 1)], term_send.at[h])
        for c in range(chunks):
            arrived(ret_send.at[h, c, pl.ds(0, near - 1)], ret_sem.at[h, c])
            for j in range(places):
                arrived(pair_send.at[h, c, j], pair_send_sem.at[h, c, j])
                if j:
                    arrived(side_send.at[h, c, j], side_send_sem.at[h, c, j])
    arrived(home_s.at[pl.ds(0, groups - 1)], back_send)
    for c in range(chunks):
        arrived(comb.at[c], comb_send.at[c])


def exchange(tokens, upstream, ids, gates, w_gate, w_up, w_down, groups, parts, cap):
    toks, part = upstream.shape
    rows = groups * cap
    near = groups // 2
    half = near * cap
    hid, width = w_gate.shape
    places = parts // 2
    chunks = 2
    wide_part = part // chunks
    bf, f32 = jnp.bfloat16, jnp.float32
    dma = pltpu.SemaphoreType.DMA
    vmem = pl.BlockSpec(memory_space=pltpu.VMEM)
    hbm = pl.BlockSpec(memory_space=pl.ANY)
    return pl.pallas_call(
        functools.partial(kernel, groups, parts, cap),
        out_shape=(
            pltpu.VMEM((hid, width), bf), pltpu.VMEM((hid, width), bf), pltpu.VMEM((hid, width), bf),
            pltpu.VMEM((chunks, near, cap, wide_part), bf), pltpu.VMEM((chunks, toks, wide_part), bf),
            pltpu.VMEM((groups, 8, LANES), f32), pltpu.VMEM((8, toks), jnp.int32),
        ),
        in_specs=[hbm, hbm, vmem, vmem, hbm, hbm, hbm],
        out_specs=(vmem,) * 7,
        scratch_shapes=[
            pltpu.VMEM((parts, toks, part), bf),
            pltpu.VMEM((toks, part), bf),
            pltpu.VMEM((toks, part), bf),
            pltpu.VMEM((toks, part), bf),
            pltpu.VMEM((8, toks), jnp.int32),
            pltpu.VMEM((half, toks), bf),
            pltpu.VMEM((places, near, cap, part), bf),
            pltpu.VMEM((near, cap, part), bf),
            pltpu.VMEM((2, near, cap, part), bf),
            pltpu.VMEM((parts, groups, cap, part), bf),
            pltpu.VMEM((parts, groups, cap, part), bf),
            pltpu.VMEM((rows // LANES, 8, LANES), f32),
            pltpu.VMEM((groups, 8, LANES), f32),
            pltpu.VMEM((parts, 2 * hid, part), bf),
            pltpu.VMEM((parts, hid, part), bf),
            pltpu.VMEM((2, 2 * hid, half), f32),
            pltpu.VMEM((2, hid, half), f32),
            pltpu.VMEM((2 * hid, rows), bf),
            pltpu.VMEM((hid, rows), bf),
            pltpu.VMEM((2, half, 2 * hid), bf),
            pltpu.VMEM((2, 8, half), f32),
            pltpu.VMEM((2, parts, 8, half), f32),
            pltpu.VMEM((rows // LANES, 8, LANES), f32),
            pltpu.VMEM((2, chunks, places, near, cap, wide_part), bf),
            pltpu.VMEM((2, chunks, places, near, cap, wide_part), bf),
            pltpu.VMEM((2, chunks, places, near, cap, wide_part), f32),
            pltpu.VMEM((2, chunks, places, near, cap, wide_part), bf),
            pltpu.VMEM((2, chunks, places, near, cap, wide_part), bf),
            pltpu.VMEM((2, chunks, near, cap, wide_part), bf),
            pltpu.VMEM((chunks, near, cap, wide_part), bf),
            pltpu.VMEM((chunks, toks, wide_part), bf),
            dma((3, parts)), dma((parts + 1,)), dma((2,)), dma((2,)), dma, dma, dma, dma((groups,)),
            dma((places,)), dma((places,)), dma((3,)), dma((4,)), dma((4, places)),
            dma((4, places)), dma((2, parts, groups)),
            dma((2,)), dma((2, parts)), dma, dma((groups,)),
            dma((2, chunks, places)), dma((2, chunks, places)), dma((2, chunks, places)),
            dma((2, chunks, places, near)), dma((2, chunks)), dma((chunks, near)),
            dma((chunks, near)), dma((chunks,)), dma((chunks,)),
        ],
        compiler_params=pltpu.CompilerParams(
            collective_id=0, has_side_effects=True, vmem_limit_bytes=46 * 1024 * 1024
        ),
    )(tokens, upstream, ids, gates, w_gate, w_up, w_down)


def closing(
    groups, cap, top, grad_g, grad_u, grad_d, home, home_far, home_s, slots,
    out_x, out_gates, out_g, out_u, out_d, sems,
):
    copies = []
    for i, (src, dst) in enumerate(((grad_g, out_g), (grad_u, out_u), (grad_d, out_d))):
        copy = pltpu.make_async_copy(src, dst, sems.at[i])
        copy.start()
        copies.append(copy)
    chunks, near, _, wide_part = home.shape
    rows, half = groups * cap, near * cap
    per = LANES // cap
    picks = [one_hot(slots[i:i + 1, :], 0, rows) for i in range(top)]
    pick = picks[0][0:half]
    for p in picks[1:]:
        pick = pick + p[0:half]
    pick = pick.astype(jnp.bfloat16)
    for c in range(chunks):
        value = contract_first(pick, home[c].reshape(half, wide_part))
        value = value + home_far[c].astype(jnp.float32)
        out_x[:, c * wide_part:(c + 1) * wide_part] = value.astype(jnp.bfloat16)
    terms = jnp.concatenate(
        [merged([home_s[q * per + i] for i in range(per)], cap) for q in range(rows // LANES)],
        axis=1,
    )
    for i, p in enumerate(picks):
        value = jnp.dot(terms, p, precision=lax.Precision.HIGHEST,
                        preferred_element_type=jnp.float32)
        out_gates[i:i + 1, :] = value[0:1, :]
    for copy in copies:
        copy.wait()


def close(grads, home, home_far, home_s, slots, groups, cap, top):
    vmem = pl.BlockSpec(memory_space=pltpu.VMEM)
    hbm = pl.BlockSpec(memory_space=pl.ANY)
    chunks, toks, wide_part = home_far.shape
    operands = [
        pltpu.with_memory_space_constraint(v, pltpu.VMEM)
        for v in (*grads, home, home_far, home_s, slots)
    ]
    return pl.pallas_call(
        functools.partial(closing, groups, cap, top),
        out_shape=(
            jax.ShapeDtypeStruct((toks, chunks * wide_part), jnp.bfloat16),
            jax.ShapeDtypeStruct((top, toks), jnp.float32),
            *[jax.ShapeDtypeStruct(g.shape, g.dtype) for g in grads],
        ),
        in_specs=[vmem] * 7,
        out_specs=(vmem, vmem, hbm, hbm, hbm),
        scratch_shapes=[pltpu.SemaphoreType.DMA((3,))],
        compiler_params=pltpu.CompilerParams(vmem_limit_bytes=8 * 1024 * 1024),
    )(*operands)


def per_device(tokens, upstream, gates, expert_ids, w_gate, w_up, w_down):
    groups = lax.axis_size("dp")
    parts = lax.axis_size("expert")
    experts = groups * w_gate.shape[0]
    toks = tokens.shape[0]
    top = expert_ids.shape[1]
    cap = 2 * toks * top // experts
    *grads, home, home_far, home_s, slots = exchange(
        tokens, upstream, expert_ids.T, gates.T, w_gate[0], w_up[0], w_down[0], groups, parts, cap
    )
    grad_x, grad_gates, *grads = close(grads, home, home_far, home_s, slots, groups, cap, top)
    return (grad_x, grad_gates.T, *[g[None] for g in grads])


def solution(mesh):
    in_specs = (
        P("dp", None),
        P("dp", "expert"),
        P("dp", None),
        P("dp", None),
        P("dp", "expert", None),
        P("dp", "expert", None),
        P("dp", "expert", None),
    )
    out_specs = (
        P("dp", "expert"),
        P("dp", None),
        P("dp", "expert", None),
        P("dp", "expert", None),
        P("dp", "expert", None),
    )
    return jax.shard_map(
        per_device, mesh=mesh, in_specs=in_specs, out_specs=out_specs, check_vma=False
    )
```
